32 devices in a mesh: strike: 8 (over y, x, core), dip: 4 (over z).
Axes of the slice: x: 2, y: 2, z: 4, core: 2. Of those that a mesh axis runs over, the one named last changes fastest.
Arguments:
- velocity: float32 [12, 128, 1024], P(None, 'strike', 'dip'), may hold values from -6 to 6
- stress: float32 [3, 12, 128, 1024], P(None, None, 'strike', 'dip'), may hold values from -6 to 6
- shear_modulus: float32 [12, 128, 1024], P(None, 'strike', 'dip'), may hold values from 0.5 to 2
- buoyancy: float32 [12, 128, 1024], P(None, 'strike', 'dip'), may hold values from 0.5 to 2
- prestress: float32 [128, 1024], P('strike', 'dip'), may hold values from -6 to 6
- normal_stress: float32 [128, 1024], P('strike', 'dip'), may hold values from 0.5 to 2
- crit_slip: float32 [128, 1024], P('strike', 'dip'), may hold values from 0.25 to 4
- slip: float32 [128, 1024], P('strike', 'dip'), may hold values from 0 to 2
- traction: float32 [128, 1024], P('strike', 'dip'), may hold values from -6 to 6
- functional: float32 [128, 1024], P('strike', 'dip'), may hold values from -6 to 6
- flags: int32 [128, 1024], P('strike', 'dip'), may hold values 0 or 1
- history: float32 [64, 2, 1024, 128], P(None, None, ('strike', 'dip')), may hold values from -6 to 6
- kernel: bfloat16 [65, 1024, 128], P(None, ('strike', 'dip')), may hold values from -0.75 to 0.75
Outputs:
- new_velocity: float32 [12, 128, 1024], P(None, 'strike', 'dip')
- new_stress: float32 [3, 12, 128, 1024], P(None, None, 'strike', 'dip')
- new_slip: float32 [128, 1024], P('strike', 'dip')
- new_traction: float32 [128, 1024], P('strike', 'dip')
- new_functional: float32 [128, 1024], P('strike', 'dip')
The draws below stay inside these ranges and needn't reach their ends.
Inputs may be any that keep to these rules, and one draw needn't show every extreme that they name: `flags`: 1 marks a fault cell on the slip-weakening branch, 0 a stuck cell.
All inputs are finite; a program needn't handle non-finite values. No bound on the sum of `flags` on one device may be relied on, other than what follows from the above.
Results may differ from the reference program's by a relative error of at most 0.0003.
Values sent between devices are 32-bit elements; how exact they have to be, the bound alone decides.
A program may use at most 64 MiB of HBM per device.

```python
import math
import jax
import jax.numpy as jnp
from jax import lax

NZ = 12
HIST = 64
STEPS = 2
NX = 128
NY = 1024


def touch_ends(result, stream_key, low, high):
    extent = result.shape
    place = [jax.random.randint(jax.random.fold_in(stream_key, axis), (), 0, extent[axis]) for axis in range(len(extent))]
    result = result.at[tuple(place)].set(low)
    longest = extent.index(max(extent))
    place[longest] = (place[longest] + 1) % extent[longest]
    return result.at[tuple(place)].set(high)


def steps_of(stream_key, dims, pieces, smallest, top_value):
    factor_of, own = 1.0, jax.random.fold_in(stream_key, 6)
    for axis_at, blocks in pieces:
        heights = jnp.exp(jax.random.uniform(jax.random.fold_in(own, axis_at), (blocks,), jnp.float32, smallest / len(pieces), top_value / len(pieces)))
        factor_of = factor_of * jnp.repeat(heights, dims[axis_at] // blocks).reshape([-1 if axis == axis_at else 1 for axis in range(len(dims))])
    return factor_of


def gaussian(key, extent, scale, limit, pieces=(), kind=jnp.bfloat16):
    values = scale * jax.random.normal(key, extent, jnp.float32)
    if pieces:
        values = values * steps_of(key, extent, pieces, -0.22, 0.18)
    return jnp.clip(values, -limit, limit).astype(kind)


def setup_inputs(seed: int = 0) -> dict:
    keys = jax.random.split(jax.random.key(seed), 14)
    velocity = gaussian(keys[0], (NZ, NX, NY), 1.0, 6.0, ((1, 8), (2, 4)), jnp.float32)
    stress = gaussian(keys[1], (3, NZ, NX, NY), 1.0, 6.0, ((2, 8), (3, 4)), jnp.float32)
    shear_modulus = jnp.clip(jnp.exp(math.log(2.0) - 1.3862944 * jax.random.uniform(keys[2], (NZ, NX, NY), jnp.float32) ** steps_of(keys[2], (NZ, NX, NY), ((1, 8), (2, 4)), -0.2, 0.2)), 0.5, 2.0)
    buoyancy = jnp.clip(jnp.exp(math.log(2.0) - 1.3862944 * jax.random.uniform(keys[3], (NZ, NX, NY), jnp.float32) ** steps_of(keys[3], (NZ, NX, NY), ((1, 8), (2, 4)), -0.2, 0.2)), 0.5, 2.0)
    prestress = gaussian(keys[4], (NX, NY), 1.0, 6.0, ((0, 8), (1, 4)), jnp.float32)
    normal_stress = jnp.clip(jnp.exp(math.log(2.0) - 1.3862944 * jax.random.uniform(keys[5], (NX, NY), jnp.float32) ** steps_of(keys[5], (NX, NY), ((0, 8), (1, 4)), -0.2, 0.2)), 0.5, 2.0)
    crit_slip = jnp.clip(jnp.exp(math.log(4.0) - 2.7725887 * jax.random.uniform(keys[6], (NX, NY), jnp.float32) ** steps_of(keys[6], (NX, NY), ((0, 8), (1, 4)), -0.2, 0.2)), 0.25, 4.0)
    slip = jnp.clip(2.0 * jax.random.uniform(keys[7], (NX, NY), jnp.float32) ** steps_of(keys[7], (NX, NY), ((0, 8), (1, 4)), -0.2, 0.2), 0.0, 2.0)
    traction = gaussian(keys[8], (NX, NY), 1.0, 6.0, ((0, 8), (1, 4)), jnp.float32)
    functional = gaussian(keys[9], (NX, NY), 1.0, 6.0, ((0, 8), (1, 4)), jnp.float32)
    flags = touch_ends((jax.random.randint(keys[10], (NX, NY), 0, 4) < 3).astype(jnp.int32), jax.random.fold_in(keys[10], 1), 0, 1)
    history = gaussian(keys[11], (HIST, 2, NY, NX), 1.0, 6.0, ((2, 32),), jnp.float32)
    kernel = gaussian(keys[12], (HIST + 1, NY, NX), 0.125, 0.75, ((1, 32),))
    return {"velocity": velocity, "stress": stress, "shear_modulus": shear_modulus, "buoyancy": buoyancy, "prestress": prestress, "normal_stress": normal_stress, "crit_slip": crit_slip, "slip": slip, "traction": traction, "functional": functional, "flags": flags, "history": history, "kernel": kernel}


coef_near = 2.0 / 3.0
coef_far = -1.0 / 12.0
courant = 0.3
static_friction = 0.677
dynamic_friction = 0.525
damping = 0.5
time_step = 0.3


def periodic_diff(field, axis):
    return coef_near * (jnp.roll(field, -1, axis) - jnp.roll(field, 1, axis)) + coef_far * (jnp.roll(field, -2, axis) - jnp.roll(field, 2, axis))


def normal_diff(field, ghost):
    zeros = jnp.zeros_like(ghost)
    padded = jnp.concatenate([ghost, ghost, field, zeros, zeros], axis=0)
    count = field.shape[0]
    return coef_near * (padded[3:count + 3] - padded[1:count + 1]) + coef_far * (padded[4:count + 4] - padded[0:count])


def fault_update(prestress, normal_stress, crit_slip, flags, slip, stress_z, functional):
    trial = prestress + stress_z[0] + functional
    weaken = jnp.maximum(0.0, 1.0 - jnp.abs(slip) / crit_slip)
    strength = normal_stress * (dynamic_friction + (static_friction - dynamic_friction) * weaken)
    clipped = jnp.clip(trial, -strength, strength)
    traction = jnp.where(flags == 1, clipped, trial)
    rate = (trial - traction) / damping
    return traction, slip + time_step * rate


def stored_sum(kernel, history, shift):
    count = history.shape[0] - shift

    def add_term(index, carry):
        weight = lax.dynamic_index_in_dim(kernel, index + shift + 1, 0, keepdims=False).astype(jnp.float32)
        term = lax.dynamic_index_in_dim(history, index, 0, keepdims=False)
        return carry + weight[None] * term

    return lax.fori_loop(0, count, add_term, jnp.zeros_like(history[0]))


def reference(velocity, stress, shear_modulus, buoyancy, prestress, normal_stress, crit_slip, slip, traction, functional, flags, history, kernel):
    stress_x, stress_y, stress_z = stress[0], stress[1], stress[2]
    spectra = []
    for iteration in range(STEPS):
        divergence = periodic_diff(stress_x, 1) + periodic_diff(stress_y, 2) + normal_diff(stress_z, traction[None])
        velocity = velocity + courant * buoyancy * divergence
        ghost_zero = jnp.zeros_like(traction[None])
        stress_x = stress_x + courant * shear_modulus * periodic_diff(velocity, 1)
        stress_y = stress_y + courant * shear_modulus * periodic_diff(velocity, 2)
        stress_z = stress_z + courant * shear_modulus * normal_diff(velocity, ghost_zero)
        traction, slip = fault_update(prestress, normal_stress, crit_slip, flags, slip, stress_z, functional)
        spectrum = jnp.transpose(jnp.fft.fft2(slip, norm="ortho"))
        spectra = [spectrum] + spectra
        stored = stored_sum(kernel, history, iteration)
        sum_real = stored[0]
        sum_imag = stored[1]
        for offset, item in enumerate(spectra):
            weight = kernel[offset].astype(jnp.float32)
            sum_real = sum_real + weight * jnp.real(item)
            sum_imag = sum_imag + weight * jnp.imag(item)
        combined = lax.complex(sum_real, sum_imag)
        functional = jnp.real(jnp.fft.ifft2(jnp.transpose(combined), norm="ortho"))
    return velocity, jnp.stack([stress_x, stress_y, stress_z]), slip, traction, functional
```

```python
import functools
import math

import jax
import jax.numpy as jnp
import numpy as np
from jax import lax
from jax.experimental import pallas as pl
from jax.experimental.pallas import tpu as pltpu
from jax.sharding import PartitionSpec as P

STEPS = 2


coef_near = 2.0 / 3.0
coef_far = -1.0 / 12.0
courant = 0.3
static_friction = 0.677
dynamic_friction = 0.525
damping = 0.5
time_step = 0.3


def padded_2(block, sides, width):
    for axis, dim in sides:
        count = lax.axis_size(axis)
        forward = [(i, i + 1) for i in range(count - 1)]
        forward.append((count - 1, 0))
        backward = [(target, source) for source, target in forward]
        low = lax.ppermute(
            lax.slice_in_dim(block, block.shape[dim] - width, None, axis=dim), axis, forward
        )
        high = lax.ppermute(lax.slice_in_dim(block, 0, width, axis=dim), axis, backward)
        block = jnp.concatenate([low, block, high], axis=dim)
    return block


def central(padded, axis, start, count):

    def window(offset):
        return lax.slice_in_dim(padded, start + offset, start + offset + count, axis=axis)

    return coef_near * (window(1) - window(-1)) + coef_far * (window(2) - window(-2))


def normal_diff(field, ghost):
    zeros = jnp.zeros_like(ghost)
    padded = jnp.concatenate([ghost, ghost, field, zeros, zeros], axis=0)
    return central(padded, 0, 2, field.shape[0])


def fault_update(prestress, normal_stress, crit_slip, flags, slip, stress_z, functional):
    trial = prestress + stress_z[0] + functional
    weaken = jnp.maximum(0.0, 1.0 - jnp.abs(slip) / crit_slip)
    strength = normal_stress * (dynamic_friction + (static_friction - dynamic_friction) * weaken)
    clipped = jnp.clip(trial, -strength, strength)
    traction = jnp.where(flags == 1, clipped, trial)
    rate = (trial - traction) / damping
    return (traction, slip + time_step * rate)


def factor_pair(length):
    first = 1
    candidate = 1
    while candidate * candidate <= length:
        if length % candidate == 0:
            first = candidate
        candidate += 1
    return (first, length // first)


def phase_table(count_a, count_b, length, sign):
    product = lax.iota(jnp.int32, count_a)[:, None] * lax.iota(jnp.int32, count_b)[None, :] % length
    angles = sign * 2.0 * math.pi / length * product.astype(jnp.float32)
    return (jnp.cos(angles), jnp.sin(angles))


def contract(form, left, right):
    return jnp.einsum(form, left, right, precision=lax.Precision.HIGHEST)


def transform_last(real_part, imag_part, sign):
    length = real_part.shape[-1]
    outer, inner = factor_pair(length)
    leading = real_part.shape[:-1]
    real_part = real_part.reshape(leading + (outer, inner))
    imag_part = imag_part.reshape(leading + (outer, inner))
    first_cos, first_sin = phase_table(outer, outer, outer, sign)
    middle_real = contract("kt,...tq->...kq", first_cos, real_part) - contract(
        "kt,...tq->...kq", first_sin, imag_part
    )
    middle_imag = contract("kt,...tq->...kq", first_cos, imag_part) + contract(
        "kt,...tq->...kq", first_sin, real_part
    )
    twist_cos, twist_sin = phase_table(outer, inner, length, sign)
    middle_real, middle_imag = (
        middle_real * twist_cos - middle_imag * twist_sin,
        middle_real * twist_sin + middle_imag * twist_cos,
    )
    second_cos, second_sin = phase_table(inner, inner, inner, sign)
    out_real = contract("...kt,tm->...km", middle_real, second_cos) - contract(
        "...kt,tm->...km", middle_imag, second_sin
    )
    out_imag = contract("...kt,tm->...km", middle_real, second_sin) + contract(
        "...kt,tm->...km", middle_imag, second_cos
    )
    scale = 1.0 / math.sqrt(length)
    out_real = jnp.swapaxes(out_real, -1, -2).reshape(leading + (length,)) * scale
    out_imag = jnp.swapaxes(out_imag, -1, -2).reshape(leading + (length,)) * scale
    return (out_real, out_imag)


def general_body(
    velocity,
    stress,
    shear_modulus,
    buoyancy,
    prestress,
    normal_stress,
    crit_slip,
    slip,
    traction,
    functional,
    flags,
    history,
    kernel,
):
    strike_count = lax.axis_size("strike")
    dip_count = lax.axis_size("dip")
    depth, rows_x, cols_y = velocity.shape
    ky_local = history.shape[2]
    total_x = history.shape[3]
    total_y = cols_y * dip_count
    line_rows = rows_x // dip_count
    stress_x, stress_y, stress_z = (stress[0], stress[1], stress[2])
    ghost_zero = jnp.zeros((1, rows_x, cols_y), jnp.float32)
    spectra = []
    for iteration in range(STEPS):
        padded_x = padded_2(stress_x, (("strike", 1),), 2)
        padded_y = padded_2(stress_y, (("dip", 2),), 2)
        divergence = (
            central(padded_x, 1, 2, rows_x)
            + central(padded_y, 2, 2, cols_y)
            + normal_diff(stress_z, traction[None])
        )
        velocity = velocity + courant * buoyancy * divergence
        padded_v = padded_2(velocity, (("strike", 1), ("dip", 2)), 2)
        grad_x = central(padded_v[:, :, 2 : cols_y + 2], 1, 2, rows_x)
        grad_y = central(padded_v[:, 2 : rows_x + 2, :], 2, 2, cols_y)
        stress_x = stress_x + courant * shear_modulus * grad_x
        stress_y = stress_y + courant * shear_modulus * grad_y
        stress_z = stress_z + courant * shear_modulus * normal_diff(velocity, ghost_zero)
        traction, slip = fault_update(
            prestress, normal_stress, crit_slip, flags, slip, stress_z, functional
        )
        lines = lax.all_to_all(slip, "dip", split_axis=0, concat_axis=1, tiled=True)
        part_real, part_imag = transform_last(lines, jnp.zeros_like(lines), -1.0)
        stacked = jnp.stack([part_real, part_imag]).reshape(
            2, line_rows, strike_count, dip_count, ky_local
        )
        stacked = stacked.transpose(0, 2, 3, 4, 1).reshape(
            2, strike_count, dip_count, ky_local, 1, 1, line_rows
        )
        halfway = lax.all_to_all(stacked, "strike", split_axis=1, concat_axis=4, tiled=True)
        owned = lax.all_to_all(halfway, "dip", split_axis=2, concat_axis=5, tiled=True)
        owned = owned.reshape(2, ky_local, total_x)
        spec_real, spec_imag = transform_last(owned[0], owned[1], -1.0)
        spectra = [(spec_real, spec_imag)] + spectra
        weights = kernel[iteration + 1 :].astype(jnp.float32)
        stored = jnp.sum(weights[:, None] * history[: history.shape[0] - iteration], axis=0)
        sum_real = stored[0]
        sum_imag = stored[1]
        for offset, item in enumerate(spectra):
            weight = kernel[offset].astype(jnp.float32)
            sum_real = sum_real + weight * item[0]
            sum_imag = sum_imag + weight * item[1]
        back_real, back_imag = transform_last(sum_real, sum_imag, 1.0)
        leaving = jnp.stack([back_real, back_imag]).reshape(
            2, 1, 1, ky_local, strike_count, dip_count, line_rows
        )
        partway = lax.all_to_all(leaving, "strike", split_axis=4, concat_axis=1, tiled=True)
        returned = lax.all_to_all(partway, "dip", split_axis=5, concat_axis=2, tiled=True)
        returned = returned.reshape(2, total_y, line_rows).transpose(0, 2, 1)
        field_real, field_imag = transform_last(returned[0], returned[1], 1.0)
        functional = lax.all_to_all(field_real, "dip", split_axis=1, concat_axis=0, tiled=True)
    return (velocity, jnp.stack([stress_x, stress_y, stress_z]), slip, traction, functional)


LANES = 128
SUBLANES = 8
MESH = pl.DeviceIdType.MESH
INPUTS = 18
KERNEL_VMEM = 67043328 - 1000000
HUGE = float(np.finfo(np.float32).max)


def split_bf16(value):
    high = value.astype(jnp.bfloat16)
    return high, (value - high.astype(jnp.float32)).astype(jnp.bfloat16)


def split_table(table):
    table = np.asarray(table, np.float32)
    high = table.astype(jnp.bfloat16)
    return high, (table - high.astype(np.float32)).astype(jnp.bfloat16)


def strike_table(total_x):
    index = np.arange(total_x)
    angle = 2.0 * np.pi / total_x * (index[:, None] * index[None, :] % total_x)
    return np.concatenate([np.cos(angle), np.sin(angle)], axis=1) / np.sqrt(total_x)


def dip_table(cols, total_y):
    count = cols // 2 + 2 * SUBLANES
    angle = 2.0 * np.pi / cols * (np.arange(count)[:, None] * np.arange(cols)[None, :] % cols)
    return np.concatenate([np.cos(angle), np.sin(angle)], axis=1) / np.sqrt(total_y)


def twiddle_table(dip_count, cols, total_y):
    place = np.arange(total_y).reshape(dip_count, 1, cols)
    freq = np.arange(dip_count)[None, :, None]
    angle = 2.0 * np.pi / total_y * (freq * place % total_y)
    return np.stack([np.cos(angle), -np.sin(angle)], axis=1).astype(np.float32)


def dot3(left, right_high, right_low):
    high, low = split_bf16(left)
    rows = left.shape[0]
    both = jnp.dot(
        jnp.concatenate([high, low], axis=0), right_high, preferred_element_type=jnp.float32
    )
    return both[:rows] + both[rows:] + jnp.dot(high, right_low, preferred_element_type=jnp.float32)


def dot3_nt(left_high, left_low, right):
    high, low = split_bf16(right)

    def product(a, b):
        return lax.dot_general(a, b, (((1,), (1,)), ((), ())), preferred_element_type=jnp.float32)

    return product(left_high, high) + product(left_high, low) + product(left_low, high)


def dot3_rows(left, right_high, right_low):
    high, low = split_bf16(left)
    rows = left.shape[0]

    def product(a, b):
        return lax.dot_general(a, b, (((1,), (1,)), ((), ())), preferred_element_type=jnp.float32)

    both = product(jnp.concatenate([high, low], axis=0), right_high)
    return both[:rows] + both[rows:] + product(high, right_low)


def rupture_kernel(strike_count, dip_count, *refs):
    sources, refs = refs[:INPUTS], refs[INPUTS:]
    results, refs = refs[:5], refs[5:]
    loaded, refs = refs[:INPUTS], refs[INPUTS:]
    (
        vel_in, stress_in, shear, buoy, prestress, normal_stress, crit_slip, slip_in, traction_in,
        functional_in, flags, hist, kern, dip_hi, dip_lo, strike_hi, strike_lo, twiddle,
    ) = loaded
    (
        vel, stress, planes_out, padded, edge_x, edge_y, halo_x, halo_y, shared, gathered, send_f,
        recv_a, recv_b, send_c, recv_c, lines_out, modal, nought, nought_in, weight, source,
        load_sem, save_sem, edge_sem, halo_sem, g_send, g_recv, a_send, a_recv, b_send, b_recv,
        c_send, c_recv, x_send, x_recv, plane_sem,
    ) = refs
    depth, rows, cols = vel_in.shape
    modes = hist.shape[2]
    total_x = hist.shape[3]
    stored_count = hist.shape[0]
    blocks = strike_count * dip_count
    half = modes // dip_count // 2
    wave = dip_count * rows
    front_modes = cols // 2
    my_s = lax.axis_index("strike")
    my_d = lax.axis_index("dip")
    my_block = my_s * dip_count + my_d
    upper = my_block // (blocks // 2)

    def ring(me, offset, count):
        return lax.rem(me + offset + count, count)

    def remote(src, dst, send_sem, recv_sem, target):
        return pltpu.make_async_remote_copy(
            src_ref=src,
            dst_ref=dst,
            send_sem=send_sem,
            recv_sem=recv_sem,
            device_id=target,
            device_id_type=MESH,
        )

    lane = lax.broadcasted_iota(jnp.int32, (rows, LANES), 1)
    column = lax.broadcasted_iota(jnp.int32, (rows, cols), 1)
    strip = lax.broadcasted_iota(jnp.int32, (SUBLANES, LANES), 1) // rows
    layer_row = lax.broadcasted_iota(jnp.int32, (SUBLANES, LANES), 0)
    real_half = layer_row < half
    sign = jnp.where(real_half, 1.0, -1.0)
    lone = jnp.logical_and(layer_row % half == 0, my_block == 0)
    swap = functools.partial(pltpu.roll, shift=half, axis=0)

    def slot(block):
        high = block // (blocks // 2)
        return 2 * block + high * (2 * blocks - 1 - 4 * block)

    def pack_x(turn, field):
        edge_x[turn, 0] = field[:, rows - 2 : rows, :]
        edge_x[turn, 1] = field[:, 0:2, :]

    def pack_y(turn, layer):
        low = jnp.zeros((rows, LANES), jnp.float32)
        high = jnp.zeros((rows, LANES), jnp.float32)
        for z in range(depth):
            here = lane // 2 == z
            last = layer(z)[:, cols - LANES :]
            first = layer(z)[:, :LANES]
            low = jnp.where(here, pltpu.roll(last, (2 * z + 2) % LANES, 1), low)
            high = jnp.where(here, pltpu.roll(first, 2 * z, 1) if z else first, high)
        edge_y[turn, 0] = low
        edge_y[turn, 1] = high

    def halo_copies(turn):
        copies = []
        for side, step in ((0, 1), (1, -1)):
            copies.append(
                remote(
                    edge_x.at[turn, side],
                    halo_x.at[turn, side],
                    edge_sem.at[turn, side],
                    halo_sem.at[turn, side],
                    {"strike": ring(my_s, step, strike_count)},
                )
            )
            copies.append(
                remote(
                    edge_y.at[turn, side],
                    halo_y.at[turn, side],
                    edge_sem.at[turn, side + 2],
                    halo_sem.at[turn, side + 2],
                    {"dip": ring(my_d, step, dip_count)},
                )
            )
        return copies

    def start_halos(turn):
        copies = halo_copies(turn)
        for copy in copies:
            copy.start()
        return copies

    def wait_halos(copies):
        for copy in copies:
            copy.wait_recv()

    def fill_padded(turn, field):
        padded[:, SUBLANES : SUBLANES + rows, :] = field[...]
        padded[:, SUBLANES - 2 : SUBLANES, :] = halo_x[turn, 0]
        padded[:, SUBLANES + rows : SUBLANES + rows + 2, :] = halo_x[turn, 1]

    def diff_x(z):
        def window(offset):
            return padded[z, SUBLANES + offset : SUBLANES + offset + rows, :]

        return coef_near * (window(1) - window(-1)) + coef_far * (window(2) - window(-2))

    def diff_y(turn, z, field):
        low = halo_y[turn, 0]
        high = halo_y[turn, 1]
        low_0, low_1 = low[:, 2 * z : 2 * z + 1], low[:, 2 * z + 1 : 2 * z + 2]
        high_0, high_1 = high[:, 2 * z : 2 * z + 1], high[:, 2 * z + 1 : 2 * z + 2]
        back_1 = jnp.where(column == 0, low_1, pltpu.roll(field, 1, 1))
        back_2 = jnp.where(
            column == 0, low_0, jnp.where(column == 1, low_1, pltpu.roll(field, 2, 1))
        )
        next_1 = jnp.where(column == cols - 1, high_0, pltpu.roll(field, cols - 1, 1))
        next_2 = jnp.where(
            column == cols - 2,
            high_0,
            jnp.where(column == cols - 1, high_1, pltpu.roll(field, cols - 2, 1)),
        )
        return coef_near * (next_1 - back_1) + coef_far * (next_2 - back_2)

    def diff_z(z, layer, ghost):
        def at(index):
            if index < 0:
                return ghost
            return layer(index) if index < depth else None

        total = None
        for offset, coef in ((1, coef_near), (-1, -coef_near), (2, coef_far), (-2, -coef_far)):
            value = at(z + offset)
            if value is not None:
                total = coef * value if total is None else total + coef * value
        return total

    def velocity_layer(turn, z, source, stress_ref, traction):
        divergence = (
            diff_x(z)
            + diff_y(turn, z, stress_ref[1, z])
            + diff_z(z, lambda i: stress_ref[2, i], traction)
        )
        vel[z] = source[z] + courant * buoy[z] * divergence

    def stress_z_layer(z, stress_ref):
        return stress_ref[2, z] + courant * shear[z] * diff_z(z, lambda i: vel[i], None)

    def stress_layers(turn, stress_ref):
        fill_padded(turn, vel)
        for z in range(depth):
            modulus = courant * shear[z]
            stress[0, z] = stress_ref[0, z] + modulus * diff_x(z)
            stress[1, z] = stress_ref[1, z] + modulus * diff_y(turn, z, vel[z])
            stress[2, z] = stress_z_layer(z, stress_ref)

    def start_gather(turn, value):
        shared[turn] = value
        gathered[turn, my_d] = value
        copies = []
        for k in range(1, dip_count):
            copy = remote(
                shared.at[turn],
                gathered.at[turn, my_d],
                g_send.at[turn, k],
                g_recv.at[turn, k],
                {"dip": ring(my_d, k, dip_count)},
            )
            copy.start()
            copies.append(copy)
        return copies

    def wait_gather(turn):
        for k in range(1, dip_count):
            source = ring(my_d, -k, dip_count)
            remote(
                shared.at[turn],
                gathered.at[turn, source],
                g_send.at[turn, k],
                g_recv.at[turn, k],
                {"dip": source},
            ).wait_recv()

    def start_b():
        recv_b[my_s] = send_f[1, slot(my_block)]
        copies = []
        for k in range(1, strike_count):
            target = ring(my_s, k, strike_count)
            copy = remote(
                send_f.at[1, slot(target * dip_count + my_d)],
                recv_b.at[my_s],
                b_send.at[k],
                b_recv.at[k],
                {"strike": target},
            )
            copy.start()
            copies.append(copy)
        return copies

    def wait_b():
        for k in range(1, strike_count):
            source_s = ring(my_s, -k, strike_count)
            remote(
                send_f.at[1, source_s],
                recv_b.at[source_s],
                b_send.at[k],
                b_recv.at[k],
                {"strike": source_s},
            ).wait_recv()

    offsets = [
        (i, k) for k in reversed(range(dip_count)) for i in reversed(range(strike_count)) if i or k
    ]

    def start_a():
        recv_a[my_d, my_s] = send_f[0, slot(my_block)]
        copies = []
        for i, k in offsets:
            target_s, target_d = ring(my_s, i, strike_count), ring(my_d, k, dip_count)
            copy = remote(
                send_f.at[0, slot(target_s * dip_count + target_d)],
                recv_a.at[my_d, my_s],
                a_send.at[k, i],
                a_recv.at[k, i],
                {"strike": target_s, "dip": target_d},
            )
            copy.start()
            copies.append(copy)
        return copies

    def wait_a():
        for i, k in reversed(offsets):
            source_s, source_d = ring(my_s, -i, strike_count), ring(my_d, -k, dip_count)
            remote(
                send_f.at[0, source_s],
                recv_a.at[source_d, source_s],
                a_send.at[k, i],
                a_recv.at[k, i],
                {"strike": source_s, "dip": source_d},
            ).wait_recv()

    def exchange_copies(turn):
        other = blocks - 1 - my_block
        single = 1 - jnp.minimum(lax.rem(my_block, blocks // 2), 1)
        mirror = lax.rem(blocks - my_block + single * (blocks // 2), blocks)
        upper_rows = pl.ds(modes // 2, modes // 2)
        return [
            remote(
                modal.at[turn, 0, :, upper_rows, :],
                modal.at[turn, 1, :, upper_rows, :],
                x_send.at[turn, 0],
                x_recv.at[turn, 0],
                {"strike": other // dip_count, "dip": lax.rem(other, dip_count)},
            ),
            remote(
                nought.at[turn],
                nought_in.at[turn],
                x_send.at[turn, 1],
                x_recv.at[turn, 1],
                {"strike": mirror // dip_count, "dip": lax.rem(mirror, dip_count)},
            ),
        ]

    def start_exchange(turn):
        copies = exchange_copies(turn)
        for copy in copies:
            copy.start()
        return copies

    def arrange(turn, copies):
        for copy in copies:
            copy.wait_recv()
        modal[turn, 1, :, modes : modes + 1, :] = nought_in[turn]
        for k0 in range(dip_count):
            for m in range(half):
                at = dip_count * m + k0
                plus = modal[turn, upper, :, pl.ds(modes // 2 * upper + at, 1), :]
                minus = modal[turn, 1 - upper, :, pl.ds(modes - modes // 2 * upper - at, 1), :]
                for side, value in enumerate((plus, minus)):
                    weight[turn, side, k0, m : m + 1, :] = value[0]
                    weight[turn, side, k0, half + m : half + m + 1, :] = value[0]
                    source[turn, side, k0, m : m + 1, :] = value[1]
                    source[turn, side, k0, half + m : half + m + 1, :] = value[2]

    def start_c(step):
        recv_c[step, slot(my_block)] = send_c[step, my_s]
        copies = []
        for i, k in offsets:
            target_s, target_d = ring(my_s, i, strike_count), ring(my_d, k, dip_count)
            copy = remote(
                send_c.at[step, target_s],
                recv_c.at[step, slot(my_block)],
                c_send.at[step, k, i],
                c_recv.at[step, k, i],
                {"strike": target_s, "dip": target_d},
            )
            copy.start()
            copies.append(copy)
        return copies

    def wait_c(step):
        for i, k in reversed(offsets):
            source_s, source_d = ring(my_s, -i, strike_count), ring(my_d, -k, dip_count)
            remote(
                send_c.at[step, source_s],
                recv_c.at[step, slot(source_s * dip_count + source_d)],
                c_send.at[step, k, i],
                c_recv.at[step, k, i],
                {"strike": source_s, "dip": source_d},
            ).wait_recv()

    def total_of(terms):
        total = None
        for left, right in terms:
            total = left * right if total is None else total + left * right
        return total

    def turned(i, part, k0):
        return twiddle[i, part, k0 : k0 + 1, :]

    def dip_forward(step, parts):
        real, imag = (
            jnp.concatenate(
                [
                    total_of([(part, turned(i, kind, k0)) for i, part in parts])
                    for k0 in range(dip_count)
                ],
                axis=0,
            )
            for kind in range(2)
        )
        both = jnp.concatenate(
            [
                jnp.concatenate([real, imag], axis=1),
                jnp.concatenate([imag, -real], axis=1),
            ],
            axis=0,
        )
        out = dot3_nt(dip_hi[...], dip_lo[...], both)
        last = pltpu.roll(out[front_modes : front_modes + SUBLANES], wave, 1)
        first = jnp.where(
            jnp.logical_and(layer_row == 0, strip == dip_count), last, out[:SUBLANES]
        )
        out = jnp.concatenate([first, out[SUBLANES:front_modes]], axis=0)
        send_f[step] = out.reshape(blocks, half, LANES)

    def strike_forward(pieces):
        stacks = [None] * dip_count
        for s, piece in enumerate(pieces):
            pair = jnp.concatenate([piece, pltpu.roll(piece, wave, 1)], axis=0)
            for k0 in range(dip_count):
                shift = rows * (s - k0) % LANES
                moved = pltpu.roll(pair, shift, 1) if shift else pair
                stacks[k0] = moved if s == 0 else jnp.where(strip == s, moved, stacks[k0])
        both = dot3(jnp.concatenate(stacks, axis=0), strike_hi[...], strike_lo[...])
        plus, minus = [], []
        for k0 in range(dip_count):
            tile = both[k0 * SUBLANES : (k0 + 1) * SUBLANES]
            cos, sin = tile[:, :total_x], tile[:, total_x:]
            crossed = swap(sin)
            ahead = cos + sign * crossed
            behind = sign * cos - crossed
            if k0 == 0:
                ahead = jnp.where(lone, jnp.where(real_half, cos, -crossed), ahead)
                behind = jnp.where(lone, jnp.where(real_half, swap(cos), -sin), behind)
            plus.append(ahead)
            minus.append(behind)
        return plus, minus

    def convolve(step, spectra):
        sums = []
        for side in range(2):
            tiles = []
            for k0 in range(dip_count):
                total = source[step, side, k0]
                for offset, item in enumerate(spectra):
                    total = total + weight[offset, side, k0] * item[side][k0]
                tiles.append(total)
            sums.append(tiles)
        return sums

    def strike_inverse(step, plus, minus):
        tiles = []
        for k0, (ahead, behind) in enumerate(zip(plus, minus)):
            direct = ahead + sign * behind
            crossed = -sign * swap(ahead - sign * behind)
            if k0 == 0:
                direct = jnp.where(lone, jnp.where(real_half, ahead, swap(behind)), direct)
                crossed = jnp.where(lone, -jnp.where(real_half, swap(ahead), behind), crossed)
            tiles.append(jnp.concatenate([direct, crossed], axis=1))
        out = dot3_rows(jnp.concatenate(tiles, axis=0), strike_hi[...], strike_lo[...])
        for s in range(strike_count):
            block = None
            for k0 in range(dip_count):
                shift = rows * (k0 - s) % LANES
                tile = out[k0 * SUBLANES : (k0 + 1) * SUBLANES]
                moved = pltpu.roll(tile, shift, 1) if shift else tile
                block = moved if k0 == 0 else jnp.where(strip == k0, moved, block)
            block = jnp.where(strip < dip_count, block, swap(pltpu.roll(block, wave, 1)))
            send_c[step, s] = block[:half]

    def dip_inverse(step, places):
        lines = recv_c[step].reshape(front_modes, LANES).T
        out = dot3(lines, dip_hi[:front_modes], dip_lo[:front_modes])
        real = out[:wave, :cols] - out[wave:, cols:]
        imag = out[:wave, cols:] + out[wave:, :cols]
        scale = 1.0 / math.sqrt(cols * dip_count)
        last = lines[wave : wave + rows, 0:1] * jnp.where(column % 2 == 0, scale, -scale)
        result = []
        for i in places:
            terms = [(real[:rows] + last, turned(i, 0, 0))]
            for k0 in range(1, dip_count):
                at = slice(k0 * rows, (k0 + 1) * rows)
                terms += [(real[at], turned(i, 0, k0)), (imag[at], turned(i, 1, k0))]
            result.append(total_of(terms))
        return result

    def store_history():
        zero = jnp.zeros((2, modes, total_x), jnp.float32)
        common = stored_count - STEPS + 1

        def term(t, j):
            return kern[j + t + 1].astype(jnp.float32)[None] * hist[j]

        def add(j, sums):
            return tuple(total + term(t, j) for t, total in enumerate(sums))

        sums = lax.fori_loop(0, common, add, (zero,) * STEPS)
        for t in range(STEPS):
            total = sums[t]
            for j in range(common, stored_count - t):
                total = total + term(t, j)
            values = (kern[t].astype(jnp.float32), total[0], total[1])
            for i, value in enumerate(values):
                modal[t, 0, i, 0:modes, :] = value
                nought[t, i] = value[0:1]

    def bound_of(slip):
        weaken = jnp.maximum(0.0, 1.0 - jnp.abs(slip) / crit_slip[...])
        strength = normal_stress[...] * (
            dynamic_friction + (static_friction - dynamic_friction) * weaken
        )
        return jnp.where(flags[...] == 1, strength, HUGE)

    def slide(trial, bound, slip):
        traction = jnp.clip(trial, -bound, bound)
        return traction, slip + time_step * ((trial - traction) / damping)

    barrier = pltpu.get_barrier_semaphore()
    for k in range(1, strike_count):
        pl.semaphore_signal(
            barrier, inc=1, device_id={"strike": ring(my_s, k, strike_count)}, device_id_type=MESH
        )
    for k in range(1, dip_count):
        pl.semaphore_signal(
            barrier, inc=1, device_id={"dip": ring(my_d, k, dip_count)}, device_id_type=MESH
        )
    loads = [
        pltpu.make_async_copy(sources[i], loaded[i], load_sem.at[i]) for i in range(INPUTS)
    ]
    loads[1].start()
    for i in range(INPUTS):
        if i != 1:
            loads[i].start()
    loads[1].wait()
    pack_x(0, stress_in.at[0])
    pack_y(0, lambda z: stress_in[1, z])
    pl.semaphore_wait(barrier, strike_count + dip_count - 2)

    started = []
    halos = start_halos(0)
    started += halos
    for k in range(1, dip_count):
        pl.semaphore_signal(
            plane_sem, inc=1, device_id={"dip": ring(my_d, k, dip_count)}, device_id_type=MESH
        )
    for i in range(INPUTS):
        if i != 1:
            loads[i].wait()
    store_history()
    pl.semaphore_wait(plane_sem, dip_count - 1)
    exchanged = start_exchange(0)
    started += exchanged

    ghost = traction_in[...]
    front = min(3, depth)
    base = prestress[...] + functional_in[...]
    bound = bound_of(slip_in[...])
    wait_halos(halos)
    fill_padded(0, stress_in.at[0])
    for z in range(front):
        velocity_layer(0, z, vel_in, stress_in, ghost)
    traction, slip = slide(base + stress_z_layer(0, stress_in), bound, slip_in[...])
    dip_forward(0, [(my_d, slip)])
    started += start_a()
    for z in range(front, depth):
        velocity_layer(0, z, vel_in, stress_in, ghost)
    pack_x(1, vel)
    pack_y(1, lambda z: vel[z])
    halos = start_halos(1)
    started += halos
    started += start_gather(0, slip)
    started += start_gather(1, bound_of(slip))
    late = start_exchange(1)
    started += late
    arrange(0, exchanged)
    wait_halos(halos)
    stress_layers(1, stress_in)
    pack_x(2, stress.at[0])
    pack_y(2, lambda z: stress[1, z])
    halos = start_halos(2)
    started += halos
    wait_a()
    pieces = []
    for s in range(strike_count):
        piece = recv_a[0, s]
        for i in range(1, dip_count):
            piece = piece + recv_a[i, s]
        pieces.append(piece)
    spectra = [strike_forward(pieces)]
    strike_inverse(0, *convolve(0, spectra))
    started += start_c(0)

    wait_halos(halos)
    fill_padded(2, stress.at[0])
    for z in range(front):
        velocity_layer(2, z, vel, stress, traction)
    started += start_gather(2, prestress[...] + stress_z_layer(0, stress))
    for z in range(front, depth):
        velocity_layer(2, z, vel, stress, traction)
    pack_x(3, vel)
    pack_y(3, lambda z: vel[z])
    halos = start_halos(3)
    started += halos
    arrange(1, late)
    for turn in range(3):
        wait_gather(turn)
    wait_c(0)
    functionals = dip_inverse(0, range(dip_count))
    slips = []
    for i in range(dip_count):
        traction, slip = slide(gathered[2, i] + functionals[i], gathered[1, i], gathered[0, i])
        lines_out[0, i] = slip
        lines_out[1, i] = traction
        slips.append((i, slip))
    dip_forward(1, slips)
    started += start_b()
    wait_halos(halos)
    stress_layers(3, stress)
    saves = [
        pltpu.make_async_copy(vel, results[0], save_sem.at[0]),
        pltpu.make_async_copy(stress, results[1], save_sem.at[1]),
    ]
    for copy in saves:
        copy.start()
    wait_b()
    spectra = [strike_forward([recv_b[s] for s in range(strike_count)])] + spectra
    strike_inverse(1, *convolve(1, spectra))
    started += start_c(1)
    planes_out[0] = lines_out[0, my_d]
    planes_out[1] = lines_out[1, my_d]
    for copy in started:
        copy.wait_send()
    wait_c(1)
    planes_out[2] = dip_inverse(1, [my_d])[0]
    ends = [
        pltpu.make_async_copy(planes_out.at[i], results[2 + i], save_sem.at[2 + i]) for i in range(3)
    ]
    for copy in ends:
        copy.start()
    for copy in saves + ends:
        copy.wait()


def copy_kernel(*refs):
    sources, results, sems = refs[:5], refs[5:10], refs[10]
    saves = [pltpu.make_async_copy(sources[i], results[i], sems.at[i]) for i in range(5)]
    for save in saves:
        save.start()
    for save in saves:
        save.wait()


def fits_kernel(strike_count, dip_count, rows, cols, modes, total_x):
    return (
        STEPS == 2
        and strike_count > 1
        and dip_count > 1
        and modes == dip_count * SUBLANES
        and rows % SUBLANES == 0
        and cols == 2 * LANES
        and total_x == LANES
        and 2 * dip_count * rows == LANES
        and strike_count * dip_count * SUBLANES == cols
    )


def body(*args):
    velocity, history = args[0], args[11]
    strike_count = lax.axis_size("strike")
    dip_count = lax.axis_size("dip")
    depth, rows, cols = velocity.shape
    modes, total_x = history.shape[2:]
    if not fits_kernel(strike_count, dip_count, rows, cols, modes, total_x):
        return general_body(*args)
    half = SUBLANES // 2
    blocks = strike_count * dip_count
    total_y = cols * dip_count
    tables = (
        *split_table(dip_table(cols, total_y)),
        *split_table(strike_table(total_x)),
        twiddle_table(dip_count, cols, total_y),
    )
    turns = 2 * STEPS
    f32 = jnp.float32
    dma = pltpu.SemaphoreType.DMA
    operands = (*args, *[jnp.asarray(table) for table in tables])
    shapes = (velocity.shape, args[1].shape) + ((rows, cols),) * 3
    outs = tuple(jax.ShapeDtypeStruct(shape, f32) for shape in shapes)
    held = tuple(pltpu.VMEM(shape, f32) for shape in shapes)
    scratch = [pltpu.VMEM(operand.shape, operand.dtype) for operand in operands] + [
        pltpu.VMEM(velocity.shape, f32),
        pltpu.VMEM(args[1].shape, f32),
        pltpu.VMEM((3, rows, cols), f32),
        pltpu.VMEM((depth, rows + 2 * SUBLANES, cols), f32),
        pltpu.VMEM((turns, 2, depth, 2, cols), f32),
        pltpu.VMEM((turns, 2, rows, LANES), f32),
        pltpu.VMEM((turns, 2, depth, 2, cols), f32),
        pltpu.VMEM((turns, 2, rows, LANES), f32),
        pltpu.VMEM((3, rows, cols), f32),
        pltpu.VMEM((3, dip_count, rows, cols), f32),
        pltpu.VMEM((STEPS, blocks, half, LANES), f32),
        pltpu.VMEM((dip_count, strike_count, half, LANES), f32),
        pltpu.VMEM((strike_count, half, LANES), f32),
        pltpu.VMEM((STEPS, strike_count, half, LANES), f32),
        pltpu.VMEM((STEPS, blocks, half, LANES), f32),
        pltpu.VMEM((2, dip_count, rows, cols), f32),
        pltpu.VMEM((STEPS, 2, 3, modes + SUBLANES, total_x), f32),
        pltpu.VMEM((STEPS, 3, 1, total_x), f32),
        pltpu.VMEM((STEPS, 3, 1, total_x), f32),
        pltpu.VMEM((STEPS, 2, dip_count, SUBLANES, total_x), f32),
        pltpu.VMEM((STEPS, 2, dip_count, SUBLANES, total_x), f32),
        dma((len(operands),)),
        dma((len(outs),)),
        dma((turns, 4)),
        dma((turns, 4)),
        dma((3, dip_count)),
        dma((3, dip_count)),
        dma((dip_count, strike_count)),
        dma((dip_count, strike_count)),
        dma((strike_count,)),
        dma((strike_count,)),
        dma((STEPS, dip_count, strike_count)),
        dma((STEPS, dip_count, strike_count)),
        dma((STEPS, 2)),
        dma((STEPS, 2)),
        pltpu.SemaphoreType.REGULAR,
    ]
    anywhere = pl.BlockSpec(memory_space=pl.ANY)
    results = pl.pallas_call(
        functools.partial(rupture_kernel, strike_count, dip_count),
        out_shape=held,
        in_specs=[pl.BlockSpec(memory_space=pltpu.HBM)] * len(operands),
        out_specs=(anywhere,) * len(outs),
        scratch_shapes=scratch,
        compiler_params=pltpu.CompilerParams(
            collective_id=0, has_side_effects=True, vmem_limit_bytes=KERNEL_VMEM
        ),
    )(*operands)
    return pl.pallas_call(
        copy_kernel,
        out_shape=outs,
        in_specs=[anywhere] * len(outs),
        out_specs=(anywhere,) * len(outs),
        scratch_shapes=[dma((len(outs),))],
        compiler_params=pltpu.CompilerParams(vmem_limit_bytes=2**20),
    )(*results)


def solution(mesh):
    return jax.shard_map(
        body,
        mesh=mesh,
        in_specs=(
            P(None, "strike", "dip"),
            P(None, None, "strike", "dip"),
            P(None, "strike", "dip"),
            P(None, "strike", "dip"),
            P("strike", "dip"),
            P("strike", "dip"),
            P("strike", "dip"),
            P("strike", "dip"),
            P("strike", "dip"),
            P("strike", "dip"),
            P("strike", "dip"),
            P(None, None, ("strike", "dip"), None),
            P(None, ("strike", "dip"), None),
        ),
        out_specs=(
            P(None, "strike", "dip"),
            P(None, None, "strike", "dip"),
            P("strike", "dip"),
            P("strike", "dip"),
            P("strike", "dip"),
        ),
        check_vma=False,
    )
```

```python
import functools
import math

import jax
import jax.numpy as jnp
import numpy as np
from jax import lax
from jax.experimental import pallas as pl
from jax.experimental.pallas import tpu as pltpu
from jax.sharding import PartitionSpec as P

STEPS = 2


coef_near = 2.0 / 3.0
coef_far = -1.0 / 12.0
courant = 0.3
static_friction = 0.677
dynamic_friction = 0.525
damping = 0.5
time_step = 0.3


def padded_2(block, sides, width):
    for axis, dim in sides:
        count = lax.axis_size(axis)
        forward = [(i, i + 1) for i in range(count - 1)]
        forward.append((count - 1, 0))
        backward = [(target, source) for source, target in forward]
        low = lax.ppermute(
            lax.slice_in_dim(block, block.shape[dim] - width, None, axis=dim), axis, forward
        )
        high = lax.ppermute(lax.slice_in_dim(block, 0, width, axis=dim), axis, backward)
        block = jnp.concatenate([low, block, high], axis=dim)
    return block


def central(padded, axis, start, count):

    def window(offset):
        return lax.slice_in_dim(padded, start + offset, start + offset + count, axis=axis)

    return coef_near * (window(1) - window(-1)) + coef_far * (window(2) - window(-2))


def normal_diff(field, ghost):
    zeros = jnp.zeros_like(ghost)
    padded = jnp.concatenate([ghost, ghost, field, zeros, zeros], axis=0)
    return central(padded, 0, 2, field.shape[0])


def fault_update(prestress, normal_stress, crit_slip, flags, slip, stress_z, functional):
    trial = prestress + stress_z[0] + functional
    weaken = jnp.maximum(0.0, 1.0 - jnp.abs(slip) / crit_slip)
    strength = normal_stress * (dynamic_friction + (static_friction - dynamic_friction) * weaken)
    clipped = jnp.clip(trial, -strength, strength)
    traction = jnp.where(flags == 1, clipped, trial)
    rate = (trial - traction) / damping
    return (traction, slip + time_step * rate)


def factor_pair(length):
    first = 1
    candidate = 1
    while candidate * candidate <= length:
        if length % candidate == 0:
            first = candidate
        candidate += 1
    return (first, length // first)


def phase_table(count_a, count_b, length, sign):
    product = lax.iota(jnp.int32, count_a)[:, None] * lax.iota(jnp.int32, count_b)[None, :] % length
    angles = sign * 2.0 * math.pi / length * product.astype(jnp.float32)
    return (jnp.cos(angles), jnp.sin(angles))


def contract(form, left, right):
    return jnp.einsum(form, left, right, precision=lax.Precision.HIGHEST)


def transform_last(real_part, imag_part, sign):
    length = real_part.shape[-1]
    outer, inner = factor_pair(length)
    leading = real_part.shape[:-1]
    real_part = real_part.reshape(leading + (outer, inner))
    imag_part = imag_part.reshape(leading + (outer, inner))
    first_cos, first_sin = phase_table(outer, outer, outer, sign)
    middle_real = contract("kt,...tq->...kq", first_cos, real_part) - contract(
        "kt,...tq->...kq", first_sin, imag_part
    )
    middle_imag = contract("kt,...tq->...kq", first_cos, imag_part) + contract(
        "kt,...tq->...kq", first_sin, real_part
    )
    twist_cos, twist_sin = phase_table(outer, inner, length, sign)
    middle_real, middle_imag = (
        middle_real * twist_cos - middle_imag * twist_sin,
        middle_real * twist_sin + middle_imag * twist_cos,
    )
    second_cos, second_sin = phase_table(inner, inner, inner, sign)
    out_real = contract("...kt,tm->...km", middle_real, second_cos) - contract(
        "...kt,tm->...km", middle_imag, second_sin
    )
    out_imag = contract("...kt,tm->...km", middle_real, second_sin) + contract(
        "...kt,tm->...km", middle_imag, second_cos
    )
    scale = 1.0 / math.sqrt(length)
    out_real = jnp.swapaxes(out_real, -1, -2).reshape(leading + (length,)) * scale
    out_imag = jnp.swapaxes(out_imag, -1, -2).reshape(leading + (length,)) * scale
    return (out_real, out_imag)


def general_body(
    velocity,
    stress,
    shear_modulus,
    buoyancy,
    prestress,
    normal_stress,
    crit_slip,
    slip,
    traction,
    functional,
    flags,
    history,
    kernel,
):
    strike_count = lax.axis_size("strike")
    dip_count = lax.axis_size("dip")
    depth, rows_x, cols_y = velocity.shape
    ky_local = history.shape[2]
    total_x = history.shape[3]
    total_y = cols_y * dip_count
    line_rows = rows_x // dip_count
    stress_x, stress_y, stress_z = (stress[0], stress[1], stress[2])
    ghost_zero = jnp.zeros((1, rows_x, cols_y), jnp.float32)
    spectra = []
    for iteration in range(STEPS):
        padded_x = padded_2(stress_x, (("strike", 1),), 2)
        padded_y = padded_2(stress_y, (("dip", 2),), 2)
        divergence = (
            central(padded_x, 1, 2, rows_x)
            + central(padded_y, 2, 2, cols_y)
            + normal_diff(stress_z, traction[None])
        )
        velocity = velocity + courant * buoyancy * divergence
        padded_v = padded_2(velocity, (("strike", 1), ("dip", 2)), 2)
        grad_x = central(padded_v[:, :, 2 : cols_y + 2], 1, 2, rows_x)
        grad_y = central(padded_v[:, 2 : rows_x + 2, :], 2, 2, cols_y)
        stress_x = stress_x + courant * shear_modulus * grad_x
        stress_y = stress_y + courant * shear_modulus * grad_y
        stress_z = stress_z + courant * shear_modulus * normal_diff(velocity, ghost_zero)
        traction, slip = fault_update(
            prestress, normal_stress, crit_slip, flags, slip, stress_z, functional
        )
        lines = lax.all_to_all(slip, "dip", split_axis=0, concat_axis=1, tiled=True)
        part_real, part_imag = transform_last(lines, jnp.zeros_like(lines), -1.0)
        stacked = jnp.stack([part_real, part_imag]).reshape(
            2, line_rows, strike_count, dip_count, ky_local
        )
        stacked = stacked.transpose(0, 2, 3, 4, 1).reshape(
            2, strike_count, dip_count, ky_local, 1, 1, line_rows
        )
        halfway = lax.all_to_all(stacked, "strike", split_axis=1, concat_axis=4, tiled=True)
        owned = lax.all_to_all(halfway, "dip", split_axis=2, concat_axis=5, tiled=True)
        owned = owned.reshape(2, ky_local, total_x)
        spec_real, spec_imag = transform_last(owned[0], owned[1], -1.0)
        spectra = [(spec_real, spec_imag)] + spectra
        weights = kernel[iteration + 1 :].astype(jnp.float32)
        stored = jnp.sum(weights[:, None] * history[: history.shape[0] - iteration], axis=0)
        sum_real = stored[0]
        sum_imag = stored[1]
        for offset, item in enumerate(spectra):
            weight = kernel[offset].astype(jnp.float32)
            sum_real = sum_real + weight * item[0]
            sum_imag = sum_imag + weight * item[1]
        back_real, back_imag = transform_last(sum_real, sum_imag, 1.0)
        leaving = jnp.stack([back_real, back_imag]).reshape(
            2, 1, 1, ky_local, strike_count, dip_count, line_rows
        )
        partway = lax.all_to_all(leaving, "strike", split_axis=4, concat_axis=1, tiled=True)
        returned = lax.all_to_all(partway, "dip", split_axis=5, concat_axis=2, tiled=True)
        returned = returned.reshape(2, total_y, line_rows).transpose(0, 2, 1)
        field_real, field_imag = transform_last(returned[0], returned[1], 1.0)
        functional = lax.all_to_all(field_real, "dip", split_axis=1, concat_axis=0, tiled=True)
    return (velocity, jnp.stack([stress_x, stress_y, stress_z]), slip, traction, functional)


LANES = 128
SUBLANES = 8
MESH = pl.DeviceIdType.MESH
INPUTS = 18
KERNEL_VMEM = 67043328 - 1000000
HUGE = float(np.finfo(np.float32).max)


def split_bf16(value):
    high = value.astype(jnp.bfloat16)
    return high, (value - high.astype(jnp.float32)).astype(jnp.bfloat16)


def split_table(table):
    table = np.asarray(table, np.float32)
    high = table.astype(jnp.bfloat16)
    return high, (table - high.astype(np.float32)).astype(jnp.bfloat16)


def strike_table(total_x):
    index = np.arange(total_x)
    angle = 2.0 * np.pi / total_x * (index[:, None] * index[None, :] % total_x)
    return np.concatenate([np.cos(angle), np.sin(angle)], axis=1) / np.sqrt(total_x)


def dip_table(cols, total_y):
    count = cols // 2 + 2 * SUBLANES
    angle = 2.0 * np.pi / cols * (np.arange(count)[:, None] * np.arange(cols)[None, :] % cols)
    return np.concatenate([np.cos(angle), np.sin(angle)], axis=1) / np.sqrt(total_y)


def twiddle_table(dip_count, cols, total_y):
    place = np.arange(total_y).reshape(dip_count, 1, cols)
    freq = np.arange(dip_count)[None, :, None]
    angle = 2.0 * np.pi / total_y * (freq * place % total_y)
    return np.stack([np.cos(angle), -np.sin(angle)], axis=1).astype(np.float32)


def dot3(left, right_high, right_low):
    high, low = split_bf16(left)
    rows = left.shape[0]
    both = jnp.dot(
        jnp.concatenate([high, low], axis=0), right_high, preferred_element_type=jnp.float32
    )
    return both[:rows] + both[rows:] + jnp.dot(high, right_low, preferred_element_type=jnp.float32)


def dot3_nt(left_high, left_low, right):
    high, low = split_bf16(right)

    def product(a, b):
        return lax.dot_general(a, b, (((1,), (1,)), ((), ())), preferred_element_type=jnp.float32)

    return product(left_high, high) + product(left_high, low) + product(left_low, high)


def dot3_rows(left, right_high, right_low):
    high, low = split_bf16(left)
    rows = left.shape[0]

    def product(a, b):
        return lax.dot_general(a, b, (((1,), (1,)), ((), ())), preferred_element_type=jnp.float32)

    both = product(jnp.concatenate([high, low], axis=0), right_high)
    return both[:rows] + both[rows:] + product(high, right_low)


def rupture_kernel(strike_count, dip_count, *refs):
    sources, refs = refs[:INPUTS], refs[INPUTS:]
    results, refs = refs[:5], refs[5:]
    loaded, refs = refs[:INPUTS], refs[INPUTS:]
    (
        vel_in, stress_in, shear, buoy, prestress, normal_stress, crit_slip, slip_in, traction_in,
        functional_in, flags, hist, kern, dip_hi, dip_lo, strike_hi, strike_lo, twiddle,
    ) = loaded
    (
        vel, stress, planes_out, padded, edge_x, edge_y, halo_x, halo_y, send_f, recv_a,
        send_c, recv_c, modal, nought, nought_in, weight, source,
        load_sem, save_sem, edge_sem, halo_sem, a_send, a_recv, c_send, c_recv, x_send, x_recv, plane_sem,
    ) = refs
    depth, rows, cols = vel_in.shape
    modes = hist.shape[2]
    total_x = hist.shape[3]
    stored_count = hist.shape[0]
    blocks = strike_count * dip_count
    half = modes // dip_count // 2
    wave = dip_count * rows
    front_modes = cols // 2
    my_s = lax.axis_index("strike")
    my_d = lax.axis_index("dip")
    my_block = my_s * dip_count + my_d
    upper = my_block // (blocks // 2)

    def ring(me, offset, count):
        return lax.rem(me + offset + count, count)

    def remote(src, dst, send_sem, recv_sem, target):
        return pltpu.make_async_remote_copy(
            src_ref=src,
            dst_ref=dst,
            send_sem=send_sem,
            recv_sem=recv_sem,
            device_id=target,
            device_id_type=MESH,
        )

    lane = lax.broadcasted_iota(jnp.int32, (rows, LANES), 1)
    column = lax.broadcasted_iota(jnp.int32, (rows, cols), 1)
    strip = lax.broadcasted_iota(jnp.int32, (SUBLANES, LANES), 1) // rows
    layer_row = lax.broadcasted_iota(jnp.int32, (SUBLANES, LANES), 0)
    real_half = layer_row < half
    sign = jnp.where(real_half, 1.0, -1.0)
    lone = jnp.logical_and(layer_row % half == 0, my_block == 0)
    swap = functools.partial(pltpu.roll, shift=half, axis=0)

    def slot(block):
        high = block // (blocks // 2)
        return 2 * block + high * (2 * blocks - 1 - 4 * block)

    def pack_x(turn, field):
        edge_x[turn, 0] = field[:, rows - 2 : rows, :]
        edge_x[turn, 1] = field[:, 0:2, :]

    def pack_y(turn, layer):
        low = jnp.zeros((rows, LANES), jnp.float32)
        high = jnp.zeros((rows, LANES), jnp.float32)
        for z in range(depth):
            here = lane // 2 == z
            last = layer(z)[:, cols - LANES :]
            first = layer(z)[:, :LANES]
            low = jnp.where(here, pltpu.roll(last, (2 * z + 2) % LANES, 1), low)
            high = jnp.where(here, pltpu.roll(first, 2 * z, 1) if z else first, high)
        edge_y[turn, 0] = low
        edge_y[turn, 1] = high

    def halo_copies(turn):
        copies = []
        for side, step in ((0, 1), (1, -1)):
            copies.append(
                remote(
                    edge_x.at[turn, side],
                    halo_x.at[turn, side],
                    edge_sem.at[turn, side],
                    halo_sem.at[turn, side],
                    {"strike": ring(my_s, step, strike_count)},
                )
            )
            copies.append(
                remote(
                    edge_y.at[turn, side],
                    halo_y.at[turn, side],
                    edge_sem.at[turn, side + 2],
                    halo_sem.at[turn, side + 2],
                    {"dip": ring(my_d, step, dip_count)},
                )
            )
        return copies

    def start_halos(turn):
        copies = halo_copies(turn)
        for copy in copies:
            copy.start()
        return copies

    def wait_halos(copies):
        for copy in copies:
            copy.wait_recv()

    def fill_padded(turn, field):
        padded[:, SUBLANES : SUBLANES + rows, :] = field[...]
        padded[:, SUBLANES - 2 : SUBLANES, :] = halo_x[turn, 0]
        padded[:, SUBLANES + rows : SUBLANES + rows + 2, :] = halo_x[turn, 1]

    def diff_x(z):
        def window(offset):
            return padded[z, SUBLANES + offset : SUBLANES + offset + rows, :]

        return coef_near * (window(1) - window(-1)) + coef_far * (window(2) - window(-2))

    def diff_y(turn, z, field):
        low = halo_y[turn, 0]
        high = halo_y[turn, 1]
        low_0, low_1 = low[:, 2 * z : 2 * z + 1], low[:, 2 * z + 1 : 2 * z + 2]
        high_0, high_1 = high[:, 2 * z : 2 * z + 1], high[:, 2 * z + 1 : 2 * z + 2]
        back_1 = jnp.where(column == 0, low_1, pltpu.roll(field, 1, 1))
        back_2 = jnp.where(
            column == 0, low_0, jnp.where(column == 1, low_1, pltpu.roll(field, 2, 1))
        )
        next_1 = jnp.where(column == cols - 1, high_0, pltpu.roll(field, cols - 1, 1))
        next_2 = jnp.where(
            column == cols - 2,
            high_0,
            jnp.where(column == cols - 1, high_1, pltpu.roll(field, cols - 2, 1)),
        )
        return coef_near * (next_1 - back_1) + coef_far * (next_2 - back_2)

    def diff_z(z, layer, ghost):
        def at(index):
            if index < 0:
                return ghost
            return layer(index) if index < depth else None

        total = None
        for offset, coef in ((1, coef_near), (-1, -coef_near), (2, coef_far), (-2, -coef_far)):
            value = at(z + offset)
            if value is not None:
                total = coef * value if total is None else total + coef * value
        return total

    def velocity_layer(turn, z, source, stress_ref, traction):
        divergence = (
            diff_x(z)
            + diff_y(turn, z, stress_ref[1, z])
            + diff_z(z, lambda i: stress_ref[2, i], traction)
        )
        vel[z] = source[z] + courant * buoy[z] * divergence

    def stress_z_layer(z, stress_ref):
        return stress_ref[2, z] + courant * shear[z] * diff_z(z, lambda i: vel[i], None)

    def stress_layers(turn, stress_ref):
        fill_padded(turn, vel)
        for z in range(depth):
            modulus = courant * shear[z]
            stress[0, z] = stress_ref[0, z] + modulus * diff_x(z)
            stress[1, z] = stress_ref[1, z] + modulus * diff_y(turn, z, vel[z])
            stress[2, z] = stress_z_layer(z, stress_ref)

    offsets = [
        (i, k) for k in reversed(range(dip_count)) for i in reversed(range(strike_count)) if i or k
    ]

    def start_a(step):
        recv_a[step, my_d, my_s] = send_f[step, slot(my_block)]
        copies = []
        for i, k in offsets:
            target_s, target_d = ring(my_s, i, strike_count), ring(my_d, k, dip_count)
            copy = remote(
                send_f.at[step, slot(target_s * dip_count + target_d)],
                recv_a.at[step, my_d, my_s],
                a_send.at[step, k, i],
                a_recv.at[step, k, i],
                {"strike": target_s, "dip": target_d},
            )
            copy.start()
            copies.append(copy)
        return copies

    def wait_a(step):
        for i, k in reversed(offsets):
            source_s, source_d = ring(my_s, -i, strike_count), ring(my_d, -k, dip_count)
            remote(
                send_f.at[step, source_s],
                recv_a.at[step, source_d, source_s],
                a_send.at[step, k, i],
                a_recv.at[step, k, i],
                {"strike": source_s, "dip": source_d},
            ).wait_recv()

    def exchange_copies(turn):
        other = blocks - 1 - my_block
        single = 1 - jnp.minimum(lax.rem(my_block, blocks // 2), 1)
        mirror = lax.rem(blocks - my_block + single * (blocks // 2), blocks)
        upper_rows = pl.ds(modes // 2, modes // 2)
        return [
            remote(
                modal.at[turn, 0, :, upper_rows, :],
                modal.at[turn, 1, :, upper_rows, :],
                x_send.at[turn, 0],
                x_recv.at[turn, 0],
                {"strike": other // dip_count, "dip": lax.rem(other, dip_count)},
            ),
            remote(
                nought.at[turn],
                nought_in.at[turn],
                x_send.at[turn, 1],
                x_recv.at[turn, 1],
                {"strike": mirror // dip_count, "dip": lax.rem(mirror, dip_count)},
            ),
        ]

    def start_exchange(turn):
        copies = exchange_copies(turn)
        for copy in copies:
            copy.start()
        return copies

    def arrange(turn, copies):
        for copy in copies:
            copy.wait_recv()
        modal[turn, 1, :, modes : modes + 1, :] = nought_in[turn]
        for k0 in range(dip_count):
            for m in range(half):
                at = dip_count * m + k0
                plus = modal[turn, upper, :, pl.ds(modes // 2 * upper + at, 1), :]
                minus = modal[turn, 1 - upper, :, pl.ds(modes - modes // 2 * upper - at, 1), :]
                for side, value in enumerate((plus, minus)):
                    weight[turn, side, k0, m : m + 1, :] = value[0]
                    weight[turn, side, k0, half + m : half + m + 1, :] = value[0]
                    source[turn, side, k0, m : m + 1, :] = value[1]
                    source[turn, side, k0, half + m : half + m + 1, :] = value[2]

    def start_c(step):
        recv_c[step, slot(my_block)] = send_c[step, my_s]
        copies = []
        for i, k in offsets:
            target_s, target_d = ring(my_s, i, strike_count), ring(my_d, k, dip_count)
            copy = remote(
                send_c.at[step, target_s],
                recv_c.at[step, slot(my_block)],
                c_send.at[step, k, i],
                c_recv.at[step, k, i],
                {"strike": target_s, "dip": target_d},
            )
            copy.start()
            copies.append(copy)
        return copies

    def wait_c(step):
        for i, k in reversed(offsets):
            source_s, source_d = ring(my_s, -i, strike_count), ring(my_d, -k, dip_count)
            remote(
                send_c.at[step, source_s],
                recv_c.at[step, slot(source_s * dip_count + source_d)],
                c_send.at[step, k, i],
                c_recv.at[step, k, i],
                {"strike": source_s, "dip": source_d},
            ).wait_recv()

    def total_of(terms):
        total = None
        for left, right in terms:
            total = left * right if total is None else total + left * right
        return total

    def turned(i, part, k0):
        return twiddle[i, part, k0 : k0 + 1, :]

    def dip_forward(step, field):
        real, imag = (
            jnp.concatenate(
                [field * turned(my_d, kind, k0) for k0 in range(dip_count)], axis=0
            )
            for kind in range(2)
        )
        both = jnp.concatenate(
            [
                jnp.concatenate([real, imag], axis=1),
                jnp.concatenate([imag, -real], axis=1),
            ],
            axis=0,
        )
        out = dot3_nt(dip_hi[...], dip_lo[...], both)
        last = pltpu.roll(out[front_modes : front_modes + SUBLANES], wave, 1)
        first = jnp.where(
            jnp.logical_and(layer_row == 0, strip == dip_count), last, out[:SUBLANES]
        )
        out = jnp.concatenate([first, out[SUBLANES:front_modes]], axis=0)
        send_f[step] = out.reshape(blocks, half, LANES)

    def strike_forward(step):
        stacks = [None] * dip_count
        for s in range(strike_count):
            piece = recv_a[step, 0, s]
            for i in range(1, dip_count):
                piece = piece + recv_a[step, i, s]
            pair = jnp.concatenate([piece, pltpu.roll(piece, wave, 1)], axis=0)
            for k0 in range(dip_count):
                shift = rows * (s - k0) % LANES
                moved = pltpu.roll(pair, shift, 1) if shift else pair
                stacks[k0] = moved if s == 0 else jnp.where(strip == s, moved, stacks[k0])
        both = dot3(jnp.concatenate(stacks, axis=0), strike_hi[...], strike_lo[...])
        plus, minus = [], []
        for k0 in range(dip_count):
            tile = both[k0 * SUBLANES : (k0 + 1) * SUBLANES]
            cos, sin = tile[:, :total_x], tile[:, total_x:]
            crossed = swap(sin)
            ahead = cos + sign * crossed
            behind = sign * cos - crossed
            if k0 == 0:
                ahead = jnp.where(lone, jnp.where(real_half, cos, -crossed), ahead)
                behind = jnp.where(lone, jnp.where(real_half, swap(cos), -sin), behind)
            plus.append(ahead)
            minus.append(behind)
        return plus, minus

    def convolve(step, spectra):
        sums = []
        for side in range(2):
            tiles = []
            for k0 in range(dip_count):
                total = source[step, side, k0]
                for offset, item in enumerate(spectra):
                    total = total + weight[offset, side, k0] * item[side][k0]
                tiles.append(total)
            sums.append(tiles)
        return sums

    def strike_inverse(step, plus, minus):
        tiles = []
        for k0, (ahead, behind) in enumerate(zip(plus, minus)):
            direct = ahead + sign * behind
            crossed = -sign * swap(ahead - sign * behind)
            if k0 == 0:
                direct = jnp.where(lone, jnp.where(real_half, ahead, swap(behind)), direct)
                crossed = jnp.where(lone, -jnp.where(real_half, swap(ahead), behind), crossed)
            tiles.append(jnp.concatenate([direct, crossed], axis=1))
        out = dot3_rows(jnp.concatenate(tiles, axis=0), strike_hi[...], strike_lo[...])
        for s in range(strike_count):
            block = None
            for k0 in range(dip_count):
                shift = rows * (k0 - s) % LANES
                tile = out[k0 * SUBLANES : (k0 + 1) * SUBLANES]
                moved = pltpu.roll(tile, shift, 1) if shift else tile
                block = moved if k0 == 0 else jnp.where(strip == k0, moved, block)
            block = jnp.where(strip < dip_count, block, swap(pltpu.roll(block, wave, 1)))
            send_c[step, s] = block[:half]

    def dip_inverse(step):
        lines = recv_c[step].reshape(front_modes, LANES).T
        out = dot3(lines, dip_hi[:front_modes], dip_lo[:front_modes])
        real = out[:wave, :cols] - out[wave:, cols:]
        imag = out[:wave, cols:] + out[wave:, :cols]
        scale = 1.0 / math.sqrt(cols * dip_count)
        last = lines[wave : wave + rows, 0:1] * jnp.where(column % 2 == 0, scale, -scale)
        terms = [(real[:rows] + last, turned(my_d, 0, 0))]
        for k0 in range(1, dip_count):
            at = slice(k0 * rows, (k0 + 1) * rows)
            terms += [(real[at], turned(my_d, 0, k0)), (imag[at], turned(my_d, 1, k0))]
        return total_of(terms)

    def store_history():
        zero = jnp.zeros((2, modes, total_x), jnp.float32)
        common = stored_count - STEPS + 1

        def term(t, j):
            return kern[j + t + 1].astype(jnp.float32)[None] * hist[j]

        def add(j, sums):
            return tuple(total + term(t, j) for t, total in enumerate(sums))

        sums = lax.fori_loop(0, common, add, (zero,) * STEPS)
        for t in range(STEPS):
            total = sums[t]
            for j in range(common, stored_count - t):
                total = total + term(t, j)
            values = (kern[t].astype(jnp.float32), total[0], total[1])
            for i, value in enumerate(values):
                modal[t, 0, i, 0:modes, :] = value
                nought[t, i] = value[0:1]

    def bound_of(slip):
        weaken = jnp.maximum(0.0, 1.0 - jnp.abs(slip) / crit_slip[...])
        strength = normal_stress[...] * (
            dynamic_friction + (static_friction - dynamic_friction) * weaken
        )
        return jnp.where(flags[...] == 1, strength, HUGE)

    def slide(trial, bound, slip):
        traction = jnp.clip(trial, -bound, bound)
        return traction, slip + time_step * ((trial - traction) / damping)

    barrier = pltpu.get_barrier_semaphore()
    for k in range(1, strike_count):
        pl.semaphore_signal(
            barrier, inc=1, device_id={"strike": ring(my_s, k, strike_count)}, device_id_type=MESH
        )
    for k in range(1, dip_count):
        pl.semaphore_signal(
            barrier, inc=1, device_id={"dip": ring(my_d, k, dip_count)}, device_id_type=MESH
        )
    loads = [
        pltpu.make_async_copy(sources[i], loaded[i], load_sem.at[i]) for i in range(INPUTS)
    ]
    loads[1].start()
    for i in range(INPUTS):
        if i != 1:
            loads[i].start()
    loads[1].wait()
    pack_x(0, stress_in.at[0])
    pack_y(0, lambda z: stress_in[1, z])
    pl.semaphore_wait(barrier, strike_count + dip_count - 2)

    started = []
    halos = start_halos(0)
    started += halos
    for k in range(1, dip_count):
        pl.semaphore_signal(
            plane_sem, inc=1, device_id={"dip": ring(my_d, k, dip_count)}, device_id_type=MESH
        )
    for i in range(INPUTS):
        if i != 1:
            loads[i].wait()
    store_history()
    pl.semaphore_wait(plane_sem, dip_count - 1)
    exchanged = start_exchange(0)
    started += exchanged

    ghost = traction_in[...]
    front = min(3, depth)
    base = prestress[...] + functional_in[...]
    bound = bound_of(slip_in[...])
    wait_halos(halos)
    fill_padded(0, stress_in.at[0])
    for z in range(front):
        velocity_layer(0, z, vel_in, stress_in, ghost)
    traction, slip = slide(base + stress_z_layer(0, stress_in), bound, slip_in[...])
    dip_forward(0, slip)
    started += start_a(0)
    for z in range(front, depth):
        velocity_layer(0, z, vel_in, stress_in, ghost)
    pack_x(1, vel)
    pack_y(1, lambda z: vel[z])
    halos = start_halos(1)
    started += halos
    late = start_exchange(1)
    started += late
    arrange(0, exchanged)
    wait_halos(halos)
    stress_layers(1, stress_in)
    pack_x(2, stress.at[0])
    pack_y(2, lambda z: stress[1, z])
    halos = start_halos(2)
    started += halos
    wait_a(0)
    spectra = [strike_forward(0)]
    strike_inverse(0, *convolve(0, spectra))
    started += start_c(0)

    wait_halos(halos)
    fill_padded(2, stress.at[0])
    for z in range(front):
        velocity_layer(2, z, vel, stress, traction)
    for z in range(front, depth):
        velocity_layer(2, z, vel, stress, traction)
    pack_x(3, vel)
    pack_y(3, lambda z: vel[z])
    halos = start_halos(3)
    started += halos
    arrange(1, late)
    base = prestress[...] + stress_z_layer(0, stress)
    bound = bound_of(slip)
    wait_c(0)
    traction, slip = slide(base + dip_inverse(0), bound, slip)
    dip_forward(1, slip)
    started += start_a(1)
    planes_out[0] = slip
    planes_out[1] = traction
    wait_halos(halos)
    stress_layers(3, stress)
    saves = [
        pltpu.make_async_copy(vel, results[0], save_sem.at[0]),
        pltpu.make_async_copy(stress, results[1], save_sem.at[1]),
    ]
    for copy in saves:
        copy.start()
    wait_a(1)
    spectra = [strike_forward(1)] + spectra
    strike_inverse(1, *convolve(1, spectra))
    started += start_c(1)
    for copy in started:
        copy.wait_send()
    wait_c(1)
    planes_out[2] = dip_inverse(1)
    ends = [
        pltpu.make_async_copy(planes_out.at[i], results[2 + i], save_sem.at[2 + i]) for i in range(3)
    ]
    for copy in ends:
        copy.start()
    for copy in saves + ends:
        copy.wait()


def copy_kernel(*refs):
    sources, results, sems = refs[:5], refs[5:10], refs[10]
    saves = [pltpu.make_async_copy(sources[i], results[i], sems.at[i]) for i in range(5)]
    for save in saves:
        save.start()
    for save in saves:
        save.wait()


def fits_kernel(strike_count, dip_count, rows, cols, modes, total_x):
    return (
        STEPS == 2
        and strike_count > 1
        and dip_count > 1
        and modes == dip_count * SUBLANES
        and rows % SUBLANES == 0
        and cols == 2 * LANES
        and total_x == LANES
        and 2 * dip_count * rows == LANES
        and strike_count * dip_count * SUBLANES == cols
    )


def body(*args):
    velocity, history = args[0], args[11]
    strike_count = lax.axis_size("strike")
    dip_count = lax.axis_size("dip")
    depth, rows, cols = velocity.shape
    modes, total_x = history.shape[2:]
    if not fits_kernel(strike_count, dip_count, rows, cols, modes, total_x):
        return general_body(*args)
    half = SUBLANES // 2
    blocks = strike_count * dip_count
    total_y = cols * dip_count
    tables = (
        *split_table(dip_table(cols, total_y)),
        *split_table(strike_table(total_x)),
        twiddle_table(dip_count, cols, total_y),
    )
    turns = 2 * STEPS
    f32 = jnp.float32
    dma = pltpu.SemaphoreType.DMA
    operands = (*args, *[jnp.asarray(table) for table in tables])
    shapes = (velocity.shape, args[1].shape) + ((rows, cols),) * 3
    outs = tuple(jax.ShapeDtypeStruct(shape, f32) for shape in shapes)
    held = tuple(pltpu.VMEM(shape, f32) for shape in shapes)
    scratch = [pltpu.VMEM(operand.shape, operand.dtype) for operand in operands] + [
        pltpu.VMEM(velocity.shape, f32),
        pltpu.VMEM(args[1].shape, f32),
        pltpu.VMEM((3, rows, cols), f32),
        pltpu.VMEM((depth, rows + 2 * SUBLANES, cols), f32),
        pltpu.VMEM((turns, 2, depth, 2, cols), f32),
        pltpu.VMEM((turns, 2, rows, LANES), f32),
        pltpu.VMEM((turns, 2, depth, 2, cols), f32),
        pltpu.VMEM((turns, 2, rows, LANES), f32),
        pltpu.VMEM((STEPS, blocks, half, LANES), f32),
        pltpu.VMEM((STEPS, dip_count, strike_count, half, LANES), f32),
        pltpu.VMEM((STEPS, strike_count, half, LANES), f32),
        pltpu.VMEM((STEPS, blocks, half, LANES), f32),
        pltpu.VMEM((STEPS, 2, 3, modes + SUBLANES, total_x), f32),
        pltpu.VMEM((STEPS, 3, 1, total_x), f32),
        pltpu.VMEM((STEPS, 3, 1, total_x), f32),
        pltpu.VMEM((STEPS, 2, dip_count, SUBLANES, total_x), f32),
        pltpu.VMEM((STEPS, 2, dip_count, SUBLANES, total_x), f32),
        dma((len(operands),)),
        dma((len(outs),)),
        dma((turns, 4)),
        dma((turns, 4)),
        dma((STEPS, dip_count, strike_count)),
        dma((STEPS, dip_count, strike_count)),
        dma((STEPS, dip_count, strike_count)),
        dma((STEPS, dip_count, strike_count)),
        dma((STEPS, 2)),
        dma((STEPS, 2)),
        pltpu.SemaphoreType.REGULAR,
    ]
    anywhere = pl.BlockSpec(memory_space=pl.ANY)
    results = pl.pallas_call(
        functools.partial(rupture_kernel, strike_count, dip_count),
        out_shape=held,
        in_specs=[pl.BlockSpec(memory_space=pltpu.HBM)] * len(operands),
        out_specs=(anywhere,) * len(outs),
        scratch_shapes=scratch,
        compiler_params=pltpu.CompilerParams(
            collective_id=0, has_side_effects=True, vmem_limit_bytes=KERNEL_VMEM
        ),
    )(*operands)
    return pl.pallas_call(
        copy_kernel,
        out_shape=outs,
        in_specs=[anywhere] * len(outs),
        out_specs=(anywhere,) * len(outs),
        scratch_shapes=[dma((len(outs),))],
        compiler_params=pltpu.CompilerParams(vmem_limit_bytes=2**20),
    )(*results)


def solution(mesh):
    return jax.shard_map(
        body,
        mesh=mesh,
        in_specs=(
            P(None, "strike", "dip"),
            P(None, None, "strike", "dip"),
            P(None, "strike", "dip"),
            P(None, "strike", "dip"),
            P("strike", "dip"),
            P("strike", "dip"),
            P("strike", "dip"),
            P("strike", "dip"),
            P("strike", "dip"),
            P("strike", "dip"),
            P("strike", "dip"),
            P(None, None, ("strike", "dip"), None),
            P(None, ("strike", "dip"), None),
        ),
        out_specs=(
            P(None, "strike", "dip"),
            P(None, None, "strike", "dip"),
            P("strike", "dip"),
            P("strike", "dip"),
            P("strike", "dip"),
        ),
        check_vma=False,
    )
```

```python
import functools
import math

import jax
import jax.numpy as jnp
import numpy as np
from jax import lax
from jax.experimental import pallas as pl
from jax.experimental.pallas import tpu as pltpu
from jax.sharding import PartitionSpec as P

STEPS = 2


coef_near = 2.0 / 3.0
coef_far = -1.0 / 12.0
courant = 0.3
static_friction = 0.677
dynamic_friction = 0.525
damping = 0.5
time_step = 0.3


def padded_2(block, sides, width):
    for axis, dim in sides:
        count = lax.axis_size(axis)
        forward = [(i, i + 1) for i in range(count - 1)]
        forward.append((count - 1, 0))
        backward = [(target, source) for source, target in forward]
        low = lax.ppermute(
            lax.slice_in_dim(block, block.shape[dim] - width, None, axis=dim), axis, forward
        )
        high = lax.ppermute(lax.slice_in_dim(block, 0, width, axis=dim), axis, backward)
        block = jnp.concatenate([low, block, high], axis=dim)
    return block


def central(padded, axis, start, count):

    def window(offset):
        return lax.slice_in_dim(padded, start + offset, start + offset + count, axis=axis)

    return coef_near * (window(1) - window(-1)) + coef_far * (window(2) - window(-2))


def normal_diff(field, ghost):
    zeros = jnp.zeros_like(ghost)
    padded = jnp.concatenate([ghost, ghost, field, zeros, zeros], axis=0)
    return central(padded, 0, 2, field.shape[0])


def fault_update(prestress, normal_stress, crit_slip, flags, slip, stress_z, functional):
    trial = prestress + stress_z[0] + functional
    weaken = jnp.maximum(0.0, 1.0 - jnp.abs(slip) / crit_slip)
    strength = normal_stress * (dynamic_friction + (static_friction - dynamic_friction) * weaken)
    clipped = jnp.clip(trial, -strength, strength)
    traction = jnp.where(flags == 1, clipped, trial)
    rate = (trial - traction) / damping
    return (traction, slip + time_step * rate)


def factor_pair(length):
    first = 1
    candidate = 1
    while candidate * candidate <= length:
        if length % candidate == 0:
            first = candidate
        candidate += 1
    return (first, length // first)


def phase_table(count_a, count_b, length, sign):
    product = lax.iota(jnp.int32, count_a)[:, None] * lax.iota(jnp.int32, count_b)[None, :] % length
    angles = sign * 2.0 * math.pi / length * product.astype(jnp.float32)
    return (jnp.cos(angles), jnp.sin(angles))


def contract(form, left, right):
    return jnp.einsum(form, left, right, precision=lax.Precision.HIGHEST)


def transform_last(real_part, imag_part, sign):
    length = real_part.shape[-1]
    outer, inner = factor_pair(length)
    leading = real_part.shape[:-1]
    real_part = real_part.reshape(leading + (outer, inner))
    imag_part = imag_part.reshape(leading + (outer, inner))
    first_cos, first_sin = phase_table(outer, outer, outer, sign)
    middle_real = contract("kt,...tq->...kq", first_cos, real_part) - contract(
        "kt,...tq->...kq", first_sin, imag_part
    )
    middle_imag = contract("kt,...tq->...kq", first_cos, imag_part) + contract(
        "kt,...tq->...kq", first_sin, real_part
    )
    twist_cos, twist_sin = phase_table(outer, inner, length, sign)
    middle_real, middle_imag = (
        middle_real * twist_cos - middle_imag * twist_sin,
        middle_real * twist_sin + middle_imag * twist_cos,
    )
    second_cos, second_sin = phase_table(inner, inner, inner, sign)
    out_real = contract("...kt,tm->...km", middle_real, second_cos) - contract(
        "...kt,tm->...km", middle_imag, second_sin
    )
    out_imag = contract("...kt,tm->...km", middle_real, second_sin) + contract(
        "...kt,tm->...km", middle_imag, second_cos
    )
    scale = 1.0 / math.sqrt(length)
    out_real = jnp.swapaxes(out_real, -1, -2).reshape(leading + (length,)) * scale
    out_imag = jnp.swapaxes(out_imag, -1, -2).reshape(leading + (length,)) * scale
    return (out_real, out_imag)


def general_body(
    velocity,
    stress,
    shear_modulus,
    buoyancy,
    prestress,
    normal_stress,
    crit_slip,
    slip,
    traction,
    functional,
    flags,
    history,
    kernel,
):
    strike_count = lax.axis_size("strike")
    dip_count = lax.axis_size("dip")
    depth, rows_x, cols_y = velocity.shape
    ky_local = history.shape[2]
    total_x = history.shape[3]
    total_y = cols_y * dip_count
    line_rows = rows_x // dip_count
    stress_x, stress_y, stress_z = (stress[0], stress[1], stress[2])
    ghost_zero = jnp.zeros((1, rows_x, cols_y), jnp.float32)
    spectra = []
    for iteration in range(STEPS):
        padded_x = padded_2(stress_x, (("strike", 1),), 2)
        padded_y = padded_2(stress_y, (("dip", 2),), 2)
        divergence = (
            central(padded_x, 1, 2, rows_x)
            + central(padded_y, 2, 2, cols_y)
            + normal_diff(stress_z, traction[None])
        )
        velocity = velocity + courant * buoyancy * divergence
        padded_v = padded_2(velocity, (("strike", 1), ("dip", 2)), 2)
        grad_x = central(padded_v[:, :, 2 : cols_y + 2], 1, 2, rows_x)
        grad_y = central(padded_v[:, 2 : rows_x + 2, :], 2, 2, cols_y)
        stress_x = stress_x + courant * shear_modulus * grad_x
        stress_y = stress_y + courant * shear_modulus * grad_y
        stress_z = stress_z + courant * shear_modulus * normal_diff(velocity, ghost_zero)
        traction, slip = fault_update(
            prestress, normal_stress, crit_slip, flags, slip, stress_z, functional
        )
        lines = lax.all_to_all(slip, "dip", split_axis=0, concat_axis=1, tiled=True)
        part_real, part_imag = transform_last(lines, jnp.zeros_like(lines), -1.0)
        stacked = jnp.stack([part_real, part_imag]).reshape(
            2, line_rows, strike_count, dip_count, ky_local
        )
        stacked = stacked.transpose(0, 2, 3, 4, 1).reshape(
            2, strike_count, dip_count, ky_local, 1, 1, line_rows
        )
        halfway = lax.all_to_all(stacked, "strike", split_axis=1, concat_axis=4, tiled=True)
        owned = lax.all_to_all(halfway, "dip", split_axis=2, concat_axis=5, tiled=True)
        owned = owned.reshape(2, ky_local, total_x)
        spec_real, spec_imag = transform_last(owned[0], owned[1], -1.0)
        spectra = [(spec_real, spec_imag)] + spectra
        weights = kernel[iteration + 1 :].astype(jnp.float32)
        stored = jnp.sum(weights[:, None] * history[: history.shape[0] - iteration], axis=0)
        sum_real = stored[0]
        sum_imag = stored[1]
        for offset, item in enumerate(spectra):
            weight = kernel[offset].astype(jnp.float32)
            sum_real = sum_real + weight * item[0]
            sum_imag = sum_imag + weight * item[1]
        back_real, back_imag = transform_last(sum_real, sum_imag, 1.0)
        leaving = jnp.stack([back_real, back_imag]).reshape(
            2, 1, 1, ky_local, strike_count, dip_count, line_rows
        )
        partway = lax.all_to_all(leaving, "strike", split_axis=4, concat_axis=1, tiled=True)
        returned = lax.all_to_all(partway, "dip", split_axis=5, concat_axis=2, tiled=True)
        returned = returned.reshape(2, total_y, line_rows).transpose(0, 2, 1)
        field_real, field_imag = transform_last(returned[0], returned[1], 1.0)
        functional = lax.all_to_all(field_real, "dip", split_axis=1, concat_axis=0, tiled=True)
    return (velocity, jnp.stack([stress_x, stress_y, stress_z]), slip, traction, functional)


LANES = 128
SUBLANES = 8
MESH = pl.DeviceIdType.MESH
INPUTS = 18
KERNEL_VMEM = 67043328 - 1000000
HUGE = float(np.finfo(np.float32).max)


def split_bf16(value):
    high = value.astype(jnp.bfloat16)
    return high, (value - high.astype(jnp.float32)).astype(jnp.bfloat16)


def split_table(table):
    table = np.asarray(table, np.float32)
    high = table.astype(jnp.bfloat16)
    return high, (table - high.astype(np.float32)).astype(jnp.bfloat16)


def strike_table(total_x):
    index = np.arange(total_x)
    angle = 2.0 * np.pi / total_x * (index[:, None] * index[None, :] % total_x)
    return np.concatenate([np.cos(angle), np.sin(angle)], axis=1) / np.sqrt(total_x)


def dip_table(cols, total_y):
    count = cols // 2 + 2 * SUBLANES
    angle = 2.0 * np.pi / cols * (np.arange(count)[:, None] * np.arange(cols)[None, :] % cols)
    return np.concatenate([np.cos(angle), np.sin(angle)], axis=1) / np.sqrt(total_y)


def twiddle_table(dip_count, cols, total_y):
    place = np.arange(total_y).reshape(dip_count, 1, cols)
    freq = np.arange(dip_count)[None, :, None]
    angle = 2.0 * np.pi / total_y * (freq * place % total_y)
    return np.stack([np.cos(angle), -np.sin(angle)], axis=1).astype(np.float32)


def dot3(left, right_high, right_low):
    high, low = split_bf16(left)
    rows = left.shape[0]
    both = jnp.dot(
        jnp.concatenate([high, low], axis=0), right_high, preferred_element_type=jnp.float32
    )
    return both[:rows] + both[rows:] + jnp.dot(high, right_low, preferred_element_type=jnp.float32)


def dot3_nt(left_high, left_low, right):
    high, low = split_bf16(right)

    def product(a, b):
        return lax.dot_general(a, b, (((1,), (1,)), ((), ())), preferred_element_type=jnp.float32)

    return product(left_high, high) + product(left_high, low) + product(left_low, high)


def dot3_rows(left, right_high, right_low):
    high, low = split_bf16(left)
    rows = left.shape[0]

    def product(a, b):
        return lax.dot_general(a, b, (((1,), (1,)), ((), ())), preferred_element_type=jnp.float32)

    both = product(jnp.concatenate([high, low], axis=0), right_high)
    return both[:rows] + both[rows:] + product(high, right_low)


def rupture_kernel(strike_count, dip_count, *refs):
    sources, refs = refs[:INPUTS], refs[INPUTS:]
    results, refs = refs[:5], refs[5:]
    loaded, refs = refs[:INPUTS], refs[INPUTS:]
    (
        vel_in, stress_in, shear, buoy, prestress, normal_stress, crit_slip, slip_in, traction_in,
        functional_in, flags, hist, kern, dip_hi, dip_lo, strike_hi, strike_lo, twiddle,
    ) = loaded
    (
        padded, edge_x, edge_y, halo_x, halo_y, send_f, recv_a,
        send_c, recv_c, modal, nought, nought_in, weight, source,
        load_sem, edge_sem, halo_sem, a_send, a_recv, c_send, c_recv, x_send, x_recv, plane_sem,
    ) = refs
    vel, stress = results[:2]
    depth, rows, cols = vel_in.shape
    modes = hist.shape[2]
    total_x = hist.shape[3]
    stored_count = hist.shape[0]
    blocks = strike_count * dip_count
    half = modes // dip_count // 2
    wave = dip_count * rows
    front_modes = cols // 2
    my_s = lax.axis_index("strike")
    my_d = lax.axis_index("dip")
    my_block = my_s * dip_count + my_d
    upper = my_block // (blocks // 2)

    def ring(me, offset, count):
        return lax.rem(me + offset + count, count)

    def remote(src, dst, send_sem, recv_sem, target):
        return pltpu.make_async_remote_copy(
            src_ref=src,
            dst_ref=dst,
            send_sem=send_sem,
            recv_sem=recv_sem,
            device_id=target,
            device_id_type=MESH,
        )

    lane = lax.broadcasted_iota(jnp.int32, (rows, LANES), 1)
    column = lax.broadcasted_iota(jnp.int32, (rows, cols), 1)
    strip = lax.broadcasted_iota(jnp.int32, (SUBLANES, LANES), 1) // rows
    layer_row = lax.broadcasted_iota(jnp.int32, (SUBLANES, LANES), 0)
    real_half = layer_row < half
    sign = jnp.where(real_half, 1.0, -1.0)
    lone = jnp.logical_and(layer_row % half == 0, my_block == 0)
    swap = functools.partial(pltpu.roll, shift=half, axis=0)

    def slot(block):
        high = block // (blocks // 2)
        return 2 * block + high * (2 * blocks - 1 - 4 * block)

    def pack_x(turn, field):
        edge_x[turn, 0] = field[:, rows - 2 : rows, :]
        edge_x[turn, 1] = field[:, 0:2, :]

    def pack_y(turn, layer):
        low = jnp.zeros((rows, LANES), jnp.float32)
        high = jnp.zeros((rows, LANES), jnp.float32)
        for z in range(depth):
            here = lane // 2 == z
            last = layer(z)[:, cols - LANES :]
            first = layer(z)[:, :LANES]
            low = jnp.where(here, pltpu.roll(last, (2 * z + 2) % LANES, 1), low)
            high = jnp.where(here, pltpu.roll(first, 2 * z, 1) if z else first, high)
        edge_y[turn, 0] = low
        edge_y[turn, 1] = high

    def halo_copies(turn):
        copies = []
        for side, step in ((0, 1), (1, -1)):
            copies.append(
                remote(
                    edge_x.at[turn, side],
                    halo_x.at[turn, side],
                    edge_sem.at[turn, side],
                    halo_sem.at[turn, side],
                    {"strike": ring(my_s, step, strike_count)},
                )
            )
            copies.append(
                remote(
                    edge_y.at[turn, side],
                    halo_y.at[turn, side],
                    edge_sem.at[turn, side + 2],
                    halo_sem.at[turn, side + 2],
                    {"dip": ring(my_d, step, dip_count)},
                )
            )
        return copies

    def start_halos(turn):
        copies = halo_copies(turn)
        for copy in copies:
            copy.start()
        return copies

    def wait_halos(copies):
        for copy in copies:
            copy.wait_recv()

    def fill_padded(turn, field):
        padded[:, SUBLANES : SUBLANES + rows, :] = field[...]
        padded[:, SUBLANES - 2 : SUBLANES, :] = halo_x[turn, 0]
        padded[:, SUBLANES + rows : SUBLANES + rows + 2, :] = halo_x[turn, 1]

    def diff_x(z):
        def window(offset):
            return padded[z, SUBLANES + offset : SUBLANES + offset + rows, :]

        return coef_near * (window(1) - window(-1)) + coef_far * (window(2) - window(-2))

    def diff_y(turn, z, field):
        low = halo_y[turn, 0]
        high = halo_y[turn, 1]
        low_0, low_1 = low[:, 2 * z : 2 * z + 1], low[:, 2 * z + 1 : 2 * z + 2]
        high_0, high_1 = high[:, 2 * z : 2 * z + 1], high[:, 2 * z + 1 : 2 * z + 2]
        back_1 = jnp.where(column == 0, low_1, pltpu.roll(field, 1, 1))
        back_2 = jnp.where(
            column == 0, low_0, jnp.where(column == 1, low_1, pltpu.roll(field, 2, 1))
        )
        next_1 = jnp.where(column == cols - 1, high_0, pltpu.roll(field, cols - 1, 1))
        next_2 = jnp.where(
            column == cols - 2,
            high_0,
            jnp.where(column == cols - 1, high_1, pltpu.roll(field, cols - 2, 1)),
        )
        return coef_near * (next_1 - back_1) + coef_far * (next_2 - back_2)

    def diff_z(z, layer, ghost):
        def at(index):
            if index < 0:
                return ghost
            return layer(index) if index < depth else None

        total = None
        for offset, coef in ((1, coef_near), (-1, -coef_near), (2, coef_far), (-2, -coef_far)):
            value = at(z + offset)
            if value is not None:
                total = coef * value if total is None else total + coef * value
        return total

    def velocity_layer(turn, z, source, stress_ref, traction):
        divergence = (
            diff_x(z)
            + diff_y(turn, z, stress_ref[1, z])
            + diff_z(z, lambda i: stress_ref[2, i], traction)
        )
        vel[z] = source[z] + courant * buoy[z] * divergence

    def stress_z_layer(z, stress_ref):
        return stress_ref[2, z] + courant * shear[z] * diff_z(z, lambda i: vel[i], None)

    def stress_layers(turn, stress_ref):
        fill_padded(turn, vel)
        for z in range(depth):
            modulus = courant * shear[z]
            stress[0, z] = stress_ref[0, z] + modulus * diff_x(z)
            stress[1, z] = stress_ref[1, z] + modulus * diff_y(turn, z, vel[z])
            stress[2, z] = stress_z_layer(z, stress_ref)

    offsets = [
        (i, k) for k in reversed(range(dip_count)) for i in reversed(range(strike_count)) if i or k
    ]

    def start_a(step):
        recv_a[step, my_d, my_s] = send_f[step, slot(my_block)]
        copies = []
        for i, k in offsets:
            target_s, target_d = ring(my_s, i, strike_count), ring(my_d, k, dip_count)
            copy = remote(
                send_f.at[step, slot(target_s * dip_count + target_d)],
                recv_a.at[step, my_d, my_s],
                a_send.at[step, k, i],
                a_recv.at[step, k, i],
                {"strike": target_s, "dip": target_d},
            )
            copy.start()
            copies.append(copy)
        return copies

    def wait_a(step):
        for i, k in reversed(offsets):
            source_s, source_d = ring(my_s, -i, strike_count), ring(my_d, -k, dip_count)
            remote(
                send_f.at[step, source_s],
                recv_a.at[step, source_d, source_s],
                a_send.at[step, k, i],
                a_recv.at[step, k, i],
                {"strike": source_s, "dip": source_d},
            ).wait_recv()

    def exchange_copies(turn):
        other = blocks - 1 - my_block
        single = 1 - jnp.minimum(lax.rem(my_block, blocks // 2), 1)
        mirror = lax.rem(blocks - my_block + single * (blocks // 2), blocks)
        upper_rows = pl.ds(modes // 2, modes // 2)
        return [
            remote(
                modal.at[turn, 0, :, upper_rows, :],
                modal.at[turn, 1, :, upper_rows, :],
                x_send.at[turn, 0],
                x_recv.at[turn, 0],
                {"strike": other // dip_count, "dip": lax.rem(other, dip_count)},
            ),
            remote(
                nought.at[turn],
                nought_in.at[turn],
                x_send.at[turn, 1],
                x_recv.at[turn, 1],
                {"strike": mirror // dip_count, "dip": lax.rem(mirror, dip_count)},
            ),
        ]

    def start_exchange(turn):
        copies = exchange_copies(turn)
        for copy in copies:
            copy.start()
        return copies

    def arrange(turn, copies):
        for copy in copies:
            copy.wait_recv()
        modal[turn, 1, :, modes : modes + 1, :] = nought_in[turn]
        for k0 in range(dip_count):
            for m in range(half):
                at = dip_count * m + k0
                plus = modal[turn, upper, :, pl.ds(modes // 2 * upper + at, 1), :]
                minus = modal[turn, 1 - upper, :, pl.ds(modes - modes // 2 * upper - at, 1), :]
                for side, value in enumerate((plus, minus)):
                    weight[turn, side, k0, m : m + 1, :] = value[0]
                    weight[turn, side, k0, half + m : half + m + 1, :] = value[0]
                    source[turn, side, k0, m : m + 1, :] = value[1]
                    source[turn, side, k0, half + m : half + m + 1, :] = value[2]

    def start_c(step):
        recv_c[step, slot(my_block)] = send_c[step, my_s]
        copies = []
        for i, k in offsets:
            target_s, target_d = ring(my_s, i, strike_count), ring(my_d, k, dip_count)
            copy = remote(
                send_c.at[step, target_s],
                recv_c.at[step, slot(my_block)],
                c_send.at[step, k, i],
                c_recv.at[step, k, i],
                {"strike": target_s, "dip": target_d},
            )
            copy.start()
            copies.append(copy)
        return copies

    def wait_c(step):
        for i, k in reversed(offsets):
            source_s, source_d = ring(my_s, -i, strike_count), ring(my_d, -k, dip_count)
            remote(
                send_c.at[step, source_s],
                recv_c.at[step, slot(source_s * dip_count + source_d)],
                c_send.at[step, k, i],
                c_recv.at[step, k, i],
                {"strike": source_s, "dip": source_d},
            ).wait_recv()

    def total_of(terms):
        total = None
        for left, right in terms:
            total = left * right if total is None else total + left * right
        return total

    def turned(i, part, k0):
        return twiddle[i, part, k0 : k0 + 1, :]

    def dip_forward(step, field):
        real, imag = (
            jnp.concatenate(
                [field * turned(my_d, kind, k0) for k0 in range(dip_count)], axis=0
            )
            for kind in range(2)
        )
        both = jnp.concatenate(
            [
                jnp.concatenate([real, imag], axis=1),
                jnp.concatenate([imag, -real], axis=1),
            ],
            axis=0,
        )
        out = dot3_nt(dip_hi[...], dip_lo[...], both)
        last = pltpu.roll(out[front_modes : front_modes + SUBLANES], wave, 1)
        first = jnp.where(
            jnp.logical_and(layer_row == 0, strip == dip_count), last, out[:SUBLANES]
        )
        out = jnp.concatenate([first, out[SUBLANES:front_modes]], axis=0)
        send_f[step] = out.reshape(blocks, half, LANES)

    def strike_forward(step):
        stacks = [None] * dip_count
        for s in range(strike_count):
            piece = recv_a[step, 0, s]
            for i in range(1, dip_count):
                piece = piece + recv_a[step, i, s]
            pair = jnp.concatenate([piece, pltpu.roll(piece, wave, 1)], axis=0)
            for k0 in range(dip_count):
                shift = rows * (s - k0) % LANES
                moved = pltpu.roll(pair, shift, 1) if shift else pair
                stacks[k0] = moved if s == 0 else jnp.where(strip == s, moved, stacks[k0])
        both = dot3(jnp.concatenate(stacks, axis=0), strike_hi[...], strike_lo[...])
        plus, minus = [], []
        for k0 in range(dip_count):
            tile = both[k0 * SUBLANES : (k0 + 1) * SUBLANES]
            cos, sin = tile[:, :total_x], tile[:, total_x:]
            crossed = swap(sin)
            ahead = cos + sign * crossed
            behind = sign * cos - crossed
            if k0 == 0:
                ahead = jnp.where(lone, jnp.where(real_half, cos, -crossed), ahead)
                behind = jnp.where(lone, jnp.where(real_half, swap(cos), -sin), behind)
            plus.append(ahead)
            minus.append(behind)
        return plus, minus

    def convolve(step, spectra):
        sums = []
        for side in range(2):
            tiles = []
            for k0 in range(dip_count):
                total = source[step, side, k0]
                for offset, item in enumerate(spectra):
                    total = total + weight[offset, side, k0] * item[side][k0]
                tiles.append(total)
            sums.append(tiles)
        return sums

    def strike_inverse(step, plus, minus):
        tiles = []
        for k0, (ahead, behind) in enumerate(zip(plus, minus)):
            direct = ahead + sign * behind
            crossed = -sign * swap(ahead - sign * behind)
            if k0 == 0:
                direct = jnp.where(lone, jnp.where(real_half, ahead, swap(behind)), direct)
                crossed = jnp.where(lone, -jnp.where(real_half, swap(ahead), behind), crossed)
            tiles.append(jnp.concatenate([direct, crossed], axis=1))
        out = dot3_rows(jnp.concatenate(tiles, axis=0), strike_hi[...], strike_lo[...])
        for s in range(strike_count):
            block = None
            for k0 in range(dip_count):
                shift = rows * (k0 - s) % LANES
                tile = out[k0 * SUBLANES : (k0 + 1) * SUBLANES]
                moved = pltpu.roll(tile, shift, 1) if shift else tile
                block = moved if k0 == 0 else jnp.where(strip == k0, moved, block)
            block = jnp.where(strip < dip_count, block, swap(pltpu.roll(block, wave, 1)))
            send_c[step, s] = block[:half]

    def dip_inverse(step):
        lines = recv_c[step].reshape(front_modes, LANES).T
        out = dot3(lines, dip_hi[:front_modes], dip_lo[:front_modes])
        real = out[:wave, :cols] - out[wave:, cols:]
        imag = out[:wave, cols:] + out[wave:, :cols]
        scale = 1.0 / math.sqrt(cols * dip_count)
        last = lines[wave : wave + rows, 0:1] * jnp.where(column % 2 == 0, scale, -scale)
        terms = [(real[:rows] + last, turned(my_d, 0, 0))]
        for k0 in range(1, dip_count):
            at = slice(k0 * rows, (k0 + 1) * rows)
            terms += [(real[at], turned(my_d, 0, k0)), (imag[at], turned(my_d, 1, k0))]
        return total_of(terms)

    def store_history():
        zero = jnp.zeros((2, modes, total_x), jnp.float32)
        common = stored_count - STEPS + 1

        def term(t, j):
            return kern[j + t + 1].astype(jnp.float32)[None] * hist[j]

        def add(j, sums):
            return tuple(total + term(t, j) for t, total in enumerate(sums))

        sums = lax.fori_loop(0, common, add, (zero,) * STEPS)
        for t in range(STEPS):
            total = sums[t]
            for j in range(common, stored_count - t):
                total = total + term(t, j)
            values = (kern[t].astype(jnp.float32), total[0], total[1])
            for i, value in enumerate(values):
                modal[t, 0, i, 0:modes, :] = value
                nought[t, i] = value[0:1]

    def bound_of(slip):
        weaken = jnp.maximum(0.0, 1.0 - jnp.abs(slip) / crit_slip[...])
        strength = normal_stress[...] * (
            dynamic_friction + (static_friction - dynamic_friction) * weaken
        )
        return jnp.where(flags[...] == 1, strength, HUGE)

    def slide(trial, bound, slip):
        traction = jnp.clip(trial, -bound, bound)
        return traction, slip + time_step * ((trial - traction) / damping)

    barrier = pltpu.get_barrier_semaphore()
    for k in range(1, strike_count):
        pl.semaphore_signal(
            barrier, inc=1, device_id={"strike": ring(my_s, k, strike_count)}, device_id_type=MESH
        )
    for k in range(1, dip_count):
        pl.semaphore_signal(
            barrier, inc=1, device_id={"dip": ring(my_d, k, dip_count)}, device_id_type=MESH
        )
    loads = [
        pltpu.make_async_copy(sources[i], loaded[i], load_sem.at[i]) for i in range(INPUTS)
    ]
    loads[1].start()
    for i in range(INPUTS):
        if i != 1:
            loads[i].start()
    loads[1].wait()
    pack_x(0, stress_in.at[0])
    pack_y(0, lambda z: stress_in[1, z])
    pl.semaphore_wait(barrier, strike_count + dip_count - 2)

    started = []
    halos = start_halos(0)
    started += halos
    for k in range(1, dip_count):
        pl.semaphore_signal(
            plane_sem, inc=1, device_id={"dip": ring(my_d, k, dip_count)}, device_id_type=MESH
        )
    for i in range(INPUTS):
        if i != 1:
            loads[i].wait()
    store_history()
    pl.semaphore_wait(plane_sem, dip_count - 1)
    exchanged = start_exchange(0)
    started += exchanged

    ghost = traction_in[...]
    front = min(3, depth)
    base = prestress[...] + functional_in[...]
    bound = bound_of(slip_in[...])
    wait_halos(halos)
    fill_padded(0, stress_in.at[0])
    for z in range(1, front):
        velocity_layer(0, z, vel_in, stress_in, ghost)
    traction, slip = slide(base + stress_z_layer(0, stress_in), bound, slip_in[...])
    dip_forward(0, slip)
    started += start_a(0)
    for z in (0, *range(front, depth)):
        velocity_layer(0, z, vel_in, stress_in, ghost)
    pack_x(1, vel)
    pack_y(1, lambda z: vel[z])
    halos = start_halos(1)
    started += halos
    late = start_exchange(1)
    started += late
    arrange(0, exchanged)
    wait_a(0)
    spectra = [strike_forward(0)]
    strike_inverse(0, *convolve(0, spectra))
    started += start_c(0)

    wait_halos(halos)
    stress_layers(1, stress_in)
    pack_x(2, stress.at[0])
    pack_y(2, lambda z: stress[1, z])
    halos = start_halos(2)
    started += halos
    arrange(1, late)
    bound = bound_of(slip)
    wait_halos(halos)
    fill_padded(2, stress.at[0])
    for z in range(1, front):
        velocity_layer(2, z, vel, stress, traction)
    base = prestress[...] + stress_z_layer(0, stress)
    ghost = traction
    wait_c(0)
    traction, slip = slide(base + dip_inverse(0), bound, slip)
    dip_forward(1, slip)
    started += start_a(1)
    results[2][...] = slip
    results[3][...] = traction
    for z in (0, *range(front, depth)):
        velocity_layer(2, z, vel, stress, ghost)
    pack_x(3, vel)
    pack_y(3, lambda z: vel[z])
    halos = start_halos(3)
    started += halos
    wait_a(1)
    spectra = [strike_forward(1)] + spectra
    strike_inverse(1, *convolve(1, spectra))
    started += start_c(1)
    wait_halos(halos)
    stress_layers(3, stress)
    for copy in started:
        copy.wait_send()
    wait_c(1)
    results[4][...] = dip_inverse(1)


def copy_kernel(*refs):
    sources, results, sems = refs[:5], refs[5:10], refs[10]
    saves = [pltpu.make_async_copy(sources[i], results[i], sems.at[i]) for i in range(5)]
    for save in saves:
        save.start()
    for save in saves:
        save.wait()


def fits_kernel(strike_count, dip_count, rows, cols, modes, total_x):
    return (
        STEPS == 2
        and strike_count > 1
        and dip_count > 1
        and modes == dip_count * SUBLANES
        and rows % SUBLANES == 0
        and cols == 2 * LANES
        and total_x == LANES
        and 2 * dip_count * rows == LANES
        and strike_count * dip_count * SUBLANES == cols
    )


def body(*args):
    velocity, history = args[0], args[11]
    strike_count = lax.axis_size("strike")
    dip_count = lax.axis_size("dip")
    depth, rows, cols = velocity.shape
    modes, total_x = history.shape[2:]
    if not fits_kernel(strike_count, dip_count, rows, cols, modes, total_x):
        return general_body(*args)
    half = SUBLANES // 2
    blocks = strike_count * dip_count
    total_y = cols * dip_count
    tables = (
        *split_table(dip_table(cols, total_y)),
        *split_table(strike_table(total_x)),
        twiddle_table(dip_count, cols, total_y),
    )
    turns = 2 * STEPS
    f32 = jnp.float32
    dma = pltpu.SemaphoreType.DMA
    operands = (*args, *[jnp.asarray(table) for table in tables])
    shapes = (velocity.shape, args[1].shape) + ((rows, cols),) * 3
    outs = tuple(jax.ShapeDtypeStruct(shape, f32) for shape in shapes)
    held = tuple(pltpu.VMEM(shape, f32) for shape in shapes)
    scratch = [pltpu.VMEM(operand.shape, operand.dtype) for operand in operands] + [
        pltpu.VMEM((depth, rows + 2 * SUBLANES, cols), f32),
        pltpu.VMEM((turns, 2, depth, 2, cols), f32),
        pltpu.VMEM((turns, 2, rows, LANES), f32),
        pltpu.VMEM((turns, 2, depth, 2, cols), f32),
        pltpu.VMEM((turns, 2, rows, LANES), f32),
        pltpu.VMEM((STEPS, blocks, half, LANES), f32),
        pltpu.VMEM((STEPS, dip_count, strike_count, half, LANES), f32),
        pltpu.VMEM((STEPS, strike_count, half, LANES), f32),
        pltpu.VMEM((STEPS, blocks, half, LANES), f32),
        pltpu.VMEM((STEPS, 2, 3, modes + SUBLANES, total_x), f32),
        pltpu.VMEM((STEPS, 3, 1, total_x), f32),
        pltpu.VMEM((STEPS, 3, 1, total_x), f32),
        pltpu.VMEM((STEPS, 2, dip_count, SUBLANES, total_x), f32),
        pltpu.VMEM((STEPS, 2, dip_count, SUBLANES, total_x), f32),
        dma((len(operands),)),
        dma((turns, 4)),
        dma((turns, 4)),
        dma((STEPS, dip_count, strike_count)),
        dma((STEPS, dip_count, strike_count)),
        dma((STEPS, dip_count, strike_count)),
        dma((STEPS, dip_count, strike_count)),
        dma((STEPS, 2)),
        dma((STEPS, 2)),
        pltpu.SemaphoreType.REGULAR,
    ]
    anywhere = pl.BlockSpec(memory_space=pl.ANY)
    results = pl.pallas_call(
        functools.partial(rupture_kernel, strike_count, dip_count),
        out_shape=held,
        in_specs=[pl.BlockSpec(memory_space=pltpu.HBM)] * len(operands),
        out_specs=(pl.BlockSpec(memory_space=pltpu.VMEM),) * len(outs),
        scratch_shapes=scratch,
        compiler_params=pltpu.CompilerParams(
            collective_id=0, has_side_effects=True, vmem_limit_bytes=KERNEL_VMEM
        ),
    )(*operands)
    return pl.pallas_call(
        copy_kernel,
        out_shape=outs,
        in_specs=[pl.BlockSpec(memory_space=pltpu.VMEM)] * len(outs),
        out_specs=(anywhere,) * len(outs),
        scratch_shapes=[dma((len(outs),))],
        compiler_params=pltpu.CompilerParams(vmem_limit_bytes=2**20),
    )(*results)


def solution(mesh):
    return jax.shard_map(
        body,
        mesh=mesh,
        in_specs=(
            P(None, "strike", "dip"),
            P(None, None, "strike", "dip"),
            P(None, "strike", "dip"),
            P(None, "strike", "dip"),
            P("strike", "dip"),
            P("strike", "dip"),
            P("strike", "dip"),
            P("strike", "dip"),
            P("strike", "dip"),
            P("strike", "dip"),
            P("strike", "dip"),
            P(None, None, ("strike", "dip"), None),
            P(None, ("strike", "dip"), None),
        ),
        out_specs=(
            P(None, "strike", "dip"),
            P(None, None, "strike", "dip"),
            P("strike", "dip"),
            P("strike", "dip"),
            P("strike", "dip"),
        ),
        check_vma=False,
    )
```

```python
import functools
import math

import jax
import jax.numpy as jnp
import numpy as np
from jax import lax
from jax.experimental import pallas as pl
from jax.experimental.pallas import tpu as pltpu
from jax.sharding import PartitionSpec as P

STEPS = 2


coef_near = 2.0 / 3.0
coef_far = -1.0 / 12.0
courant = 0.3
static_friction = 0.677
dynamic_friction = 0.525
damping = 0.5
time_step = 0.3


def padded_2(block, sides, width):
    for axis, dim in sides:
        count = lax.axis_size(axis)
        forward = [(i, i + 1) for i in range(count - 1)]
        forward.append((count - 1, 0))
        backward = [(target, source) for source, target in forward]
        low = lax.ppermute(
            lax.slice_in_dim(block, block.shape[dim] - width, None, axis=dim), axis, forward
        )
        high = lax.ppermute(lax.slice_in_dim(block, 0, width, axis=dim), axis, backward)
        block = jnp.concatenate([low, block, high], axis=dim)
    return block


def central(padded, axis, start, count):

    def window(offset):
        return lax.slice_in_dim(padded, start + offset, start + offset + count, axis=axis)

    return coef_near * (window(1) - window(-1)) + coef_far * (window(2) - window(-2))


def normal_diff(field, ghost):
    zeros = jnp.zeros_like(ghost)
    padded = jnp.concatenate([ghost, ghost, field, zeros, zeros], axis=0)
    return central(padded, 0, 2, field.shape[0])


def fault_update(prestress, normal_stress, crit_slip, flags, slip, stress_z, functional):
    trial = prestress + stress_z[0] + functional
    weaken = jnp.maximum(0.0, 1.0 - jnp.abs(slip) / crit_slip)
    strength = normal_stress * (dynamic_friction + (static_friction - dynamic_friction) * weaken)
    clipped = jnp.clip(trial, -strength, strength)
    traction = jnp.where(flags == 1, clipped, trial)
    rate = (trial - traction) / damping
    return (traction, slip + time_step * rate)


def factor_pair(length):
    first = 1
    candidate = 1
    while candidate * candidate <= length:
        if length % candidate == 0:
            first = candidate
        candidate += 1
    return (first, length // first)


def phase_table(count_a, count_b, length, sign):
    product = lax.iota(jnp.int32, count_a)[:, None] * lax.iota(jnp.int32, count_b)[None, :] % length
    angles = sign * 2.0 * math.pi / length * product.astype(jnp.float32)
    return (jnp.cos(angles), jnp.sin(angles))


def contract(form, left, right):
    return jnp.einsum(form, left, right, precision=lax.Precision.HIGHEST)


def transform_last(real_part, imag_part, sign):
    length = real_part.shape[-1]
    outer, inner = factor_pair(length)
    leading = real_part.shape[:-1]
    real_part = real_part.reshape(leading + (outer, inner))
    imag_part = imag_part.reshape(leading + (outer, inner))
    first_cos, first_sin = phase_table(outer, outer, outer, sign)
    middle_real = contract("kt,...tq->...kq", first_cos, real_part) - contract(
        "kt,...tq->...kq", first_sin, imag_part
    )
    middle_imag = contract("kt,...tq->...kq", first_cos, imag_part) + contract(
        "kt,...tq->...kq", first_sin, real_part
    )
    twist_cos, twist_sin = phase_table(outer, inner, length, sign)
    middle_real, middle_imag = (
        middle_real * twist_cos - middle_imag * twist_sin,
        middle_real * twist_sin + middle_imag * twist_cos,
    )
    second_cos, second_sin = phase_table(inner, inner, inner, sign)
    out_real = contract("...kt,tm->...km", middle_real, second_cos) - contract(
        "...kt,tm->...km", middle_imag, second_sin
    )
    out_imag = contract("...kt,tm->...km", middle_real, second_sin) + contract(
        "...kt,tm->...km", middle_imag, second_cos
    )
    scale = 1.0 / math.sqrt(length)
    out_real = jnp.swapaxes(out_real, -1, -2).reshape(leading + (length,)) * scale
    out_imag = jnp.swapaxes(out_imag, -1, -2).reshape(leading + (length,)) * scale
    return (out_real, out_imag)


def general_body(
    velocity,
    stress,
    shear_modulus,
    buoyancy,
    prestress,
    normal_stress,
    crit_slip,
    slip,
    traction,
    functional,
    flags,
    history,
    kernel,
):
    strike_count = lax.axis_size("strike")
    dip_count = lax.axis_size("dip")
    depth, rows_x, cols_y = velocity.shape
    ky_local = history.shape[2]
    total_x = history.shape[3]
    total_y = cols_y * dip_count
    line_rows = rows_x // dip_count
    stress_x, stress_y, stress_z = (stress[0], stress[1], stress[2])
    ghost_zero = jnp.zeros((1, rows_x, cols_y), jnp.float32)
    spectra = []
    for iteration in range(STEPS):
        padded_x = padded_2(stress_x, (("strike", 1),), 2)
        padded_y = padded_2(stress_y, (("dip", 2),), 2)
        divergence = (
            central(padded_x, 1, 2, rows_x)
            + central(padded_y, 2, 2, cols_y)
            + normal_diff(stress_z, traction[None])
        )
        velocity = velocity + courant * buoyancy * divergence
        padded_v = padded_2(velocity, (("strike", 1), ("dip", 2)), 2)
        grad_x = central(padded_v[:, :, 2 : cols_y + 2], 1, 2, rows_x)
        grad_y = central(padded_v[:, 2 : rows_x + 2, :], 2, 2, cols_y)
        stress_x = stress_x + courant * shear_modulus * grad_x
        stress_y = stress_y + courant * shear_modulus * grad_y
        stress_z = stress_z + courant * shear_modulus * normal_diff(velocity, ghost_zero)
        traction, slip = fault_update(
            prestress, normal_stress, crit_slip, flags, slip, stress_z, functional
        )
        lines = lax.all_to_all(slip, "dip", split_axis=0, concat_axis=1, tiled=True)
        part_real, part_imag = transform_last(lines, jnp.zeros_like(lines), -1.0)
        stacked = jnp.stack([part_real, part_imag]).reshape(
            2, line_rows, strike_count, dip_count, ky_local
        )
        stacked = stacked.transpose(0, 2, 3, 4, 1).reshape(
            2, strike_count, dip_count, ky_local, 1, 1, line_rows
        )
        halfway = lax.all_to_all(stacked, "strike", split_axis=1, concat_axis=4, tiled=True)
        owned = lax.all_to_all(halfway, "dip", split_axis=2, concat_axis=5, tiled=True)
        owned = owned.reshape(2, ky_local, total_x)
        spec_real, spec_imag = transform_last(owned[0], owned[1], -1.0)
        spectra = [(spec_real, spec_imag)] + spectra
        weights = kernel[iteration + 1 :].astype(jnp.float32)
        stored = jnp.sum(weights[:, None] * history[: history.shape[0] - iteration], axis=0)
        sum_real = stored[0]
        sum_imag = stored[1]
        for offset, item in enumerate(spectra):
            weight = kernel[offset].astype(jnp.float32)
            sum_real = sum_real + weight * item[0]
            sum_imag = sum_imag + weight * item[1]
        back_real, back_imag = transform_last(sum_real, sum_imag, 1.0)
        leaving = jnp.stack([back_real, back_imag]).reshape(
            2, 1, 1, ky_local, strike_count, dip_count, line_rows
        )
        partway = lax.all_to_all(leaving, "strike", split_axis=4, concat_axis=1, tiled=True)
        returned = lax.all_to_all(partway, "dip", split_axis=5, concat_axis=2, tiled=True)
        returned = returned.reshape(2, total_y, line_rows).transpose(0, 2, 1)
        field_real, field_imag = transform_last(returned[0], returned[1], 1.0)
        functional = lax.all_to_all(field_real, "dip", split_axis=1, concat_axis=0, tiled=True)
    return (velocity, jnp.stack([stress_x, stress_y, stress_z]), slip, traction, functional)


LANES = 128
SUBLANES = 8
MESH = pl.DeviceIdType.MESH
INPUTS = 18
KERNEL_VMEM = 67043328 - 1000000
HUGE = float(np.finfo(np.float32).max)


def split_bf16(value):
    high = value.astype(jnp.bfloat16)
    return high, (value - high.astype(jnp.float32)).astype(jnp.bfloat16)


def split_table(table):
    table = np.asarray(table, np.float32)
    high = table.astype(jnp.bfloat16)
    return high, (table - high.astype(np.float32)).astype(jnp.bfloat16)


def strike_table(total_x):
    index = np.arange(total_x)
    angle = 2.0 * np.pi / total_x * (index[:, None] * index[None, :] % total_x)
    return np.concatenate([np.cos(angle), np.sin(angle)], axis=1) / np.sqrt(total_x)


def dip_table(cols, total_y):
    count = cols // 2 + 2 * SUBLANES
    angle = 2.0 * np.pi / cols * (np.arange(count)[:, None] * np.arange(cols)[None, :] % cols)
    return np.concatenate([np.cos(angle), np.sin(angle)], axis=1) / np.sqrt(total_y)


def twiddle_table(dip_count, cols, total_y):
    place = np.arange(total_y).reshape(dip_count, 1, cols)
    freq = np.arange(dip_count)[None, :, None]
    angle = 2.0 * np.pi / total_y * (freq * place % total_y)
    return np.stack([np.cos(angle), -np.sin(angle)], axis=1).astype(np.float32)


def dot3(left, right_high, right_low):
    high, low = split_bf16(left)
    rows = left.shape[0]
    both = jnp.dot(
        jnp.concatenate([high, low], axis=0), right_high, preferred_element_type=jnp.float32
    )
    return both[:rows] + both[rows:] + jnp.dot(high, right_low, preferred_element_type=jnp.float32)


def dot3_nt(left_high, left_low, right):
    high, low = split_bf16(right)

    def product(a, b):
        return lax.dot_general(a, b, (((1,), (1,)), ((), ())), preferred_element_type=jnp.float32)

    return product(left_high, high) + product(left_high, low) + product(left_low, high)


def dot3_rows(left, right_high, right_low):
    high, low = split_bf16(left)
    rows = left.shape[0]

    def product(a, b):
        return lax.dot_general(a, b, (((1,), (1,)), ((), ())), preferred_element_type=jnp.float32)

    both = product(jnp.concatenate([high, low], axis=0), right_high)
    return both[:rows] + both[rows:] + product(high, right_low)


def rupture_kernel(strike_count, dip_count, *refs):
    sources, refs = refs[:INPUTS], refs[INPUTS:]
    results, refs = refs[:5], refs[5:]
    loaded, refs = refs[:INPUTS], refs[INPUTS:]
    (
        vel_in, stress_in, shear, buoy, prestress, normal_stress, crit_slip, slip_in, traction_in,
        functional_in, flags, hist, kern, dip_hi, dip_lo, strike_hi, strike_lo, twiddle,
    ) = loaded
    (
        padded, edge_x, edge_y, halo_x, halo_y, near_x, near_y,
        shared, gathered, send_f, recv_a, recv_b, lines_out,
        send_c, recv_c, modal, nought, nought_in, weight, source,
        load_sem, edge_sem, halo_sem, n_send, n_recv, g_send, g_recv,
        a_send, a_recv, b_send, b_recv, c_send, c_recv, x_send, x_recv, plane_sem,
    ) = refs
    vel, stress = results[:2]
    depth, rows, cols = vel_in.shape
    modes = hist.shape[2]
    total_x = hist.shape[3]
    stored_count = hist.shape[0]
    blocks = strike_count * dip_count
    half = modes // dip_count // 2
    wave = dip_count * rows
    front_modes = cols // 2
    my_s = lax.axis_index("strike")
    my_d = lax.axis_index("dip")
    my_block = my_s * dip_count + my_d
    upper = my_block // (blocks // 2)

    def ring(me, offset, count):
        return lax.rem(me + offset + count, count)

    def remote(src, dst, send_sem, recv_sem, target):
        return pltpu.make_async_remote_copy(
            src_ref=src,
            dst_ref=dst,
            send_sem=send_sem,
            recv_sem=recv_sem,
            device_id=target,
            device_id_type=MESH,
        )

    lane = lax.broadcasted_iota(jnp.int32, (rows, LANES), 1)
    column = lax.broadcasted_iota(jnp.int32, (rows, cols), 1)
    strip = lax.broadcasted_iota(jnp.int32, (SUBLANES, LANES), 1) // rows
    layer_row = lax.broadcasted_iota(jnp.int32, (SUBLANES, LANES), 0)
    real_half = layer_row < half
    sign = jnp.where(real_half, 1.0, -1.0)
    lone = jnp.logical_and(layer_row % half == 0, my_block == 0)
    swap = functools.partial(pltpu.roll, shift=half, axis=0)

    def slot(block):
        high = block // (blocks // 2)
        return 2 * block + high * (2 * blocks - 1 - 4 * block)

    def pack_x(turn, field):
        edge_x[turn, 0] = field[:, rows - 2 : rows, :]
        edge_x[turn, 1] = field[:, 0:2, :]

    def pack_y(turn, layer):
        low = jnp.zeros((rows, LANES), jnp.float32)
        high = jnp.zeros((rows, LANES), jnp.float32)
        for z in range(depth):
            here = lane // 2 == z
            last = layer(z)[:, cols - LANES :]
            first = layer(z)[:, :LANES]
            low = jnp.where(here, pltpu.roll(last, (2 * z + 2) % LANES, 1), low)
            high = jnp.where(here, pltpu.roll(first, 2 * z, 1) if z else first, high)
        edge_y[turn, 0] = low
        edge_y[turn, 1] = high

    def halo_copies(turn):
        copies = []
        for side, step in ((0, 1), (1, -1)):
            copies.append(
                remote(
                    edge_x.at[turn, side],
                    halo_x.at[turn, side],
                    edge_sem.at[turn, side],
                    halo_sem.at[turn, side],
                    {"strike": ring(my_s, step, strike_count)},
                )
            )
            copies.append(
                remote(
                    edge_y.at[turn, side],
                    halo_y.at[turn, side],
                    edge_sem.at[turn, side + 2],
                    halo_sem.at[turn, side + 2],
                    {"dip": ring(my_d, step, dip_count)},
                )
            )
        return copies

    def start_halos(turn):
        copies = halo_copies(turn)
        for copy in copies:
            copy.start()
        return copies

    def wait_halos(copies):
        for copy in copies:
            copy.wait_recv()

    def fill_padded(turn, field):
        padded[:, SUBLANES : SUBLANES + rows, :] = field[...]
        padded[:, SUBLANES - 2 : SUBLANES, :] = halo_x[turn, 0]
        padded[:, SUBLANES + rows : SUBLANES + rows + 2, :] = halo_x[turn, 1]

    def diff_x(z):
        def window(offset):
            return padded[z, SUBLANES + offset : SUBLANES + offset + rows, :]

        return coef_near * (window(1) - window(-1)) + coef_far * (window(2) - window(-2))

    def diff_y(turn, z, field):
        low = halo_y[turn, 0]
        high = halo_y[turn, 1]
        low_0, low_1 = low[:, 2 * z : 2 * z + 1], low[:, 2 * z + 1 : 2 * z + 2]
        high_0, high_1 = high[:, 2 * z : 2 * z + 1], high[:, 2 * z + 1 : 2 * z + 2]
        back_1 = jnp.where(column == 0, low_1, pltpu.roll(field, 1, 1))
        back_2 = jnp.where(
            column == 0, low_0, jnp.where(column == 1, low_1, pltpu.roll(field, 2, 1))
        )
        next_1 = jnp.where(column == cols - 1, high_0, pltpu.roll(field, cols - 1, 1))
        next_2 = jnp.where(
            column == cols - 2,
            high_0,
            jnp.where(column == cols - 1, high_1, pltpu.roll(field, cols - 2, 1)),
        )
        return coef_near * (next_1 - back_1) + coef_far * (next_2 - back_2)

    def diff_z(z, layer, ghost):
        def at(index):
            if index < 0:
                return ghost
            return layer(index) if index < depth else None

        total = None
        for offset, coef in ((1, coef_near), (-1, -coef_near), (2, coef_far), (-2, -coef_far)):
            value = at(z + offset)
            if value is not None:
                total = coef * value if total is None else total + coef * value
        return total

    def velocity_layer(turn, z, source, stress_ref, traction):
        divergence = (
            diff_x(z)
            + diff_y(turn, z, stress_ref[1, z])
            + diff_z(z, lambda i: stress_ref[2, i], traction)
        )
        vel[z] = source[z] + courant * buoy[z] * divergence

    def stress_z_layer(z, stress_ref):
        return stress_ref[2, z] + courant * shear[z] * diff_z(z, lambda i: vel[i], None)

    def stress_layers(turn, stress_ref):
        fill_padded(turn, vel)
        for z in range(depth):
            modulus = courant * shear[z]
            stress[0, z] = stress_ref[0, z] + modulus * diff_x(z)
            stress[1, z] = stress_ref[1, z] + modulus * diff_y(turn, z, vel[z])
            stress[2, z] = stress_z_layer(z, stress_ref)

    def start_near(kind, field):
        copies = []
        for side, step in ((0, 1), (1, -1)):
            row = 0 if side else rows - SUBLANES
            col = 0 if side else cols - LANES
            copies.append(
                remote(
                    field.at[pl.ds(1, 2), pl.ds(row, SUBLANES), :],
                    near_x.at[kind, side],
                    n_send.at[kind, side],
                    n_recv.at[kind, side],
                    {"strike": ring(my_s, step, strike_count)},
                )
            )
            copies.append(
                remote(
                    field.at[pl.ds(1, 2), :, pl.ds(col, LANES)],
                    near_y.at[kind, side],
                    n_send.at[kind, side + 2],
                    n_recv.at[kind, side + 2],
                    {"dip": ring(my_d, step, dip_count)},
                )
            )
        for copy in copies:
            copy.start()
        return copies

    def slope(field, axis):
        size = field.shape[axis]

        def at(offset):
            return pltpu.roll(field, -offset % size, axis)

        return coef_near * (at(1) - at(-1)) + coef_far * (at(2) - at(-2))

    def early_trial(traction):
        normal = [
            stress_in[2, z] + courant * shear[z] * diff_z(z, lambda i: vel[i], None)
            for z in range(min(5, depth))
        ]
        ahead = [None]
        zero = jnp.zeros((SUBLANES - 2, cols), jnp.float32)

        def widened(kind, field, z, axis):
            near = (near_x, near_y)[axis]
            return jnp.concatenate([near[kind, 0, z - 1], field[z], near[kind, 1, z - 1]], axis=axis)

        for z in (1, 2):
            face = jnp.concatenate(
                [zero, halo_x[0, 0, z], stress_in[0, z], halo_x[0, 1, z], zero], axis=0
            )
            face = face + courant * widened(0, shear, z, 0) * slope(widened(1, vel, z, 0), 0)
            total = slope(face, 0)[SUBLANES : SUBLANES + rows]
            face = jnp.concatenate(
                [
                    pltpu.roll(halo_y[0, 0], LANES - 2 - 2 * z, 1),
                    stress_in[1, z],
                    pltpu.roll(halo_y[0, 1], LANES - 2 * z, 1),
                ],
                axis=1,
            )
            face = face + courant * widened(0, shear, z, 1) * slope(widened(1, vel, z, 1), 1)
            total = total + slope(face, 1)[:, LANES : LANES + cols]
            total = total + diff_z(z, lambda i: normal[i], traction)
            ahead.append(vel[z] + courant * buoy[z] * total)
        return prestress[...] + (
            normal[0] + courant * shear[0] * diff_z(0, lambda i: ahead[i], None)
        )

    def start_gather(turn, value):
        shared[turn] = value
        gathered[turn, my_d] = value
        copies = []
        for k in range(1, dip_count):
            copy = remote(
                shared.at[turn],
                gathered.at[turn, my_d],
                g_send.at[turn, k],
                g_recv.at[turn, k],
                {"dip": ring(my_d, k, dip_count)},
            )
            copy.start()
            copies.append(copy)
        return copies

    def wait_gather(turn):
        for k in range(1, dip_count):
            source = ring(my_d, -k, dip_count)
            remote(
                shared.at[turn],
                gathered.at[turn, source],
                g_send.at[turn, k],
                g_recv.at[turn, k],
                {"dip": source},
            ).wait_recv()

    def start_b():
        recv_b[my_s] = send_f[1, slot(my_block)]
        copies = []
        for k in range(1, strike_count):
            target = ring(my_s, k, strike_count)
            copy = remote(
                send_f.at[1, slot(target * dip_count + my_d)],
                recv_b.at[my_s],
                b_send.at[k],
                b_recv.at[k],
                {"strike": target},
            )
            copy.start()
            copies.append(copy)
        return copies

    def wait_b():
        for k in range(1, strike_count):
            source_s = ring(my_s, -k, strike_count)
            remote(
                send_f.at[1, source_s],
                recv_b.at[source_s],
                b_send.at[k],
                b_recv.at[k],
                {"strike": source_s},
            ).wait_recv()

    offsets = [
        (i, k) for k in reversed(range(dip_count)) for i in reversed(range(strike_count)) if i or k
    ]

    def start_a():
        recv_a[my_d, my_s] = send_f[0, slot(my_block)]
        copies = []
        for i, k in offsets:
            target_s, target_d = ring(my_s, i, strike_count), ring(my_d, k, dip_count)
            copy = remote(
                send_f.at[0, slot(target_s * dip_count + target_d)],
                recv_a.at[my_d, my_s],
                a_send.at[k, i],
                a_recv.at[k, i],
                {"strike": target_s, "dip": target_d},
            )
            copy.start()
            copies.append(copy)
        return copies

    def wait_a():
        for i, k in reversed(offsets):
            source_s, source_d = ring(my_s, -i, strike_count), ring(my_d, -k, dip_count)
            remote(
                send_f.at[0, source_s],
                recv_a.at[source_d, source_s],
                a_send.at[k, i],
                a_recv.at[k, i],
                {"strike": source_s, "dip": source_d},
            ).wait_recv()

    def exchange_copies(turn):
        other = blocks - 1 - my_block
        single = 1 - jnp.minimum(lax.rem(my_block, blocks // 2), 1)
        mirror = lax.rem(blocks - my_block + single * (blocks // 2), blocks)
        upper_rows = pl.ds(modes // 2, modes // 2)
        return [
            remote(
                modal.at[turn, 0, :, upper_rows, :],
                modal.at[turn, 1, :, upper_rows, :],
                x_send.at[turn, 0],
                x_recv.at[turn, 0],
                {"strike": other // dip_count, "dip": lax.rem(other, dip_count)},
            ),
            remote(
                nought.at[turn],
                nought_in.at[turn],
                x_send.at[turn, 1],
                x_recv.at[turn, 1],
                {"strike": mirror // dip_count, "dip": lax.rem(mirror, dip_count)},
            ),
        ]

    def start_exchange(turn):
        copies = exchange_copies(turn)
        for copy in copies:
            copy.start()
        return copies

    def arrange(turn, copies):
        for copy in copies:
            copy.wait_recv()
        modal[turn, 1, :, modes : modes + 1, :] = nought_in[turn]
        for k0 in range(dip_count):
            for m in range(half):
                at = dip_count * m + k0
                plus = modal[turn, upper, :, pl.ds(modes // 2 * upper + at, 1), :]
                minus = modal[turn, 1 - upper, :, pl.ds(modes - modes // 2 * upper - at, 1), :]
                for side, value in enumerate((plus, minus)):
                    weight[turn, side, k0, m : m + 1, :] = value[0]
                    weight[turn, side, k0, half + m : half + m + 1, :] = value[0]
                    source[turn, side, k0, m : m + 1, :] = value[1]
                    source[turn, side, k0, half + m : half + m + 1, :] = value[2]

    def start_c(step):
        recv_c[step, slot(my_block)] = send_c[step, my_s]
        copies = []
        for i, k in offsets:
            target_s, target_d = ring(my_s, i, strike_count), ring(my_d, k, dip_count)
            copy = remote(
                send_c.at[step, target_s],
                recv_c.at[step, slot(my_block)],
                c_send.at[step, k, i],
                c_recv.at[step, k, i],
                {"strike": target_s, "dip": target_d},
            )
            copy.start()
            copies.append(copy)
        return copies

    def wait_c(step):
        for i, k in reversed(offsets):
            source_s, source_d = ring(my_s, -i, strike_count), ring(my_d, -k, dip_count)
            remote(
                send_c.at[step, source_s],
                recv_c.at[step, slot(source_s * dip_count + source_d)],
                c_send.at[step, k, i],
                c_recv.at[step, k, i],
                {"strike": source_s, "dip": source_d},
            ).wait_recv()

    def total_of(terms):
        total = None
        for left, right in terms:
            total = left * right if total is None else total + left * right
        return total

    def turned(i, part, k0):
        return twiddle[i, part, k0 : k0 + 1, :]

    def dip_forward(step, parts):
        real, imag = (
            jnp.concatenate(
                [
                    total_of([(part, turned(i, kind, k0)) for i, part in parts])
                    for k0 in range(dip_count)
                ],
                axis=0,
            )
            for kind in range(2)
        )
        both = jnp.concatenate(
            [
                jnp.concatenate([real, imag], axis=1),
                jnp.concatenate([imag, -real], axis=1),
            ],
            axis=0,
        )
        out = dot3_nt(dip_hi[...], dip_lo[...], both)
        last = pltpu.roll(out[front_modes : front_modes + SUBLANES], wave, 1)
        first = jnp.where(
            jnp.logical_and(layer_row == 0, strip == dip_count), last, out[:SUBLANES]
        )
        out = jnp.concatenate([first, out[SUBLANES:front_modes]], axis=0)
        send_f[step] = out.reshape(blocks, half, LANES)

    def strike_forward(pieces):
        stacks = [None] * dip_count
        for s, piece in enumerate(pieces):
            pair = jnp.concatenate([piece, pltpu.roll(piece, wave, 1)], axis=0)
            for k0 in range(dip_count):
                shift = rows * (s - k0) % LANES
                moved = pltpu.roll(pair, shift, 1) if shift else pair
                stacks[k0] = moved if s == 0 else jnp.where(strip == s, moved, stacks[k0])
        both = dot3(jnp.concatenate(stacks, axis=0), strike_hi[...], strike_lo[...])
        plus, minus = [], []
        for k0 in range(dip_count):
            tile = both[k0 * SUBLANES : (k0 + 1) * SUBLANES]
            cos, sin = tile[:, :total_x], tile[:, total_x:]
            crossed = swap(sin)
            ahead = cos + sign * crossed
            behind = sign * cos - crossed
            if k0 == 0:
                ahead = jnp.where(lone, jnp.where(real_half, cos, -crossed), ahead)
                behind = jnp.where(lone, jnp.where(real_half, swap(cos), -sin), behind)
            plus.append(ahead)
            minus.append(behind)
        return plus, minus

    def convolve(step, spectra):
        sums = []
        for side in range(2):
            tiles = []
            for k0 in range(dip_count):
                total = source[step, side, k0]
                for offset, item in enumerate(spectra):
                    total = total + weight[offset, side, k0] * item[side][k0]
                tiles.append(total)
            sums.append(tiles)
        return sums

    def strike_inverse(step, plus, minus):
        tiles = []
        for k0, (ahead, behind) in enumerate(zip(plus, minus)):
            direct = ahead + sign * behind
            crossed = -sign * swap(ahead - sign * behind)
            if k0 == 0:
                direct = jnp.where(lone, jnp.where(real_half, ahead, swap(behind)), direct)
                crossed = jnp.where(lone, -jnp.where(real_half, swap(ahead), behind), crossed)
            tiles.append(jnp.concatenate([direct, crossed], axis=1))
        out = dot3_rows(jnp.concatenate(tiles, axis=0), strike_hi[...], strike_lo[...])
        for s in range(strike_count):
            block = None
            for k0 in range(dip_count):
                shift = rows * (k0 - s) % LANES
                tile = out[k0 * SUBLANES : (k0 + 1) * SUBLANES]
                moved = pltpu.roll(tile, shift, 1) if shift else tile
                block = moved if k0 == 0 else jnp.where(strip == k0, moved, block)
            block = jnp.where(strip < dip_count, block, swap(pltpu.roll(block, wave, 1)))
            send_c[step, s] = block[:half]

    def dip_inverse(step, places):
        lines = recv_c[step].reshape(front_modes, LANES).T
        out = dot3(lines, dip_hi[:front_modes], dip_lo[:front_modes])
        real = out[:wave, :cols] - out[wave:, cols:]
        imag = out[:wave, cols:] + out[wave:, :cols]
        scale = 1.0 / math.sqrt(cols * dip_count)
        last = lines[wave : wave + rows, 0:1] * jnp.where(column % 2 == 0, scale, -scale)
        result = []
        for i in places:
            terms = [(real[:rows] + last, turned(i, 0, 0))]
            for k0 in range(1, dip_count):
                at = slice(k0 * rows, (k0 + 1) * rows)
                terms += [(real[at], turned(i, 0, k0)), (imag[at], turned(i, 1, k0))]
            result.append(total_of(terms))
        return result

    def store_history():
        zero = jnp.zeros((2, modes, total_x), jnp.float32)
        common = stored_count - STEPS + 1

        def term(t, j):
            return kern[j + t + 1].astype(jnp.float32)[None] * hist[j]

        def add(j, sums):
            return tuple(total + term(t, j) for t, total in enumerate(sums))

        sums = lax.fori_loop(0, common, add, (zero,) * STEPS)
        for t in range(STEPS):
            total = sums[t]
            for j in range(common, stored_count - t):
                total = total + term(t, j)
            values = (kern[t].astype(jnp.float32), total[0], total[1])
            for i, value in enumerate(values):
                modal[t, 0, i, 0:modes, :] = value
                nought[t, i] = value[0:1]

    def bound_of(slip):
        weaken = jnp.maximum(0.0, 1.0 - jnp.abs(slip) / crit_slip[...])
        strength = normal_stress[...] * (
            dynamic_friction + (static_friction - dynamic_friction) * weaken
        )
        return jnp.where(flags[...] == 1, strength, HUGE)

    def slide(trial, bound, slip):
        traction = jnp.clip(trial, -bound, bound)
        return traction, slip + time_step * ((trial - traction) / damping)

    barrier = pltpu.get_barrier_semaphore()
    for k in range(1, strike_count):
        pl.semaphore_signal(
            barrier, inc=1, device_id={"strike": ring(my_s, k, strike_count)}, device_id_type=MESH
        )
    for k in range(1, dip_count):
        pl.semaphore_signal(
            barrier, inc=1, device_id={"dip": ring(my_d, k, dip_count)}, device_id_type=MESH
        )
    loads = [
        pltpu.make_async_copy(sources[i], loaded[i], load_sem.at[i]) for i in range(INPUTS)
    ]
    loads[1].start()
    for i in range(INPUTS):
        if i != 1:
            loads[i].start()
    loads[1].wait()
    pack_x(0, stress_in.at[0])
    pack_y(0, lambda z: stress_in[1, z])
    pl.semaphore_wait(barrier, strike_count + dip_count - 2)

    started = []
    halos = start_halos(0)
    started += halos
    for k in range(1, dip_count):
        pl.semaphore_signal(
            plane_sem, inc=1, device_id={"dip": ring(my_d, k, dip_count)}, device_id_type=MESH
        )
    for i in range(INPUTS):
        if i != 1:
            loads[i].wait()
    near = start_near(0, shear)
    started += near
    store_history()
    pl.semaphore_wait(plane_sem, dip_count - 1)
    exchanged = start_exchange(0)
    started += exchanged

    ghost = traction_in[...]
    front = min(3, depth)
    base = prestress[...] + functional_in[...]
    bound = bound_of(slip_in[...])
    wait_halos(halos)
    fill_padded(0, stress_in.at[0])
    for z in range(1, front):
        velocity_layer(0, z, vel_in, stress_in, ghost)
    traction, slip = slide(base + stress_z_layer(0, stress_in), bound, slip_in[...])
    dip_forward(0, [(my_d, slip)])
    started += start_a()
    wide = start_near(1, vel)
    started += start_gather(0, bound_of(slip))
    for z in (0, *range(front, depth)):
        velocity_layer(0, z, vel_in, stress_in, ghost)
    pack_x(1, vel)
    pack_y(1, lambda z: vel[z])
    halos = start_halos(1)
    started += halos
    late = start_exchange(1)
    started += late
    wait_halos(near + wide)
    started += start_gather(1, early_trial(traction))
    arrange(0, exchanged)
    wait_a()
    pieces = []
    for s in range(strike_count):
        piece = recv_a[0, s]
        for i in range(1, dip_count):
            piece = piece + recv_a[i, s]
        pieces.append(piece)
    spectra = [strike_forward(pieces)]
    strike_inverse(0, *convolve(0, spectra))
    started += start_c(0)

    wait_halos(halos)
    stress_layers(1, stress_in)
    pack_x(2, stress.at[0])
    pack_y(2, lambda z: stress[1, z])
    halos = start_halos(2)
    started += halos
    arrange(1, late)
    for turn in range(2):
        wait_gather(turn)
    wait_c(0)
    changes = []
    for i, value in enumerate(dip_inverse(0, range(dip_count))):
        trial = gathered[1, i] + value
        bound = gathered[0, i]
        clipped = jnp.clip(trial, -bound, bound)
        change = time_step * ((trial - clipped) / damping)
        lines_out[0, i] = change
        lines_out[1, i] = clipped
        changes.append((i, change))
    dip_forward(1, changes)
    started += start_b()
    results[2][...] = slip + lines_out[0, my_d]
    results[3][...] = lines_out[1, my_d]
    wait_halos(halos)
    fill_padded(2, stress.at[0])
    for copy in wide:
        copy.wait_send()
    for z in range(depth):
        velocity_layer(2, z, vel, stress, traction)
    pack_x(3, vel)
    pack_y(3, lambda z: vel[z])
    halos = start_halos(3)
    started += halos
    wait_b()
    change = strike_forward([recv_b[s] for s in range(strike_count)])
    latest = [[old + new for old, new in zip(*pair)] for pair in zip(spectra[0], change)]
    spectra = [latest] + spectra
    strike_inverse(1, *convolve(1, spectra))
    started += start_c(1)
    wait_halos(halos)
    stress_layers(3, stress)
    for copy in started:
        copy.wait_send()
    wait_c(1)
    results[4][...] = dip_inverse(1, [my_d])[0]


def copy_kernel(*refs):
    sources, results, sems = refs[:5], refs[5:10], refs[10]
    saves = [pltpu.make_async_copy(sources[i], results[i], sems.at[i]) for i in range(5)]
    for save in saves:
        save.start()
    for save in saves:
        save.wait()


def fits_kernel(strike_count, dip_count, depth, rows, cols, modes, total_x):
    return (
        STEPS == 2
        and depth > 2
        and strike_count > 1
        and dip_count > 1
        and modes == dip_count * SUBLANES
        and rows % SUBLANES == 0
        and cols == 2 * LANES
        and total_x == LANES
        and 2 * dip_count * rows == LANES
        and strike_count * dip_count * SUBLANES == cols
    )


def body(*args):
    velocity, history = args[0], args[11]
    strike_count = lax.axis_size("strike")
    dip_count = lax.axis_size("dip")
    depth, rows, cols = velocity.shape
    modes, total_x = history.shape[2:]
    if not fits_kernel(strike_count, dip_count, depth, rows, cols, modes, total_x):
        return general_body(*args)
    half = SUBLANES // 2
    blocks = strike_count * dip_count
    total_y = cols * dip_count
    tables = (
        *split_table(dip_table(cols, total_y)),
        *split_table(strike_table(total_x)),
        twiddle_table(dip_count, cols, total_y),
    )
    turns = 2 * STEPS
    f32 = jnp.float32
    dma = pltpu.SemaphoreType.DMA
    operands = (*args, *[jnp.asarray(table) for table in tables])
    shapes = (velocity.shape, args[1].shape) + ((rows, cols),) * 3
    outs = tuple(jax.ShapeDtypeStruct(shape, f32) for shape in shapes)
    held = tuple(pltpu.VMEM(shape, f32) for shape in shapes)
    scratch = [pltpu.VMEM(operand.shape, operand.dtype) for operand in operands] + [
        pltpu.VMEM((depth, rows + 2 * SUBLANES, cols), f32),
        pltpu.VMEM((turns, 2, depth, 2, cols), f32),
        pltpu.VMEM((turns, 2, rows, LANES), f32),
        pltpu.VMEM((turns, 2, depth, 2, cols), f32),
        pltpu.VMEM((turns, 2, rows, LANES), f32),
        pltpu.VMEM((2, 2, 2, SUBLANES, cols), f32),
        pltpu.VMEM((2, 2, 2, rows, LANES), f32),
        pltpu.VMEM((2, rows, cols), f32),
        pltpu.VMEM((2, dip_count, rows, cols), f32),
        pltpu.VMEM((STEPS, blocks, half, LANES), f32),
        pltpu.VMEM((dip_count, strike_count, half, LANES), f32),
        pltpu.VMEM((strike_count, half, LANES), f32),
        pltpu.VMEM((2, dip_count, rows, cols), f32),
        pltpu.VMEM((STEPS, strike_count, half, LANES), f32),
        pltpu.VMEM((STEPS, blocks, half, LANES), f32),
        pltpu.VMEM((STEPS, 2, 3, modes + SUBLANES, total_x), f32),
        pltpu.VMEM((STEPS, 3, 1, total_x), f32),
        pltpu.VMEM((STEPS, 3, 1, total_x), f32),
        pltpu.VMEM((STEPS, 2, dip_count, SUBLANES, total_x), f32),
        pltpu.VMEM((STEPS, 2, dip_count, SUBLANES, total_x), f32),
        dma((len(operands),)),
        dma((turns, 4)),
        dma((turns, 4)),
        dma((2, 4)),
        dma((2, 4)),
        dma((2, dip_count)),
        dma((2, dip_count)),
        dma((dip_count, strike_count)),
        dma((dip_count, strike_count)),
        dma((strike_count,)),
        dma((strike_count,)),
        dma((STEPS, dip_count, strike_count)),
        dma((STEPS, dip_count, strike_count)),
        dma((STEPS, 2)),
        dma((STEPS, 2)),
        pltpu.SemaphoreType.REGULAR,
    ]
    anywhere = pl.BlockSpec(memory_space=pl.ANY)
    results = pl.pallas_call(
        functools.partial(rupture_kernel, strike_count, dip_count),
        out_shape=held,
        in_specs=[pl.BlockSpec(memory_space=pltpu.HBM)] * len(operands),
        out_specs=(pl.BlockSpec(memory_space=pltpu.VMEM),) * len(outs),
        scratch_shapes=scratch,
        compiler_params=pltpu.CompilerParams(
            collective_id=0, has_side_effects=True, vmem_limit_bytes=KERNEL_VMEM
        ),
    )(*operands)
    return pl.pallas_call(
        copy_kernel,
        out_shape=outs,
        in_specs=[pl.BlockSpec(memory_space=pltpu.VMEM)] * len(outs),
        out_specs=(anywhere,) * len(outs),
        scratch_shapes=[dma((len(outs),))],
        compiler_params=pltpu.CompilerParams(vmem_limit_bytes=2**20),
    )(*results)


def solution(mesh):
    return jax.shard_map(
        body,
        mesh=mesh,
        in_specs=(
            P(None, "strike", "dip"),
            P(None, None, "strike", "dip"),
            P(None, "strike", "dip"),
            P(None, "strike", "dip"),
            P("strike", "dip"),
            P("strike", "dip"),
            P("strike", "dip"),
            P("strike", "dip"),
            P("strike", "dip"),
            P("strike", "dip"),
            P("strike", "dip"),
            P(None, None, ("strike", "dip"), None),
            P(None, ("strike", "dip"), None),
        ),
        out_specs=(
            P(None, "strike", "dip"),
            P(None, None, "strike", "dip"),
            P("strike", "dip"),
            P("strike", "dip"),
            P("strike", "dip"),
        ),
        check_vma=False,
    )
```

```python
import functools
import math

import jax
import jax.numpy as jnp
import numpy as np
from jax import lax
from jax.experimental import pallas as pl
from jax.experimental.pallas import tpu as pltpu
from jax.sharding import PartitionSpec as P

STEPS = 2


coef_near = 2.0 / 3.0
coef_far = -1.0 / 12.0
courant = 0.3
static_friction = 0.677
dynamic_friction = 0.525
damping = 0.5
time_step = 0.3


def padded_2(block, sides, width):
    for axis, dim in sides:
        count = lax.axis_size(axis)
        forward = [(i, i + 1) for i in range(count - 1)]
        forward.append((count - 1, 0))
        backward = [(target, source) for source, target in forward]
        low = lax.ppermute(
            lax.slice_in_dim(block, block.shape[dim] - width, None, axis=dim), axis, forward
        )
        high = lax.ppermute(lax.slice_in_dim(block, 0, width, axis=dim), axis, backward)
        block = jnp.concatenate([low, block, high], axis=dim)
    return block


def central(padded, axis, start, count):

    def window(offset):
        return lax.slice_in_dim(padded, start + offset, start + offset + count, axis=axis)

    return coef_near * (window(1) - window(-1)) + coef_far * (window(2) - window(-2))


def normal_diff(field, ghost):
    zeros = jnp.zeros_like(ghost)
    padded = jnp.concatenate([ghost, ghost, field, zeros, zeros], axis=0)
    return central(padded, 0, 2, field.shape[0])


def fault_update(prestress, normal_stress, crit_slip, flags, slip, stress_z, functional):
    trial = prestress + stress_z[0] + functional
    weaken = jnp.maximum(0.0, 1.0 - jnp.abs(slip) / crit_slip)
    strength = normal_stress * (dynamic_friction + (static_friction - dynamic_friction) * weaken)
    clipped = jnp.clip(trial, -strength, strength)
    traction = jnp.where(flags == 1, clipped, trial)
    rate = (trial - traction) / damping
    return (traction, slip + time_step * rate)


def factor_pair(length):
    first = 1
    candidate = 1
    while candidate * candidate <= length:
        if length % candidate == 0:
            first = candidate
        candidate += 1
    return (first, length // first)


def phase_table(count_a, count_b, length, sign):
    product = lax.iota(jnp.int32, count_a)[:, None] * lax.iota(jnp.int32, count_b)[None, :] % length
    angles = sign * 2.0 * math.pi / length * product.astype(jnp.float32)
    return (jnp.cos(angles), jnp.sin(angles))


def contract(form, left, right):
    return jnp.einsum(form, left, right, precision=lax.Precision.HIGHEST)


def transform_last(real_part, imag_part, sign):
    length = real_part.shape[-1]
    outer, inner = factor_pair(length)
    leading = real_part.shape[:-1]
    real_part = real_part.reshape(leading + (outer, inner))
    imag_part = imag_part.reshape(leading + (outer, inner))
    first_cos, first_sin = phase_table(outer, outer, outer, sign)
    middle_real = contract("kt,...tq->...kq", first_cos, real_part) - contract(
        "kt,...tq->...kq", first_sin, imag_part
    )
    middle_imag = contract("kt,...tq->...kq", first_cos, imag_part) + contract(
        "kt,...tq->...kq", first_sin, real_part
    )
    twist_cos, twist_sin = phase_table(outer, inner, length, sign)
    middle_real, middle_imag = (
        middle_real * twist_cos - middle_imag * twist_sin,
        middle_real * twist_sin + middle_imag * twist_cos,
    )
    second_cos, second_sin = phase_table(inner, inner, inner, sign)
    out_real = contract("...kt,tm->...km", middle_real, second_cos) - contract(
        "...kt,tm->...km", middle_imag, second_sin
    )
    out_imag = contract("...kt,tm->...km", middle_real, second_sin) + contract(
        "...kt,tm->...km", middle_imag, second_cos
    )
    scale = 1.0 / math.sqrt(length)
    out_real = jnp.swapaxes(out_real, -1, -2).reshape(leading + (length,)) * scale
    out_imag = jnp.swapaxes(out_imag, -1, -2).reshape(leading + (length,)) * scale
    return (out_real, out_imag)


def general_body(
    velocity,
    stress,
    shear_modulus,
    buoyancy,
    prestress,
    normal_stress,
    crit_slip,
    slip,
    traction,
    functional,
    flags,
    history,
    kernel,
):
    strike_count = lax.axis_size("strike")
    dip_count = lax.axis_size("dip")
    depth, rows_x, cols_y = velocity.shape
    ky_local = history.shape[2]
    total_x = history.shape[3]
    total_y = cols_y * dip_count
    line_rows = rows_x // dip_count
    stress_x, stress_y, stress_z = (stress[0], stress[1], stress[2])
    ghost_zero = jnp.zeros((1, rows_x, cols_y), jnp.float32)
    spectra = []
    for iteration in range(STEPS):
        padded_x = padded_2(stress_x, (("strike", 1),), 2)
        padded_y = padded_2(stress_y, (("dip", 2),), 2)
        divergence = (
            central(padded_x, 1, 2, rows_x)
            + central(padded_y, 2, 2, cols_y)
            + normal_diff(stress_z, traction[None])
        )
        velocity = velocity + courant * buoyancy * divergence
        padded_v = padded_2(velocity, (("strike", 1), ("dip", 2)), 2)
        grad_x = central(padded_v[:, :, 2 : cols_y + 2], 1, 2, rows_x)
        grad_y = central(padded_v[:, 2 : rows_x + 2, :], 2, 2, cols_y)
        stress_x = stress_x + courant * shear_modulus * grad_x
        stress_y = stress_y + courant * shear_modulus * grad_y
        stress_z = stress_z + courant * shear_modulus * normal_diff(velocity, ghost_zero)
        traction, slip = fault_update(
            prestress, normal_stress, crit_slip, flags, slip, stress_z, functional
        )
        lines = lax.all_to_all(slip, "dip", split_axis=0, concat_axis=1, tiled=True)
        part_real, part_imag = transform_last(lines, jnp.zeros_like(lines), -1.0)
        stacked = jnp.stack([part_real, part_imag]).reshape(
            2, line_rows, strike_count, dip_count, ky_local
        )
        stacked = stacked.transpose(0, 2, 3, 4, 1).reshape(
            2, strike_count, dip_count, ky_local, 1, 1, line_rows
        )
        halfway = lax.all_to_all(stacked, "strike", split_axis=1, concat_axis=4, tiled=True)
        owned = lax.all_to_all(halfway, "dip", split_axis=2, concat_axis=5, tiled=True)
        owned = owned.reshape(2, ky_local, total_x)
        spec_real, spec_imag = transform_last(owned[0], owned[1], -1.0)
        spectra = [(spec_real, spec_imag)] + spectra
        weights = kernel[iteration + 1 :].astype(jnp.float32)
        stored = jnp.sum(weights[:, None] * history[: history.shape[0] - iteration], axis=0)
        sum_real = stored[0]
        sum_imag = stored[1]
        for offset, item in enumerate(spectra):
            weight = kernel[offset].astype(jnp.float32)
            sum_real = sum_real + weight * item[0]
            sum_imag = sum_imag + weight * item[1]
        back_real, back_imag = transform_last(sum_real, sum_imag, 1.0)
        leaving = jnp.stack([back_real, back_imag]).reshape(
            2, 1, 1, ky_local, strike_count, dip_count, line_rows
        )
        partway = lax.all_to_all(leaving, "strike", split_axis=4, concat_axis=1, tiled=True)
        returned = lax.all_to_all(partway, "dip", split_axis=5, concat_axis=2, tiled=True)
        returned = returned.reshape(2, total_y, line_rows).transpose(0, 2, 1)
        field_real, field_imag = transform_last(returned[0], returned[1], 1.0)
        functional = lax.all_to_all(field_real, "dip", split_axis=1, concat_axis=0, tiled=True)
    return (velocity, jnp.stack([stress_x, stress_y, stress_z]), slip, traction, functional)


LANES = 128
SUBLANES = 8
MESH = pl.DeviceIdType.MESH
INPUTS = 18
KERNEL_VMEM = 67043328 - 1000000
HUGE = float(np.finfo(np.float32).max)


def split_bf16(value):
    high = value.astype(jnp.bfloat16)
    return high, (value - high.astype(jnp.float32)).astype(jnp.bfloat16)


def split_table(table):
    table = np.asarray(table, np.float32)
    high = table.astype(jnp.bfloat16)
    return high, (table - high.astype(np.float32)).astype(jnp.bfloat16)


def strike_table(total_x):
    index = np.arange(total_x)
    angle = 2.0 * np.pi / total_x * (index[:, None] * index[None, :] % total_x)
    return np.concatenate([np.cos(angle), np.sin(angle)], axis=1) / np.sqrt(total_x)


def dip_table(cols, total_y):
    count = cols // 2 + 2 * SUBLANES
    angle = 2.0 * np.pi / cols * (np.arange(count)[:, None] * np.arange(cols)[None, :] % cols)
    return np.concatenate([np.cos(angle), np.sin(angle)], axis=1) / np.sqrt(total_y)


def twiddle_table(dip_count, cols, total_y):
    place = np.arange(total_y).reshape(dip_count, 1, cols)
    freq = np.arange(dip_count)[None, :, None]
    angle = 2.0 * np.pi / total_y * (freq * place % total_y)
    return np.stack([np.cos(angle), -np.sin(angle)], axis=1).astype(np.float32)


def dot3(left, right_high, right_low):
    high, low = split_bf16(left)
    rows = left.shape[0]
    both = jnp.dot(
        jnp.concatenate([high, low], axis=0), right_high, preferred_element_type=jnp.float32
    )
    return both[:rows] + both[rows:] + jnp.dot(high, right_low, preferred_element_type=jnp.float32)


def dot3_nt(left_high, left_low, right):
    high, low = split_bf16(right)

    def product(a, b):
        return lax.dot_general(a, b, (((1,), (1,)), ((), ())), preferred_element_type=jnp.float32)

    return product(left_high, high) + product(left_high, low) + product(left_low, high)


def dot3_rows(left, right_high, right_low):
    high, low = split_bf16(left)
    rows = left.shape[0]

    def product(a, b):
        return lax.dot_general(a, b, (((1,), (1,)), ((), ())), preferred_element_type=jnp.float32)

    both = product(jnp.concatenate([high, low], axis=0), right_high)
    return both[:rows] + both[rows:] + product(high, right_low)


def rupture_kernel(strike_count, dip_count, *refs):
    sources, refs = refs[:INPUTS], refs[INPUTS:]
    results, refs = refs[:5], refs[5:]
    loaded, refs = refs[:INPUTS], refs[INPUTS:]
    (
        vel_in, stress_in, shear, buoy, prestress, normal_stress, crit_slip, slip_in, traction_in,
        functional_in, flags, hist, kern, dip_hi, dip_lo, strike_hi, strike_lo, twiddle,
    ) = loaded
    (
        padded, edge_x, edge_y, halo_x, halo_y, near_x, near_y,
        shared, gathered, send_f, recv_a, recv_b, lines_out,
        send_c, recv_c, modal, nought, nought_in, weight, source,
        load_sem, edge_sem, halo_sem, n_send, n_recv, g_send, g_recv,
        a_send, a_recv, b_send, b_recv, c_send, c_recv, x_send, x_recv, plane_sem,
    ) = refs
    vel, stress = results[:2]
    depth, rows, cols = vel_in.shape
    modes = hist.shape[2]
    total_x = hist.shape[3]
    stored_count = hist.shape[0]
    blocks = strike_count * dip_count
    half = modes // dip_count // 2
    wave = dip_count * rows
    front_modes = cols // 2
    my_s = lax.axis_index("strike")
    my_d = lax.axis_index("dip")
    my_block = my_s * dip_count + my_d
    upper = my_block // (blocks // 2)

    def ring(me, offset, count):
        return lax.rem(me + offset + count, count)

    def remote(src, dst, send_sem, recv_sem, target):
        return pltpu.make_async_remote_copy(
            src_ref=src,
            dst_ref=dst,
            send_sem=send_sem,
            recv_sem=recv_sem,
            device_id=target,
            device_id_type=MESH,
        )

    lane = lax.broadcasted_iota(jnp.int32, (rows, LANES), 1)
    column = lax.broadcasted_iota(jnp.int32, (rows, cols), 1)
    strip = lax.broadcasted_iota(jnp.int32, (SUBLANES, LANES), 1) // rows
    layer_row = lax.broadcasted_iota(jnp.int32, (SUBLANES, LANES), 0)
    real_half = layer_row < half
    sign = jnp.where(real_half, 1.0, -1.0)
    lone = jnp.logical_and(layer_row % half == 0, my_block == 0)
    swap = functools.partial(pltpu.roll, shift=half, axis=0)

    def slot(block):
        high = block // (blocks // 2)
        return 2 * block + high * (2 * blocks - 1 - 4 * block)

    def pack_x(turn, field):
        edge_x[turn, 0] = field[:, rows - 2 : rows, :]
        edge_x[turn, 1] = field[:, 0:2, :]

    def pack_y(turn, layer):
        low = jnp.zeros((rows, LANES), jnp.float32)
        high = jnp.zeros((rows, LANES), jnp.float32)
        for z in range(depth):
            here = lane // 2 == z
            last = layer(z)[:, cols - LANES :]
            first = layer(z)[:, :LANES]
            low = jnp.where(here, pltpu.roll(last, (2 * z + 2) % LANES, 1), low)
            high = jnp.where(here, pltpu.roll(first, 2 * z, 1) if z else first, high)
        edge_y[turn, 0] = low
        edge_y[turn, 1] = high

    def halo_copies(turn):
        copies = []
        for side, step in ((0, 1), (1, -1)):
            copies.append(
                remote(
                    edge_x.at[turn, side],
                    halo_x.at[turn, side],
                    edge_sem.at[turn, side],
                    halo_sem.at[turn, side],
                    {"strike": ring(my_s, step, strike_count)},
                )
            )
            copies.append(
                remote(
                    edge_y.at[turn, side],
                    halo_y.at[turn, side],
                    edge_sem.at[turn, side + 2],
                    halo_sem.at[turn, side + 2],
                    {"dip": ring(my_d, step, dip_count)},
                )
            )
        return copies

    def start_halos(turn):
        copies = halo_copies(turn)
        for copy in copies:
            copy.start()
        return copies

    def wait_halos(copies):
        for copy in copies:
            copy.wait_recv()

    def fill_padded(turn, field):
        padded[:, SUBLANES : SUBLANES + rows, :] = field[...]
        padded[:, SUBLANES - 2 : SUBLANES, :] = halo_x[turn, 0]
        padded[:, SUBLANES + rows : SUBLANES + rows + 2, :] = halo_x[turn, 1]

    def diff_x(z):
        def window(offset):
            return padded[z, SUBLANES + offset : SUBLANES + offset + rows, :]

        return coef_near * (window(1) - window(-1)) + coef_far * (window(2) - window(-2))

    def diff_y(turn, z, field):
        low = halo_y[turn, 0]
        high = halo_y[turn, 1]
        low_0, low_1 = low[:, 2 * z : 2 * z + 1], low[:, 2 * z + 1 : 2 * z + 2]
        high_0, high_1 = high[:, 2 * z : 2 * z + 1], high[:, 2 * z + 1 : 2 * z + 2]
        back_1 = jnp.where(column == 0, low_1, pltpu.roll(field, 1, 1))
        back_2 = jnp.where(
            column == 0, low_0, jnp.where(column == 1, low_1, pltpu.roll(field, 2, 1))
        )
        next_1 = jnp.where(column == cols - 1, high_0, pltpu.roll(field, cols - 1, 1))
        next_2 = jnp.where(
            column == cols - 2,
            high_0,
            jnp.where(column == cols - 1, high_1, pltpu.roll(field, cols - 2, 1)),
        )
        return coef_near * (next_1 - back_1) + coef_far * (next_2 - back_2)

    def diff_z(z, layer, ghost):
        def at(index):
            if index < 0:
                return ghost
            return layer(index) if index < depth else None

        total = None
        for offset, coef in ((1, coef_near), (-1, -coef_near), (2, coef_far), (-2, -coef_far)):
            value = at(z + offset)
            if value is not None:
                total = coef * value if total is None else total + coef * value
        return total

    def velocity_layer(turn, z, source, stress_ref, traction):
        divergence = (
            diff_x(z)
            + diff_y(turn, z, stress_ref[1, z])
            + diff_z(z, lambda i: stress_ref[2, i], traction)
        )
        vel[z] = source[z] + courant * buoy[z] * divergence

    def stress_z_layer(z, stress_ref):
        return stress_ref[2, z] + courant * shear[z] * diff_z(z, lambda i: vel[i], None)

    def stress_layers(turn, stress_ref):
        fill_padded(turn, vel)
        for z in range(depth):
            modulus = courant * shear[z]
            stress[0, z] = stress_ref[0, z] + modulus * diff_x(z)
            stress[1, z] = stress_ref[1, z] + modulus * diff_y(turn, z, vel[z])
            stress[2, z] = stress_z_layer(z, stress_ref)

    def start_near(kind, field):
        copies = []
        for side, step in ((0, 1), (1, -1)):
            row = 0 if side else rows - SUBLANES
            col = 0 if side else cols - LANES
            copies.append(
                remote(
                    field.at[pl.ds(1, 2), pl.ds(row, SUBLANES), :],
                    near_x.at[kind, side],
                    n_send.at[kind, side],
                    n_recv.at[kind, side],
                    {"strike": ring(my_s, step, strike_count)},
                )
            )
            copies.append(
                remote(
                    field.at[pl.ds(1, 2), :, pl.ds(col, LANES)],
                    near_y.at[kind, side],
                    n_send.at[kind, side + 2],
                    n_recv.at[kind, side + 2],
                    {"dip": ring(my_d, step, dip_count)},
                )
            )
        for copy in copies:
            copy.start()
        return copies

    def slope(field, axis):
        size = field.shape[axis]

        def at(offset):
            return pltpu.roll(field, -offset % size, axis)

        return coef_near * (at(1) - at(-1)) + coef_far * (at(2) - at(-2))

    def early_trial(traction):
        normal = [
            stress_in[2, z] + courant * shear[z] * diff_z(z, lambda i: vel[i], None)
            for z in range(min(5, depth))
        ]
        ahead = [None]
        zero = jnp.zeros((SUBLANES - 2, cols), jnp.float32)

        def widened(kind, field, z, axis):
            near = (near_x, near_y)[axis]
            return jnp.concatenate([near[kind, 0, z - 1], field[z], near[kind, 1, z - 1]], axis=axis)

        for z in (1, 2):
            face = jnp.concatenate(
                [zero, halo_x[0, 0, z], stress_in[0, z], halo_x[0, 1, z], zero], axis=0
            )
            face = face + courant * widened(0, shear, z, 0) * slope(widened(1, vel, z, 0), 0)
            total = slope(face, 0)[SUBLANES : SUBLANES + rows]
            face = jnp.concatenate(
                [
                    pltpu.roll(halo_y[0, 0], LANES - 2 - 2 * z, 1),
                    stress_in[1, z],
                    pltpu.roll(halo_y[0, 1], LANES - 2 * z, 1),
                ],
                axis=1,
            )
            face = face + courant * widened(0, shear, z, 1) * slope(widened(1, vel, z, 1), 1)
            total = total + slope(face, 1)[:, LANES : LANES + cols]
            total = total + diff_z(z, lambda i: normal[i], traction)
            ahead.append(vel[z] + courant * buoy[z] * total)
        return prestress[...] + (
            normal[0] + courant * shear[0] * diff_z(0, lambda i: ahead[i], None)
        )

    def start_gather(turn, value):
        shared[turn] = value
        gathered[turn, my_d] = value
        copies = []
        for k in range(1, dip_count):
            copy = remote(
                shared.at[turn],
                gathered.at[turn, my_d],
                g_send.at[turn, k],
                g_recv.at[turn, k],
                {"dip": ring(my_d, k, dip_count)},
            )
            copy.start()
            copies.append(copy)
        return copies

    def wait_gather(turn):
        for k in range(1, dip_count):
            source = ring(my_d, -k, dip_count)
            remote(
                shared.at[turn],
                gathered.at[turn, source],
                g_send.at[turn, k],
                g_recv.at[turn, k],
                {"dip": source},
            ).wait_recv()

    def start_b():
        recv_b[my_s] = send_f[1, slot(my_block)]
        copies = []
        for k in range(1, strike_count):
            target = ring(my_s, k, strike_count)
            copy = remote(
                send_f.at[1, slot(target * dip_count + my_d)],
                recv_b.at[my_s],
                b_send.at[k],
                b_recv.at[k],
                {"strike": target},
            )
            copy.start()
            copies.append(copy)
        return copies

    def wait_b():
        for k in range(1, strike_count):
            source_s = ring(my_s, -k, strike_count)
            remote(
                send_f.at[1, source_s],
                recv_b.at[source_s],
                b_send.at[k],
                b_recv.at[k],
                {"strike": source_s},
            ).wait_recv()

    offsets = [
        (i, k) for k in reversed(range(dip_count)) for i in reversed(range(strike_count)) if i or k
    ]

    def start_a():
        recv_a[my_d, my_s] = send_f[0, slot(my_block)]
        copies = []
        for i, k in offsets:
            target_s, target_d = ring(my_s, i, strike_count), ring(my_d, k, dip_count)
            copy = remote(
                send_f.at[0, slot(target_s * dip_count + target_d)],
                recv_a.at[my_d, my_s],
                a_send.at[k, i],
                a_recv.at[k, i],
                {"strike": target_s, "dip": target_d},
            )
            copy.start()
            copies.append(copy)
        return copies

    def wait_a():
        for i, k in reversed(offsets):
            source_s, source_d = ring(my_s, -i, strike_count), ring(my_d, -k, dip_count)
            remote(
                send_f.at[0, source_s],
                recv_a.at[source_d, source_s],
                a_send.at[k, i],
                a_recv.at[k, i],
                {"strike": source_s, "dip": source_d},
            ).wait_recv()

    def exchange_copies(turn):
        other = blocks - 1 - my_block
        single = 1 - jnp.minimum(lax.rem(my_block, blocks // 2), 1)
        mirror = lax.rem(blocks - my_block + single * (blocks // 2), blocks)
        upper_rows = pl.ds(modes // 2, modes // 2)
        return [
            remote(
                modal.at[turn, 0, :, upper_rows, :],
                modal.at[turn, 1, :, upper_rows, :],
                x_send.at[turn, 0],
                x_recv.at[turn, 0],
                {"strike": other // dip_count, "dip": lax.rem(other, dip_count)},
            ),
            remote(
                nought.at[turn],
                nought_in.at[turn],
                x_send.at[turn, 1],
                x_recv.at[turn, 1],
                {"strike": mirror // dip_count, "dip": lax.rem(mirror, dip_count)},
            ),
        ]

    def start_exchange(turn):
        copies = exchange_copies(turn)
        for copy in copies:
            copy.start()
        return copies

    def arrange(turn, copies):
        for copy in copies:
            copy.wait_recv()
        modal[turn, 1, :, modes : modes + 1, :] = nought_in[turn]
        for k0 in range(dip_count):
            for m in range(half):
                at = dip_count * m + k0
                plus = modal[turn, upper, :, pl.ds(modes // 2 * upper + at, 1), :]
                minus = modal[turn, 1 - upper, :, pl.ds(modes - modes // 2 * upper - at, 1), :]
                for side, value in enumerate((plus, minus)):
                    weight[turn, side, k0, m : m + 1, :] = value[0]
                    weight[turn, side, k0, half + m : half + m + 1, :] = value[0]
                    source[turn, side, k0, m : m + 1, :] = value[1]
                    source[turn, side, k0, half + m : half + m + 1, :] = value[2]

    def start_c(step):
        recv_c[step, slot(my_block)] = send_c[step, my_s]
        copies = []
        for i, k in offsets:
            target_s, target_d = ring(my_s, i, strike_count), ring(my_d, k, dip_count)
            copy = remote(
                send_c.at[step, target_s],
                recv_c.at[step, slot(my_block)],
                c_send.at[step, k, i],
                c_recv.at[step, k, i],
                {"strike": target_s, "dip": target_d},
            )
            copy.start()
            copies.append(copy)
        return copies

    def wait_c(step):
        for i, k in reversed(offsets):
            source_s, source_d = ring(my_s, -i, strike_count), ring(my_d, -k, dip_count)
            remote(
                send_c.at[step, source_s],
                recv_c.at[step, slot(source_s * dip_count + source_d)],
                c_send.at[step, k, i],
                c_recv.at[step, k, i],
                {"strike": source_s, "dip": source_d},
            ).wait_recv()

    def total_of(terms):
        total = None
        for left, right in terms:
            total = left * right if total is None else total + left * right
        return total

    def turned(i, part, k0):
        return twiddle[i, part, k0 : k0 + 1, :]

    def dip_forward(step, parts):
        real, imag = (
            jnp.concatenate(
                [
                    total_of([(part, turned(i, kind, k0)) for i, part in parts])
                    for k0 in range(dip_count)
                ],
                axis=0,
            )
            for kind in range(2)
        )
        both = jnp.concatenate(
            [
                jnp.concatenate([real, imag], axis=1),
                jnp.concatenate([imag, -real], axis=1),
            ],
            axis=0,
        )
        out = dot3_nt(dip_hi[...], dip_lo[...], both)
        last = pltpu.roll(out[front_modes : front_modes + SUBLANES], wave, 1)
        first = jnp.where(
            jnp.logical_and(layer_row == 0, strip == dip_count), last, out[:SUBLANES]
        )
        out = jnp.concatenate([first, out[SUBLANES:front_modes]], axis=0)
        send_f[step] = out.reshape(blocks, half, LANES)

    def strike_forward(pieces):
        stacks = [None] * dip_count
        for s, piece in enumerate(pieces):
            pair = jnp.concatenate([piece, pltpu.roll(piece, wave, 1)], axis=0)
            for k0 in range(dip_count):
                shift = rows * (s - k0) % LANES
                moved = pltpu.roll(pair, shift, 1) if shift else pair
                stacks[k0] = moved if s == 0 else jnp.where(strip == s, moved, stacks[k0])
        both = dot3(jnp.concatenate(stacks, axis=0), strike_hi[...], strike_lo[...])
        plus, minus = [], []
        for k0 in range(dip_count):
            tile = both[k0 * SUBLANES : (k0 + 1) * SUBLANES]
            cos, sin = tile[:, :total_x], tile[:, total_x:]
            crossed = swap(sin)
            ahead = cos + sign * crossed
            behind = sign * cos - crossed
            if k0 == 0:
                ahead = jnp.where(lone, jnp.where(real_half, cos, -crossed), ahead)
                behind = jnp.where(lone, jnp.where(real_half, swap(cos), -sin), behind)
            plus.append(ahead)
            minus.append(behind)
        return plus, minus

    def convolve(step, spectra):
        sums = []
        for side in range(2):
            tiles = []
            for k0 in range(dip_count):
                total = source[step, side, k0]
                for offset, item in enumerate(spectra):
                    total = total + weight[offset, side, k0] * item[side][k0]
                tiles.append(total)
            sums.append(tiles)
        return sums

    def strike_inverse(step, plus, minus):
        tiles = []
        for k0, (ahead, behind) in enumerate(zip(plus, minus)):
            direct = ahead + sign * behind
            crossed = -sign * swap(ahead - sign * behind)
            if k0 == 0:
                direct = jnp.where(lone, jnp.where(real_half, ahead, swap(behind)), direct)
                crossed = jnp.where(lone, -jnp.where(real_half, swap(ahead), behind), crossed)
            tiles.append(jnp.concatenate([direct, crossed], axis=1))
        out = dot3_rows(jnp.concatenate(tiles, axis=0), strike_hi[...], strike_lo[...])
        for s in range(strike_count):
            block = None
            for k0 in range(dip_count):
                shift = rows * (k0 - s) % LANES
                tile = out[k0 * SUBLANES : (k0 + 1) * SUBLANES]
                moved = pltpu.roll(tile, shift, 1) if shift else tile
                block = moved if k0 == 0 else jnp.where(strip == k0, moved, block)
            block = jnp.where(strip < dip_count, block, swap(pltpu.roll(block, wave, 1)))
            send_c[step, s] = block[:half]

    def dip_inverse(step, places):
        lines = recv_c[step].reshape(front_modes, LANES).T
        out = dot3(lines, dip_hi[:front_modes], dip_lo[:front_modes])
        real = out[:wave, :cols] - out[wave:, cols:]
        imag = out[:wave, cols:] + out[wave:, :cols]
        scale = 1.0 / math.sqrt(cols * dip_count)
        last = lines[wave : wave + rows, 0:1] * jnp.where(column % 2 == 0, scale, -scale)
        result = []
        for i in places:
            terms = [(real[:rows] + last, turned(i, 0, 0))]
            for k0 in range(1, dip_count):
                at = slice(k0 * rows, (k0 + 1) * rows)
                terms += [(real[at], turned(i, 0, k0)), (imag[at], turned(i, 1, k0))]
            result.append(total_of(terms))
        return result

    def store_history():
        zero = jnp.zeros((2, modes, total_x), jnp.float32)
        common = stored_count - STEPS + 1

        def term(t, j):
            return kern[j + t + 1].astype(jnp.float32)[None] * hist[j]

        def add(j, sums):
            return tuple(total + term(t, j) for t, total in enumerate(sums))

        sums = lax.fori_loop(0, common, add, (zero,) * STEPS)
        for t in range(STEPS):
            total = sums[t]
            for j in range(common, stored_count - t):
                total = total + term(t, j)
            values = (kern[t].astype(jnp.float32), total[0], total[1])
            for i, value in enumerate(values):
                modal[t, 0, i, 0:modes, :] = value
                nought[t, i] = value[0:1]

    def bound_of(slip):
        weaken = jnp.maximum(0.0, 1.0 - jnp.abs(slip) / crit_slip[...])
        strength = normal_stress[...] * (
            dynamic_friction + (static_friction - dynamic_friction) * weaken
        )
        return jnp.where(flags[...] == 1, strength, HUGE)

    def slide(trial, bound, slip):
        traction = jnp.clip(trial, -bound, bound)
        return traction, slip + time_step * ((trial - traction) / damping)

    barrier = pltpu.get_barrier_semaphore()
    for k in range(1, strike_count):
        pl.semaphore_signal(
            barrier, inc=1, device_id={"strike": ring(my_s, k, strike_count)}, device_id_type=MESH
        )
    for k in range(1, dip_count):
        pl.semaphore_signal(
            barrier, inc=1, device_id={"dip": ring(my_d, k, dip_count)}, device_id_type=MESH
        )
    loads = [
        pltpu.make_async_copy(sources[i], loaded[i], load_sem.at[i]) for i in range(INPUTS)
    ]
    loads[1].start()
    for i in range(INPUTS):
        if i != 1:
            loads[i].start()
    loads[1].wait()
    pack_x(0, stress_in.at[0])
    pack_y(0, lambda z: stress_in[1, z])
    pl.semaphore_wait(barrier, strike_count + dip_count - 2)

    started = []
    halos = start_halos(0)
    started += halos
    for k in range(1, dip_count):
        pl.semaphore_signal(
            plane_sem, inc=1, device_id={"dip": ring(my_d, k, dip_count)}, device_id_type=MESH
        )
    for i in range(INPUTS):
        if i != 1:
            loads[i].wait()
    near = start_near(0, shear)
    started += near
    store_history()
    pl.semaphore_wait(plane_sem, dip_count - 1)
    exchanged = start_exchange(0)
    started += exchanged

    ghost = traction_in[...]
    front = min(3, depth)
    base = prestress[...] + functional_in[...]
    bound = bound_of(slip_in[...])
    wait_halos(halos)
    fill_padded(0, stress_in.at[0])
    for z in range(1, front):
        velocity_layer(0, z, vel_in, stress_in, ghost)
    wide = start_near(1, vel)
    traction, slip = slide(base + stress_z_layer(0, stress_in), bound, slip_in[...])
    dip_forward(0, [(my_d, slip)])
    started += start_a()
    started += start_gather(0, bound_of(slip))
    for z in (0, *range(front, depth)):
        velocity_layer(0, z, vel_in, stress_in, ghost)
    pack_x(1, vel)
    pack_y(1, lambda z: vel[z])
    halos = start_halos(1)
    started += halos
    late = start_exchange(1)
    started += late
    wait_halos(near + wide)
    started += start_gather(1, early_trial(traction))
    arrange(0, exchanged)
    wait_a()
    pieces = []
    for s in range(strike_count):
        piece = recv_a[0, s]
        for i in range(1, dip_count):
            piece = piece + recv_a[i, s]
        pieces.append(piece)
    spectra = [strike_forward(pieces)]
    strike_inverse(0, *convolve(0, spectra))
    started += start_c(0)

    wait_halos(halos)
    stress_layers(1, stress_in)
    pack_x(2, stress.at[0])
    pack_y(2, lambda z: stress[1, z])
    halos = start_halos(2)
    started += halos
    arrange(1, late)
    for turn in range(2):
        wait_gather(turn)
    wait_c(0)
    changes = []
    for i, value in enumerate(dip_inverse(0, range(dip_count))):
        trial = gathered[1, i] + value
        bound = gathered[0, i]
        clipped = jnp.clip(trial, -bound, bound)
        change = time_step * ((trial - clipped) / damping)
        lines_out[0, i] = change
        lines_out[1, i] = clipped
        changes.append((i, change))
    dip_forward(1, changes)
    started += start_b()
    results[2][...] = slip + lines_out[0, my_d]
    results[3][...] = lines_out[1, my_d]
    wait_halos(halos)
    fill_padded(2, stress.at[0])
    for copy in wide:
        copy.wait_send()
    for z in range(depth):
        velocity_layer(2, z, vel, stress, traction)
    pack_x(3, vel)
    pack_y(3, lambda z: vel[z])
    halos = start_halos(3)
    started += halos
    wait_b()
    change = strike_forward([recv_b[s] for s in range(strike_count)])
    latest = [[old + new for old, new in zip(*pair)] for pair in zip(spectra[0], change)]
    spectra = [latest] + spectra
    strike_inverse(1, *convolve(1, spectra))
    started += start_c(1)
    wait_halos(halos)
    stress_layers(3, stress)
    for copy in started:
        copy.wait_send()
    wait_c(1)
    results[4][...] = dip_inverse(1, [my_d])[0]


def copy_kernel(*refs):
    sources, results, sems = refs[:5], refs[5:10], refs[10]
    saves = [pltpu.make_async_copy(sources[i], results[i], sems.at[i]) for i in range(5)]
    for save in saves:
        save.start()
    for save in saves:
        save.wait()


def fits_kernel(strike_count, dip_count, depth, rows, cols, modes, total_x):
    return (
        STEPS == 2
        and depth > 2
        and strike_count > 1
        and dip_count > 1
        and modes == dip_count * SUBLANES
        and rows % SUBLANES == 0
        and cols == 2 * LANES
        and total_x == LANES
        and 2 * dip_count * rows == LANES
        and strike_count * dip_count * SUBLANES == cols
    )


def body(*args):
    velocity, history = args[0], args[11]
    strike_count = lax.axis_size("strike")
    dip_count = lax.axis_size("dip")
    depth, rows, cols = velocity.shape
    modes, total_x = history.shape[2:]
    if not fits_kernel(strike_count, dip_count, depth, rows, cols, modes, total_x):
        return general_body(*args)
    half = SUBLANES // 2
    blocks = strike_count * dip_count
    total_y = cols * dip_count
    tables = (
        *split_table(dip_table(cols, total_y)),
        *split_table(strike_table(total_x)),
        twiddle_table(dip_count, cols, total_y),
    )
    turns = 2 * STEPS
    f32 = jnp.float32
    dma = pltpu.SemaphoreType.DMA
    operands = (*args, *[jnp.asarray(table) for table in tables])
    shapes = (velocity.shape, args[1].shape) + ((rows, cols),) * 3
    outs = tuple(jax.ShapeDtypeStruct(shape, f32) for shape in shapes)
    held = tuple(pltpu.VMEM(shape, f32) for shape in shapes)
    scratch = [pltpu.VMEM(operand.shape, operand.dtype) for operand in operands] + [
        pltpu.VMEM((depth, rows + 2 * SUBLANES, cols), f32),
        pltpu.VMEM((turns, 2, depth, 2, cols), f32),
        pltpu.VMEM((turns, 2, rows, LANES), f32),
        pltpu.VMEM((turns, 2, depth, 2, cols), f32),
        pltpu.VMEM((turns, 2, rows, LANES), f32),
        pltpu.VMEM((2, 2, 2, SUBLANES, cols), f32),
        pltpu.VMEM((2, 2, 2, rows, LANES), f32),
        pltpu.VMEM((2, rows, cols), f32),
        pltpu.VMEM((2, dip_count, rows, cols), f32),
        pltpu.VMEM((STEPS, blocks, half, LANES), f32),
        pltpu.VMEM((dip_count, strike_count, half, LANES), f32),
        pltpu.VMEM((strike_count, half, LANES), f32),
        pltpu.VMEM((2, dip_count, rows, cols), f32),
        pltpu.VMEM((STEPS, strike_count, half, LANES), f32),
        pltpu.VMEM((STEPS, blocks, half, LANES), f32),
        pltpu.VMEM((STEPS, 2, 3, modes + SUBLANES, total_x), f32),
        pltpu.VMEM((STEPS, 3, 1, total_x), f32),
        pltpu.VMEM((STEPS, 3, 1, total_x), f32),
        pltpu.VMEM((STEPS, 2, dip_count, SUBLANES, total_x), f32),
        pltpu.VMEM((STEPS, 2, dip_count, SUBLANES, total_x), f32),
        dma((len(operands),)),
        dma((turns, 4)),
        dma((turns, 4)),
        dma((2, 4)),
        dma((2, 4)),
        dma((2, dip_count)),
        dma((2, dip_count)),
        dma((dip_count, strike_count)),
        dma((dip_count, strike_count)),
        dma((strike_count,)),
        dma((strike_count,)),
        dma((STEPS, dip_count, strike_count)),
        dma((STEPS, dip_count, strike_count)),
        dma((STEPS, 2)),
        dma((STEPS, 2)),
        pltpu.SemaphoreType.REGULAR,
    ]
    anywhere = pl.BlockSpec(memory_space=pl.ANY)
    results = pl.pallas_call(
        functools.partial(rupture_kernel, strike_count, dip_count),
        out_shape=held,
        in_specs=[pl.BlockSpec(memory_space=pltpu.HBM)] * len(operands),
        out_specs=(pl.BlockSpec(memory_space=pltpu.VMEM),) * len(outs),
        scratch_shapes=scratch,
        compiler_params=pltpu.CompilerParams(
            collective_id=0, has_side_effects=True, vmem_limit_bytes=KERNEL_VMEM
        ),
    )(*operands)
    return pl.pallas_call(
        copy_kernel,
        out_shape=outs,
        in_specs=[pl.BlockSpec(memory_space=pltpu.VMEM)] * len(outs),
        out_specs=(anywhere,) * len(outs),
        scratch_shapes=[dma((len(outs),))],
        compiler_params=pltpu.CompilerParams(vmem_limit_bytes=2**20),
    )(*results)


def solution(mesh):
    return jax.shard_map(
        body,
        mesh=mesh,
        in_specs=(
            P(None, "strike", "dip"),
            P(None, None, "strike", "dip"),
            P(None, "strike", "dip"),
            P(None, "strike", "dip"),
            P("strike", "dip"),
            P("strike", "dip"),
            P("strike", "dip"),
            P("strike", "dip"),
            P("strike", "dip"),
            P("strike", "dip"),
            P("strike", "dip"),
            P(None, None, ("strike", "dip"), None),
            P(None, ("strike", "dip"), None),
        ),
        out_specs=(
            P(None, "strike", "dip"),
            P(None, None, "strike", "dip"),
            P("strike", "dip"),
            P("strike", "dip"),
            P("strike", "dip"),
        ),
        check_vma=False,
    )
```

```python
import functools
import math

import jax
import jax.numpy as jnp
import numpy as np
from jax import lax
from jax.experimental import pallas as pl
from jax.experimental.pallas import tpu as pltpu
from jax.sharding import PartitionSpec as P

STEPS = 2


coef_near = 2.0 / 3.0
coef_far = -1.0 / 12.0
courant = 0.3
static_friction = 0.677
dynamic_friction = 0.525
damping = 0.5
time_step = 0.3


def padded_2(block, sides, width):
    for axis, dim in sides:
        count = lax.axis_size(axis)
        forward = [(i, i + 1) for i in range(count - 1)]
        forward.append((count - 1, 0))
        backward = [(target, source) for source, target in forward]
        low = lax.ppermute(
            lax.slice_in_dim(block, block.shape[dim] - width, None, axis=dim), axis, forward
        )
        high = lax.ppermute(lax.slice_in_dim(block, 0, width, axis=dim), axis, backward)
        block = jnp.concatenate([low, block, high], axis=dim)
    return block


def central(padded, axis, start, count):

    def window(offset):
        return lax.slice_in_dim(padded, start + offset, start + offset + count, axis=axis)

    return coef_near * (window(1) - window(-1)) + coef_far * (window(2) - window(-2))


def normal_diff(field, ghost):
    zeros = jnp.zeros_like(ghost)
    padded = jnp.concatenate([ghost, ghost, field, zeros, zeros], axis=0)
    return central(padded, 0, 2, field.shape[0])


def fault_update(prestress, normal_stress, crit_slip, flags, slip, stress_z, functional):
    trial = prestress + stress_z[0] + functional
    weaken = jnp.maximum(0.0, 1.0 - jnp.abs(slip) / crit_slip)
    strength = normal_stress * (dynamic_friction + (static_friction - dynamic_friction) * weaken)
    clipped = jnp.clip(trial, -strength, strength)
    traction = jnp.where(flags == 1, clipped, trial)
    rate = (trial - traction) / damping
    return (traction, slip + time_step * rate)


def factor_pair(length):
    first = 1
    candidate = 1
    while candidate * candidate <= length:
        if length % candidate == 0:
            first = candidate
        candidate += 1
    return (first, length // first)


def phase_table(count_a, count_b, length, sign):
    product = lax.iota(jnp.int32, count_a)[:, None] * lax.iota(jnp.int32, count_b)[None, :] % length
    angles = sign * 2.0 * math.pi / length * product.astype(jnp.float32)
    return (jnp.cos(angles), jnp.sin(angles))


def contract(form, left, right):
    return jnp.einsum(form, left, right, precision=lax.Precision.HIGHEST)


def transform_last(real_part, imag_part, sign):
    length = real_part.shape[-1]
    outer, inner = factor_pair(length)
    leading = real_part.shape[:-1]
    real_part = real_part.reshape(leading + (outer, inner))
    imag_part = imag_part.reshape(leading + (outer, inner))
    first_cos, first_sin = phase_table(outer, outer, outer, sign)
    middle_real = contract("kt,...tq->...kq", first_cos, real_part) - contract(
        "kt,...tq->...kq", first_sin, imag_part
    )
    middle_imag = contract("kt,...tq->...kq", first_cos, imag_part) + contract(
        "kt,...tq->...kq", first_sin, real_part
    )
    twist_cos, twist_sin = phase_table(outer, inner, length, sign)
    middle_real, middle_imag = (
        middle_real * twist_cos - middle_imag * twist_sin,
        middle_real * twist_sin + middle_imag * twist_cos,
    )
    second_cos, second_sin = phase_table(inner, inner, inner, sign)
    out_real = contract("...kt,tm->...km", middle_real, second_cos) - contract(
        "...kt,tm->...km", middle_imag, second_sin
    )
    out_imag = contract("...kt,tm->...km", middle_real, second_sin) + contract(
        "...kt,tm->...km", middle_imag, second_cos
    )
    scale = 1.0 / math.sqrt(length)
    out_real = jnp.swapaxes(out_real, -1, -2).reshape(leading + (length,)) * scale
    out_imag = jnp.swapaxes(out_imag, -1, -2).reshape(leading + (length,)) * scale
    return (out_real, out_imag)


def general_body(
    velocity,
    stress,
    shear_modulus,
    buoyancy,
    prestress,
    normal_stress,
    crit_slip,
    slip,
    traction,
    functional,
    flags,
    history,
    kernel,
):
    strike_count = lax.axis_size("strike")
    dip_count = lax.axis_size("dip")
    depth, rows_x, cols_y = velocity.shape
    ky_local = history.shape[2]
    total_x = history.shape[3]
    total_y = cols_y * dip_count
    line_rows = rows_x // dip_count
    stress_x, stress_y, stress_z = (stress[0], stress[1], stress[2])
    ghost_zero = jnp.zeros((1, rows_x, cols_y), jnp.float32)
    spectra = []
    for iteration in range(STEPS):
        padded_x = padded_2(stress_x, (("strike", 1),), 2)
        padded_y = padded_2(stress_y, (("dip", 2),), 2)
        divergence = (
            central(padded_x, 1, 2, rows_x)
            + central(padded_y, 2, 2, cols_y)
            + normal_diff(stress_z, traction[None])
        )
        velocity = velocity + courant * buoyancy * divergence
        padded_v = padded_2(velocity, (("strike", 1), ("dip", 2)), 2)
        grad_x = central(padded_v[:, :, 2 : cols_y + 2], 1, 2, rows_x)
        grad_y = central(padded_v[:, 2 : rows_x + 2, :], 2, 2, cols_y)
        stress_x = stress_x + courant * shear_modulus * grad_x
        stress_y = stress_y + courant * shear_modulus * grad_y
        stress_z = stress_z + courant * shear_modulus * normal_diff(velocity, ghost_zero)
        traction, slip = fault_update(
            prestress, normal_stress, crit_slip, flags, slip, stress_z, functional
        )
        lines = lax.all_to_all(slip, "dip", split_axis=0, concat_axis=1, tiled=True)
        part_real, part_imag = transform_last(lines, jnp.zeros_like(lines), -1.0)
        stacked = jnp.stack([part_real, part_imag]).reshape(
            2, line_rows, strike_count, dip_count, ky_local
        )
        stacked = stacked.transpose(0, 2, 3, 4, 1).reshape(
            2, strike_count, dip_count, ky_local, 1, 1, line_rows
        )
        halfway = lax.all_to_all(stacked, "strike", split_axis=1, concat_axis=4, tiled=True)
        owned = lax.all_to_all(halfway, "dip", split_axis=2, concat_axis=5, tiled=True)
        owned = owned.reshape(2, ky_local, total_x)
        spec_real, spec_imag = transform_last(owned[0], owned[1], -1.0)
        spectra = [(spec_real, spec_imag)] + spectra
        weights = kernel[iteration + 1 :].astype(jnp.float32)
        stored = jnp.sum(weights[:, None] * history[: history.shape[0] - iteration], axis=0)
        sum_real = stored[0]
        sum_imag = stored[1]
        for offset, item in enumerate(spectra):
            weight = kernel[offset].astype(jnp.float32)
            sum_real = sum_real + weight * item[0]
            sum_imag = sum_imag + weight * item[1]
        back_real, back_imag = transform_last(sum_real, sum_imag, 1.0)
        leaving = jnp.stack([back_real, back_imag]).reshape(
            2, 1, 1, ky_local, strike_count, dip_count, line_rows
        )
        partway = lax.all_to_all(leaving, "strike", split_axis=4, concat_axis=1, tiled=True)
        returned = lax.all_to_all(partway, "dip", split_axis=5, concat_axis=2, tiled=True)
        returned = returned.reshape(2, total_y, line_rows).transpose(0, 2, 1)
        field_real, field_imag = transform_last(returned[0], returned[1], 1.0)
        functional = lax.all_to_all(field_real, "dip", split_axis=1, concat_axis=0, tiled=True)
    return (velocity, jnp.stack([stress_x, stress_y, stress_z]), slip, traction, functional)


LANES = 128
SUBLANES = 8
MESH = pl.DeviceIdType.MESH
INPUTS = 18
PASSED = (13, 14, 17)
KERNEL_VMEM = 67043328 - 1500000
HUGE = float(np.finfo(np.float32).max)


def split_bf16(value):
    high = value.astype(jnp.bfloat16)
    return high, (value - high.astype(jnp.float32)).astype(jnp.bfloat16)


def split_table(table):
    table = np.asarray(table, np.float32)
    high = table.astype(jnp.bfloat16)
    return high, (table - high.astype(np.float32)).astype(jnp.bfloat16)


def strike_table(total_x):
    index = np.arange(total_x)
    angle = 2.0 * np.pi / total_x * (index[:, None] * index[None, :] % total_x)
    return np.concatenate([np.cos(angle), np.sin(angle)], axis=1) / np.sqrt(total_x)


def dip_table(cols, total_y):
    count = cols // 2 + 2 * SUBLANES
    angle = 2.0 * np.pi / cols * (np.arange(count)[:, None] * np.arange(cols)[None, :] % cols)
    return np.concatenate([np.cos(angle), np.sin(angle)], axis=1) / np.sqrt(total_y)


def twiddle_table(dip_count, cols, total_y):
    place = np.arange(total_y).reshape(dip_count, 1, cols)
    freq = np.arange(dip_count)[None, :, None]
    angle = 2.0 * np.pi / total_y * (freq * place % total_y)
    return np.stack([np.cos(angle), -np.sin(angle)], axis=1).astype(np.float32)


def dot3(left, right_high, right_low):
    high, low = split_bf16(left)
    rows = left.shape[0]
    both = jnp.dot(
        jnp.concatenate([high, low], axis=0), right_high, preferred_element_type=jnp.float32
    )
    return both[:rows] + both[rows:] + jnp.dot(high, right_low, preferred_element_type=jnp.float32)


def dot3_nt(left_high, left_low, right):
    high, low = split_bf16(right)

    def product(a, b):
        return lax.dot_general(a, b, (((1,), (1,)), ((), ())), preferred_element_type=jnp.float32)

    return product(left_high, high) + product(left_high, low) + product(left_low, high)


def dot3_rows(left, right_high, right_low):
    high, low = split_bf16(left)
    rows = left.shape[0]

    def product(a, b):
        return lax.dot_general(a, b, (((1,), (1,)), ((), ())), preferred_element_type=jnp.float32)

    both = product(jnp.concatenate([high, low], axis=0), right_high)
    return both[:rows] + both[rows:] + product(high, right_low)


def total_of(terms):
    total = None
    for left, right in terms:
        total = left * right if total is None else total + left * right
    return total


def dip_inverse_lines(back, dip_hi, dip_lo, twiddle, places):
    dip_count, _, _, cols = twiddle.shape
    count = cols // 2
    wave = LANES // 2
    rows = wave // dip_count
    lines = back[...].reshape(count, LANES).T
    out = dot3(lines, dip_hi[:count], dip_lo[:count])
    real = out[:wave, :cols] - out[wave:, cols:]
    imag = out[:wave, cols:] + out[wave:, :cols]
    scale = 1.0 / math.sqrt(cols * dip_count)
    column = lax.broadcasted_iota(jnp.int32, (rows, cols), 1)
    last = lines[wave : wave + rows, 0:1] * jnp.where(column % 2 == 0, scale, -scale)
    result = []
    for i in places:
        terms = [(real[:rows] + last, twiddle[i, 0, 0:1, :])]
        for k0 in range(1, dip_count):
            at = slice(k0 * rows, (k0 + 1) * rows)
            terms.append((real[at], twiddle[i, 0, k0 : k0 + 1, :]))
            terms.append((imag[at], twiddle[i, 1, k0 : k0 + 1, :]))
        result.append(total_of(terms))
    return result


def rupture_kernel(strike_count, dip_count, *refs):
    sources, refs = refs[:INPUTS], refs[INPUTS:]
    results, refs = refs[:8], refs[8:]
    loaded, refs = list(refs[: INPUTS - 3]), refs[INPUTS - 3 :]
    for place, result in zip(PASSED, results[5:]):
        loaded.insert(place, result)
    (
        vel_in, stress_in, shear, buoy, prestress, normal_stress, crit_slip, slip_in, traction_in,
        functional_in, flags, hist, kern, dip_hi, dip_lo, strike_hi, strike_lo, twiddle,
    ) = loaded
    (
        padded, edge_x, edge_y, halo_x, halo_y, near_x, near_y,
        shared, gathered, send_f, recv_a, recv_b, lines_out,
        send_c, recv_c, modal, nought, nought_in, weight, source,
        load_sem, edge_sem, halo_sem, n_send, n_recv, g_send, g_recv,
        a_send, a_recv, b_send, b_recv, c_send, c_recv, x_send, x_recv, plane_sem,
    ) = refs
    vel, stress = results[:2]
    back = (recv_c, results[4])
    depth, rows, cols = vel_in.shape
    modes = hist.shape[2]
    total_x = hist.shape[3]
    stored_count = hist.shape[0]
    blocks = strike_count * dip_count
    half = modes // dip_count // 2
    wave = dip_count * rows
    front_modes = cols // 2
    my_s = lax.axis_index("strike")
    my_d = lax.axis_index("dip")
    my_block = my_s * dip_count + my_d
    upper = my_block // (blocks // 2)

    def ring(me, offset, count):
        return lax.rem(me + offset + count, count)

    def remote(src, dst, send_sem, recv_sem, target):
        return pltpu.make_async_remote_copy(
            src_ref=src,
            dst_ref=dst,
            send_sem=send_sem,
            recv_sem=recv_sem,
            device_id=target,
            device_id_type=MESH,
        )

    lane = lax.broadcasted_iota(jnp.int32, (rows, LANES), 1)
    column = lax.broadcasted_iota(jnp.int32, (rows, cols), 1)
    strip = lax.broadcasted_iota(jnp.int32, (SUBLANES, LANES), 1) // rows
    layer_row = lax.broadcasted_iota(jnp.int32, (SUBLANES, LANES), 0)
    real_half = layer_row < half
    sign = jnp.where(real_half, 1.0, -1.0)
    lone = jnp.logical_and(layer_row % half == 0, my_block == 0)
    swap = functools.partial(pltpu.roll, shift=half, axis=0)

    def slot(block):
        high = block // (blocks // 2)
        return 2 * block + high * (2 * blocks - 1 - 4 * block)

    def pack_x(turn, field):
        edge_x[turn, 0] = field[:, rows - 2 : rows, :]
        edge_x[turn, 1] = field[:, 0:2, :]

    def pack_y(turn, layer):
        low = jnp.zeros((rows, LANES), jnp.float32)
        high = jnp.zeros((rows, LANES), jnp.float32)
        for z in range(depth):
            here = lane // 2 == z
            last = layer(z)[:, cols - LANES :]
            first = layer(z)[:, :LANES]
            low = jnp.where(here, pltpu.roll(last, (2 * z + 2) % LANES, 1), low)
            high = jnp.where(here, pltpu.roll(first, 2 * z, 1) if z else first, high)
        edge_y[turn, 0] = low
        edge_y[turn, 1] = high

    def halo_copies(turn):
        copies = []
        for side, step in ((0, 1), (1, -1)):
            copies.append(
                remote(
                    edge_x.at[turn, side],
                    halo_x.at[turn, side],
                    edge_sem.at[turn, side],
                    halo_sem.at[turn, side],
                    {"strike": ring(my_s, step, strike_count)},
                )
            )
            copies.append(
                remote(
                    edge_y.at[turn, side],
                    halo_y.at[turn, side],
                    edge_sem.at[turn, side + 2],
                    halo_sem.at[turn, side + 2],
                    {"dip": ring(my_d, step, dip_count)},
                )
            )
        return copies

    def start_halos(turn):
        copies = halo_copies(turn)
        for copy in copies:
            copy.start()
        return copies

    def wait_halos(copies):
        for copy in copies:
            copy.wait_recv()

    def fill_padded(turn, field, first=0, last=depth):
        at = slice(first, last)
        padded[at, SUBLANES : SUBLANES + rows, :] = field[at]
        padded[at, SUBLANES - 2 : SUBLANES, :] = halo_x[turn, 0, at]
        padded[at, SUBLANES + rows : SUBLANES + rows + 2, :] = halo_x[turn, 1, at]

    def diff_x(z):
        def window(offset):
            return padded[z, SUBLANES + offset : SUBLANES + offset + rows, :]

        return coef_near * (window(1) - window(-1)) + coef_far * (window(2) - window(-2))

    def diff_y(turn, z, field):
        low = halo_y[turn, 0]
        high = halo_y[turn, 1]
        low_0, low_1 = low[:, 2 * z : 2 * z + 1], low[:, 2 * z + 1 : 2 * z + 2]
        high_0, high_1 = high[:, 2 * z : 2 * z + 1], high[:, 2 * z + 1 : 2 * z + 2]
        back_1 = jnp.where(column == 0, low_1, pltpu.roll(field, 1, 1))
        back_2 = jnp.where(
            column == 0, low_0, jnp.where(column == 1, low_1, pltpu.roll(field, 2, 1))
        )
        next_1 = jnp.where(column == cols - 1, high_0, pltpu.roll(field, cols - 1, 1))
        next_2 = jnp.where(
            column == cols - 2,
            high_0,
            jnp.where(column == cols - 1, high_1, pltpu.roll(field, cols - 2, 1)),
        )
        return coef_near * (next_1 - back_1) + coef_far * (next_2 - back_2)

    def diff_z(z, layer, ghost):
        def at(index):
            if index < 0:
                return ghost
            return layer(index) if index < depth else None

        total = None
        for offset, coef in ((1, coef_near), (-1, -coef_near), (2, coef_far), (-2, -coef_far)):
            value = at(z + offset)
            if value is not None:
                total = coef * value if total is None else total + coef * value
        return total

    def velocity_layer(turn, z, source, stress_ref, traction):
        divergence = (
            diff_x(z)
            + diff_y(turn, z, stress_ref[1, z])
            + diff_z(z, lambda i: stress_ref[2, i], traction)
        )
        vel[z] = source[z] + courant * buoy[z] * divergence

    def stress_z_layer(z, stress_ref):
        return stress_ref[2, z] + courant * shear[z] * diff_z(z, lambda i: vel[i], None)

    def stress_layers(turn, stress_ref):
        fill_padded(turn, vel)
        for z in range(depth):
            modulus = courant * shear[z]
            stress[0, z] = stress_ref[0, z] + modulus * diff_x(z)
            stress[1, z] = stress_ref[1, z] + modulus * diff_y(turn, z, vel[z])
            stress[2, z] = stress_z_layer(z, stress_ref)

    def start_near(kind, field):
        copies = []
        for side, step in ((0, 1), (1, -1)):
            row = 0 if side else rows - SUBLANES
            col = 0 if side else cols - LANES
            copies.append(
                remote(
                    field.at[pl.ds(1, 2), pl.ds(row, SUBLANES), :],
                    near_x.at[kind, side],
                    n_send.at[kind, side],
                    n_recv.at[kind, side],
                    {"strike": ring(my_s, step, strike_count)},
                )
            )
            copies.append(
                remote(
                    field.at[pl.ds(1, 2), :, pl.ds(col, LANES)],
                    near_y.at[kind, side],
                    n_send.at[kind, side + 2],
                    n_recv.at[kind, side + 2],
                    {"dip": ring(my_d, step, dip_count)},
                )
            )
        for copy in copies:
            copy.start()
        return copies

    def slope(field, axis):
        size = field.shape[axis]

        def at(offset):
            return pltpu.roll(field, -offset % size, axis)

        return coef_near * (at(1) - at(-1)) + coef_far * (at(2) - at(-2))

    def early_trial(traction):
        normal = [
            stress_in[2, z] + courant * shear[z] * diff_z(z, lambda i: vel[i], None)
            for z in range(min(5, depth))
        ]
        ahead = [None]
        zero = jnp.zeros((SUBLANES - 2, cols), jnp.float32)

        def widened(kind, field, z, axis):
            near = (near_x, near_y)[axis]
            return jnp.concatenate([near[kind, 0, z - 1], field[z], near[kind, 1, z - 1]], axis=axis)

        for z in (1, 2):
            face = jnp.concatenate(
                [zero, halo_x[0, 0, z], stress_in[0, z], halo_x[0, 1, z], zero], axis=0
            )
            face = face + courant * widened(0, shear, z, 0) * slope(widened(1, vel, z, 0), 0)
            total = slope(face, 0)[SUBLANES : SUBLANES + rows]
            face = jnp.concatenate(
                [
                    pltpu.roll(halo_y[0, 0], LANES - 2 - 2 * z, 1),
                    stress_in[1, z],
                    pltpu.roll(halo_y[0, 1], LANES - 2 * z, 1),
                ],
                axis=1,
            )
            face = face + courant * widened(0, shear, z, 1) * slope(widened(1, vel, z, 1), 1)
            total = total + slope(face, 1)[:, LANES : LANES + cols]
            total = total + diff_z(z, lambda i: normal[i], traction)
            ahead.append(vel[z] + courant * buoy[z] * total)
        return prestress[...] + (
            normal[0] + courant * shear[0] * diff_z(0, lambda i: ahead[i], None)
        )

    def start_gather(turn, value):
        shared[turn] = value
        gathered[turn, my_d] = value
        copies = []
        for k in range(1, dip_count):
            copy = remote(
                shared.at[turn],
                gathered.at[turn, my_d],
                g_send.at[turn, k],
                g_recv.at[turn, k],
                {"dip": ring(my_d, k, dip_count)},
            )
            copy.start()
            copies.append(copy)
        return copies

    def wait_gather(turn):
        for k in range(1, dip_count):
            source = ring(my_d, -k, dip_count)
            remote(
                shared.at[turn],
                gathered.at[turn, source],
                g_send.at[turn, k],
                g_recv.at[turn, k],
                {"dip": source},
            ).wait_recv()

    def start_b():
        recv_b[my_s] = send_f[1, slot(my_block)]
        copies = []
        for k in range(1, strike_count):
            target = ring(my_s, k, strike_count)
            copy = remote(
                send_f.at[1, slot(target * dip_count + my_d)],
                recv_b.at[my_s],
                b_send.at[k],
                b_recv.at[k],
                {"strike": target},
            )
            copy.start()
            copies.append(copy)
        return copies

    def wait_b():
        for k in range(1, strike_count):
            source_s = ring(my_s, -k, strike_count)
            remote(
                send_f.at[1, source_s],
                recv_b.at[source_s],
                b_send.at[k],
                b_recv.at[k],
                {"strike": source_s},
            ).wait_recv()

    offsets = [
        (i, k) for k in reversed(range(dip_count)) for i in reversed(range(strike_count)) if i or k
    ]

    def start_a():
        recv_a[my_d, my_s] = send_f[0, slot(my_block)]
        copies = []
        for i, k in offsets:
            target_s, target_d = ring(my_s, i, strike_count), ring(my_d, k, dip_count)
            copy = remote(
                send_f.at[0, slot(target_s * dip_count + target_d)],
                recv_a.at[my_d, my_s],
                a_send.at[k, i],
                a_recv.at[k, i],
                {"strike": target_s, "dip": target_d},
            )
            copy.start()
            copies.append(copy)
        return copies

    def wait_a():
        for i, k in reversed(offsets):
            source_s, source_d = ring(my_s, -i, strike_count), ring(my_d, -k, dip_count)
            remote(
                send_f.at[0, source_s],
                recv_a.at[source_d, source_s],
                a_send.at[k, i],
                a_recv.at[k, i],
                {"strike": source_s, "dip": source_d},
            ).wait_recv()

    def exchange_copies(turn):
        other = blocks - 1 - my_block
        single = 1 - jnp.minimum(lax.rem(my_block, blocks // 2), 1)
        mirror = lax.rem(blocks - my_block + single * (blocks // 2), blocks)
        upper_rows = pl.ds(modes // 2, modes // 2)
        return [
            remote(
                modal.at[turn, 0, :, upper_rows, :],
                modal.at[turn, 1, :, upper_rows, :],
                x_send.at[turn, 0],
                x_recv.at[turn, 0],
                {"strike": other // dip_count, "dip": lax.rem(other, dip_count)},
            ),
            remote(
                nought.at[turn],
                nought_in.at[turn],
                x_send.at[turn, 1],
                x_recv.at[turn, 1],
                {"strike": mirror // dip_count, "dip": lax.rem(mirror, dip_count)},
            ),
        ]

    def start_exchange(turn):
        copies = exchange_copies(turn)
        for copy in copies:
            copy.start()
        return copies

    def arrange(turn, copies):
        for copy in copies:
            copy.wait_recv()
        modal[turn, 1, :, modes : modes + 1, :] = nought_in[turn]
        for k0 in range(dip_count):
            for m in range(half):
                at = dip_count * m + k0
                plus = modal[turn, upper, :, pl.ds(modes // 2 * upper + at, 1), :]
                minus = modal[turn, 1 - upper, :, pl.ds(modes - modes // 2 * upper - at, 1), :]
                for side, value in enumerate((plus, minus)):
                    weight[turn, side, k0, m : m + 1, :] = value[0]
                    weight[turn, side, k0, half + m : half + m + 1, :] = value[0]
                    source[turn, side, k0, m : m + 1, :] = value[1]
                    source[turn, side, k0, half + m : half + m + 1, :] = value[2]

    def start_c(step):
        back[step][slot(my_block)] = send_c[step, my_s]
        copies = []
        for i, k in offsets:
            target_s, target_d = ring(my_s, i, strike_count), ring(my_d, k, dip_count)
            copy = remote(
                send_c.at[step, target_s],
                back[step].at[slot(my_block)],
                c_send.at[step, k, i],
                c_recv.at[step, k, i],
                {"strike": target_s, "dip": target_d},
            )
            copy.start()
            copies.append(copy)
        return copies

    def wait_c(step):
        for i, k in reversed(offsets):
            source_s, source_d = ring(my_s, -i, strike_count), ring(my_d, -k, dip_count)
            remote(
                send_c.at[step, source_s],
                back[step].at[slot(source_s * dip_count + source_d)],
                c_send.at[step, k, i],
                c_recv.at[step, k, i],
                {"strike": source_s, "dip": source_d},
            ).wait_recv()

    def turned(i, part, k0):
        return twiddle[i, part, k0 : k0 + 1, :]

    def dip_forward(step, parts):
        real, imag = (
            jnp.concatenate(
                [
                    total_of([(part, turned(i, kind, k0)) for i, part in parts])
                    for k0 in range(dip_count)
                ],
                axis=0,
            )
            for kind in range(2)
        )
        both = jnp.concatenate(
            [
                jnp.concatenate([real, imag], axis=1),
                jnp.concatenate([imag, -real], axis=1),
            ],
            axis=0,
        )
        out = dot3_nt(dip_hi[...], dip_lo[...], both)
        last = pltpu.roll(out[front_modes : front_modes + SUBLANES], wave, 1)
        first = jnp.where(
            jnp.logical_and(layer_row == 0, strip == dip_count), last, out[:SUBLANES]
        )
        out = jnp.concatenate([first, out[SUBLANES:front_modes]], axis=0)
        send_f[step] = out.reshape(blocks, half, LANES)

    def strike_forward(pieces):
        stacks = [None] * dip_count
        for s, piece in enumerate(pieces):
            pair = jnp.concatenate([piece, pltpu.roll(piece, wave, 1)], axis=0)
            for k0 in range(dip_count):
                shift = rows * (s - k0) % LANES
                moved = pltpu.roll(pair, shift, 1) if shift else pair
                stacks[k0] = moved if s == 0 else jnp.where(strip == s, moved, stacks[k0])
        both = dot3(jnp.concatenate(stacks, axis=0), strike_hi[...], strike_lo[...])
        plus, minus = [], []
        for k0 in range(dip_count):
            tile = both[k0 * SUBLANES : (k0 + 1) * SUBLANES]
            cos, sin = tile[:, :total_x], tile[:, total_x:]
            crossed = swap(sin)
            ahead = cos + sign * crossed
            behind = sign * cos - crossed
            if k0 == 0:
                ahead = jnp.where(lone, jnp.where(real_half, cos, -crossed), ahead)
                behind = jnp.where(lone, jnp.where(real_half, swap(cos), -sin), behind)
            plus.append(ahead)
            minus.append(behind)
        return plus, minus

    def convolve(step, spectra):
        sums = []
        for side in range(2):
            tiles = []
            for k0 in range(dip_count):
                total = source[step, side, k0]
                for offset, item in enumerate(spectra):
                    total = total + weight[offset, side, k0] * item[side][k0]
                tiles.append(total)
            sums.append(tiles)
        return sums

    def strike_inverse(step, plus, minus):
        tiles = []
        for k0, (ahead, behind) in enumerate(zip(plus, minus)):
            direct = ahead + sign * behind
            crossed = -sign * swap(ahead - sign * behind)
            if k0 == 0:
                direct = jnp.where(lone, jnp.where(real_half, ahead, swap(behind)), direct)
                crossed = jnp.where(lone, -jnp.where(real_half, swap(ahead), behind), crossed)
            tiles.append(jnp.concatenate([direct, crossed], axis=1))
        out = dot3_rows(jnp.concatenate(tiles, axis=0), strike_hi[...], strike_lo[...])
        for s in range(strike_count):
            block = None
            for k0 in range(dip_count):
                shift = rows * (k0 - s) % LANES
                tile = out[k0 * SUBLANES : (k0 + 1) * SUBLANES]
                moved = pltpu.roll(tile, shift, 1) if shift else tile
                block = moved if k0 == 0 else jnp.where(strip == k0, moved, block)
            block = jnp.where(strip < dip_count, block, swap(pltpu.roll(block, wave, 1)))
            send_c[step, s] = block[:half]

    def dip_inverse(places):
        return dip_inverse_lines(back[0], dip_hi, dip_lo, twiddle, places)

    def store_history():
        zero = jnp.zeros((2, modes, total_x), jnp.float32)
        common = stored_count - STEPS + 1

        def term(t, j):
            return kern[j + t + 1].astype(jnp.float32)[None] * hist[j]

        def add(j, sums):
            return tuple(total + term(t, j) for t, total in enumerate(sums))

        sums = lax.fori_loop(0, common, add, (zero,) * STEPS)
        for t in range(STEPS):
            total = sums[t]
            for j in range(common, stored_count - t):
                total = total + term(t, j)
            values = (kern[t].astype(jnp.float32), total[0], total[1])
            for i, value in enumerate(values):
                modal[t, 0, i, 0:modes, :] = value
                nought[t, i] = value[0:1]

    def bound_of(slip):
        weaken = jnp.maximum(0.0, 1.0 - jnp.abs(slip) / crit_slip[...])
        strength = normal_stress[...] * (
            dynamic_friction + (static_friction - dynamic_friction) * weaken
        )
        return jnp.where(flags[...] == 1, strength, HUGE)

    def slide(trial, bound, slip):
        traction = jnp.clip(trial, -bound, bound)
        return traction, slip + time_step * ((trial - traction) / damping)

    barrier = pltpu.get_barrier_semaphore()
    for k in range(1, strike_count):
        pl.semaphore_signal(
            barrier, inc=1, device_id={"strike": ring(my_s, k, strike_count)}, device_id_type=MESH
        )
    for k in range(1, dip_count):
        pl.semaphore_signal(
            barrier, inc=1, device_id={"dip": ring(my_d, k, dip_count)}, device_id_type=MESH
        )
    loads = [
        pltpu.make_async_copy(sources[i], loaded[i], load_sem.at[i]) for i in range(INPUTS)
    ]
    loads[1].start()
    for i in range(INPUTS):
        if i != 1:
            loads[i].start()
    loads[1].wait()
    pack_x(0, stress_in.at[0])
    pack_y(0, lambda z: stress_in[1, z])
    pl.semaphore_wait(barrier, strike_count + dip_count - 2)

    started = []
    halos = start_halos(0)
    started += halos
    for k in range(1, dip_count):
        pl.semaphore_signal(
            plane_sem, inc=1, device_id={"dip": ring(my_d, k, dip_count)}, device_id_type=MESH
        )
    for i in range(INPUTS):
        if i != 1:
            loads[i].wait()
    near = start_near(0, shear)
    started += near
    store_history()
    pl.semaphore_wait(plane_sem, dip_count - 1)
    exchanged = start_exchange(0)
    started += exchanged

    ghost = traction_in[...]
    front = min(3, depth)
    base = prestress[...] + functional_in[...]
    bound = bound_of(slip_in[...])
    wait_halos(halos)
    fill_padded(0, stress_in.at[0], 1, front)
    for z in range(1, front):
        velocity_layer(0, z, vel_in, stress_in, ghost)
    wide = start_near(1, vel)
    traction, slip = slide(base + stress_z_layer(0, stress_in), bound, slip_in[...])
    dip_forward(0, [(my_d, slip)])
    started += start_a()
    started += start_gather(0, bound_of(slip))
    fill_padded(0, stress_in.at[0], 0, 1)
    fill_padded(0, stress_in.at[0], front, depth)
    for z in (0, *range(front, depth)):
        velocity_layer(0, z, vel_in, stress_in, ghost)
    pack_x(1, vel)
    pack_y(1, lambda z: vel[z])
    halos = start_halos(1)
    started += halos
    late = start_exchange(1)
    started += late
    wait_halos(near + wide)
    started += start_gather(1, early_trial(traction))
    arrange(0, exchanged)
    wait_a()
    pieces = []
    for s in range(strike_count):
        piece = recv_a[0, s]
        for i in range(1, dip_count):
            piece = piece + recv_a[i, s]
        pieces.append(piece)
    spectra = [strike_forward(pieces)]
    strike_inverse(0, *convolve(0, spectra))
    started += start_c(0)

    wait_halos(halos)
    stress_layers(1, stress_in)
    pack_x(2, stress.at[0])
    pack_y(2, lambda z: stress[1, z])
    halos = start_halos(2)
    started += halos
    arrange(1, late)
    for turn in range(2):
        wait_gather(turn)
    wait_c(0)
    changes = []
    for i, value in enumerate(dip_inverse(range(dip_count))):
        trial = gathered[1, i] + value
        bound = gathered[0, i]
        clipped = jnp.clip(trial, -bound, bound)
        change = time_step * ((trial - clipped) / damping)
        lines_out[0, i] = change
        lines_out[1, i] = clipped
        changes.append((i, change))
    dip_forward(1, changes)
    started += start_b()
    results[2][...] = slip + lines_out[0, my_d]
    results[3][...] = lines_out[1, my_d]
    wait_halos(halos)
    fill_padded(2, stress.at[0])
    for copy in wide:
        copy.wait_send()
    for z in range(depth):
        velocity_layer(2, z, vel, stress, traction)
    pack_x(3, vel)
    pack_y(3, lambda z: vel[z])
    halos = start_halos(3)
    started += halos
    wait_b()
    change = strike_forward([recv_b[s] for s in range(strike_count)])
    latest = [[old + new for old, new in zip(*pair)] for pair in zip(spectra[0], change)]
    spectra = [latest] + spectra
    strike_inverse(1, *convolve(1, spectra))
    started += start_c(1)
    wait_halos(halos)
    stress_layers(3, stress)
    for copy in started:
        copy.wait_send()
    wait_c(1)


def last_kernel(*refs):
    sources, results, field, sems = refs[:8], refs[8:13], refs[13], refs[14]
    saves = [pltpu.make_async_copy(sources[i], results[i], sems.at[i]) for i in range(4)]
    for save in saves:
        save.start()
    field[...] = dip_inverse_lines(*sources[4:], [lax.axis_index("dip")])[0]
    saves.append(pltpu.make_async_copy(field, results[4], sems.at[4]))
    saves[4].start()
    for save in saves:
        save.wait()


def fits_kernel(strike_count, dip_count, depth, rows, cols, modes, total_x):
    return (
        STEPS == 2
        and depth > 2
        and strike_count > 1
        and dip_count > 1
        and modes == dip_count * SUBLANES
        and rows % SUBLANES == 0
        and cols == 2 * LANES
        and total_x == LANES
        and 2 * dip_count * rows == LANES
        and strike_count * dip_count * SUBLANES == cols
    )


def body(*args):
    velocity, history = args[0], args[11]
    strike_count = lax.axis_size("strike")
    dip_count = lax.axis_size("dip")
    depth, rows, cols = velocity.shape
    modes, total_x = history.shape[2:]
    if not fits_kernel(strike_count, dip_count, depth, rows, cols, modes, total_x):
        return general_body(*args)
    half = SUBLANES // 2
    blocks = strike_count * dip_count
    total_y = cols * dip_count
    tables = (
        *split_table(dip_table(cols, total_y)),
        *split_table(strike_table(total_x)),
        twiddle_table(dip_count, cols, total_y),
    )
    turns = 2 * STEPS
    f32 = jnp.float32
    dma = pltpu.SemaphoreType.DMA
    operands = (*args, *[jnp.asarray(table) for table in tables])
    shapes = (velocity.shape, args[1].shape) + ((rows, cols),) * 3
    outs = tuple(jax.ShapeDtypeStruct(shape, f32) for shape in shapes)
    held = tuple(pltpu.VMEM(shape, f32) for shape in shapes[:4])
    held += (pltpu.VMEM((blocks, half, LANES), f32),)
    held += tuple(pltpu.VMEM(operands[i].shape, operands[i].dtype) for i in PASSED)
    scratch = [
        pltpu.VMEM(operand.shape, operand.dtype)
        for i, operand in enumerate(operands)
        if i not in PASSED
    ] + [
        pltpu.VMEM((depth, rows + 2 * SUBLANES, cols), f32),
        pltpu.VMEM((turns, 2, depth, 2, cols), f32),
        pltpu.VMEM((turns, 2, rows, LANES), f32),
        pltpu.VMEM((turns, 2, depth, 2, cols), f32),
        pltpu.VMEM((turns, 2, rows, LANES), f32),
        pltpu.VMEM((2, 2, 2, SUBLANES, cols), f32),
        pltpu.VMEM((2, 2, 2, rows, LANES), f32),
        pltpu.VMEM((2, rows, cols), f32),
        pltpu.VMEM((2, dip_count, rows, cols), f32),
        pltpu.VMEM((STEPS, blocks, half, LANES), f32),
        pltpu.VMEM((dip_count, strike_count, half, LANES), f32),
        pltpu.VMEM((strike_count, half, LANES), f32),
        pltpu.VMEM((2, dip_count, rows, cols), f32),
        pltpu.VMEM((STEPS, strike_count, half, LANES), f32),
        pltpu.VMEM((blocks, half, LANES), f32),
        pltpu.VMEM((STEPS, 2, 3, modes + SUBLANES, total_x), f32),
        pltpu.VMEM((STEPS, 3, 1, total_x), f32),
        pltpu.VMEM((STEPS, 3, 1, total_x), f32),
        pltpu.VMEM((STEPS, 2, dip_count, SUBLANES, total_x), f32),
        pltpu.VMEM((STEPS, 2, dip_count, SUBLANES, total_x), f32),
        dma((len(operands),)),
        dma((turns, 4)),
        dma((turns, 4)),
        dma((2, 4)),
        dma((2, 4)),
        dma((2, dip_count)),
        dma((2, dip_count)),
        dma((dip_count, strike_count)),
        dma((dip_count, strike_count)),
        dma((strike_count,)),
        dma((strike_count,)),
        dma((STEPS, dip_count, strike_count)),
        dma((STEPS, dip_count, strike_count)),
        dma((STEPS, 2)),
        dma((STEPS, 2)),
        pltpu.SemaphoreType.REGULAR,
    ]
    anywhere = pl.BlockSpec(memory_space=pl.ANY)
    results = pl.pallas_call(
        functools.partial(rupture_kernel, strike_count, dip_count),
        out_shape=held,
        in_specs=[pl.BlockSpec(memory_space=pltpu.HBM)] * len(operands),
        out_specs=(pl.BlockSpec(memory_space=pltpu.VMEM),) * len(held),
        scratch_shapes=scratch,
        compiler_params=pltpu.CompilerParams(
            collective_id=0, has_side_effects=True, vmem_limit_bytes=KERNEL_VMEM
        ),
    )(*operands)
    return pl.pallas_call(
        last_kernel,
        out_shape=outs,
        in_specs=[pl.BlockSpec(memory_space=pltpu.VMEM)] * len(held),
        out_specs=(anywhere,) * len(outs),
        scratch_shapes=[pltpu.VMEM((rows, cols), f32), dma((len(outs),))],
        compiler_params=pltpu.CompilerParams(vmem_limit_bytes=2**23),
    )(*results)


def solution(mesh):
    return jax.shard_map(
        body,
        mesh=mesh,
        in_specs=(
            P(None, "strike", "dip"),
            P(None, None, "strike", "dip"),
            P(None, "strike", "dip"),
            P(None, "strike", "dip"),
            P("strike", "dip"),
            P("strike", "dip"),
            P("strike", "dip"),
            P("strike", "dip"),
            P("strike", "dip"),
            P("strike", "dip"),
            P("strike", "dip"),
            P(None, None, ("strike", "dip"), None),
            P(None, ("strike", "dip"), None),
        ),
        out_specs=(
            P(None, "strike", "dip"),
            P(None, None, "strike", "dip"),
            P("strike", "dip"),
            P("strike", "dip"),
            P("strike", "dip"),
        ),
        check_vma=False,
    )
```

```python
import functools
import math

import jax
import jax.numpy as jnp
import numpy as np
from jax import lax
from jax.experimental import pallas as pl
from jax.experimental.pallas import tpu as pltpu
from jax.sharding import PartitionSpec as P

STEPS = 2


coef_near = 2.0 / 3.0
coef_far = -1.0 / 12.0
courant = 0.3
static_friction = 0.677
dynamic_friction = 0.525
damping = 0.5
time_step = 0.3


def padded_2(block, sides, width):
    for axis, dim in sides:
        count = lax.axis_size(axis)
        forward = [(i, i + 1) for i in range(count - 1)]
        forward.append((count - 1, 0))
        backward = [(target, source) for source, target in forward]
        low = lax.ppermute(
            lax.slice_in_dim(block, block.shape[dim] - width, None, axis=dim), axis, forward
        )
        high = lax.ppermute(lax.slice_in_dim(block, 0, width, axis=dim), axis, backward)
        block = jnp.concatenate([low, block, high], axis=dim)
    return block


def central(padded, axis, start, count):

    def window(offset):
        return lax.slice_in_dim(padded, start + offset, start + offset + count, axis=axis)

    return coef_near * (window(1) - window(-1)) + coef_far * (window(2) - window(-2))


def normal_diff(field, ghost):
    zeros = jnp.zeros_like(ghost)
    padded = jnp.concatenate([ghost, ghost, field, zeros, zeros], axis=0)
    return central(padded, 0, 2, field.shape[0])


def fault_update(prestress, normal_stress, crit_slip, flags, slip, stress_z, functional):
    trial = prestress + stress_z[0] + functional
    weaken = jnp.maximum(0.0, 1.0 - jnp.abs(slip) / crit_slip)
    strength = normal_stress * (dynamic_friction + (static_friction - dynamic_friction) * weaken)
    clipped = jnp.clip(trial, -strength, strength)
    traction = jnp.where(flags == 1, clipped, trial)
    rate = (trial - traction) / damping
    return (traction, slip + time_step * rate)


def factor_pair(length):
    first = 1
    candidate = 1
    while candidate * candidate <= length:
        if length % candidate == 0:
            first = candidate
        candidate += 1
    return (first, length // first)


def phase_table(count_a, count_b, length, sign):
    product = lax.iota(jnp.int32, count_a)[:, None] * lax.iota(jnp.int32, count_b)[None, :] % length
    angles = sign * 2.0 * math.pi / length * product.astype(jnp.float32)
    return (jnp.cos(angles), jnp.sin(angles))


def contract(form, left, right):
    return jnp.einsum(form, left, right, precision=lax.Precision.HIGHEST)


def transform_last(real_part, imag_part, sign):
    length = real_part.shape[-1]
    outer, inner = factor_pair(length)
    leading = real_part.shape[:-1]
    real_part = real_part.reshape(leading + (outer, inner))
    imag_part = imag_part.reshape(leading + (outer, inner))
    first_cos, first_sin = phase_table(outer, outer, outer, sign)
    middle_real = contract("kt,...tq->...kq", first_cos, real_part) - contract(
        "kt,...tq->...kq", first_sin, imag_part
    )
    middle_imag = contract("kt,...tq->...kq", first_cos, imag_part) + contract(
        "kt,...tq->...kq", first_sin, real_part
    )
    twist_cos, twist_sin = phase_table(outer, inner, length, sign)
    middle_real, middle_imag = (
        middle_real * twist_cos - middle_imag * twist_sin,
        middle_real * twist_sin + middle_imag * twist_cos,
    )
    second_cos, second_sin = phase_table(inner, inner, inner, sign)
    out_real = contract("...kt,tm->...km", middle_real, second_cos) - contract(
        "...kt,tm->...km", middle_imag, second_sin
    )
    out_imag = contract("...kt,tm->...km", middle_real, second_sin) + contract(
        "...kt,tm->...km", middle_imag, second_cos
    )
    scale = 1.0 / math.sqrt(length)
    out_real = jnp.swapaxes(out_real, -1, -2).reshape(leading + (length,)) * scale
    out_imag = jnp.swapaxes(out_imag, -1, -2).reshape(leading + (length,)) * scale
    return (out_real, out_imag)


def general_body(
    velocity,
    stress,
    shear_modulus,
    buoyancy,
    prestress,
    normal_stress,
    crit_slip,
    slip,
    traction,
    functional,
    flags,
    history,
    kernel,
):
    strike_count = lax.axis_size("strike")
    dip_count = lax.axis_size("dip")
    depth, rows_x, cols_y = velocity.shape
    ky_local = history.shape[2]
    total_x = history.shape[3]
    total_y = cols_y * dip_count
    line_rows = rows_x // dip_count
    stress_x, stress_y, stress_z = (stress[0], stress[1], stress[2])
    ghost_zero = jnp.zeros((1, rows_x, cols_y), jnp.float32)
    spectra = []
    for iteration in range(STEPS):
        padded_x = padded_2(stress_x, (("strike", 1),), 2)
        padded_y = padded_2(stress_y, (("dip", 2),), 2)
        divergence = (
            central(padded_x, 1, 2, rows_x)
            + central(padded_y, 2, 2, cols_y)
            + normal_diff(stress_z, traction[None])
        )
        velocity = velocity + courant * buoyancy * divergence
        padded_v = padded_2(velocity, (("strike", 1), ("dip", 2)), 2)
        grad_x = central(padded_v[:, :, 2 : cols_y + 2], 1, 2, rows_x)
        grad_y = central(padded_v[:, 2 : rows_x + 2, :], 2, 2, cols_y)
        stress_x = stress_x + courant * shear_modulus * grad_x
        stress_y = stress_y + courant * shear_modulus * grad_y
        stress_z = stress_z + courant * shear_modulus * normal_diff(velocity, ghost_zero)
        traction, slip = fault_update(
            prestress, normal_stress, crit_slip, flags, slip, stress_z, functional
        )
        lines = lax.all_to_all(slip, "dip", split_axis=0, concat_axis=1, tiled=True)
        part_real, part_imag = transform_last(lines, jnp.zeros_like(lines), -1.0)
        stacked = jnp.stack([part_real, part_imag]).reshape(
            2, line_rows, strike_count, dip_count, ky_local
        )
        stacked = stacked.transpose(0, 2, 3, 4, 1).reshape(
            2, strike_count, dip_count, ky_local, 1, 1, line_rows
        )
        halfway = lax.all_to_all(stacked, "strike", split_axis=1, concat_axis=4, tiled=True)
        owned = lax.all_to_all(halfway, "dip", split_axis=2, concat_axis=5, tiled=True)
        owned = owned.reshape(2, ky_local, total_x)
        spec_real, spec_imag = transform_last(owned[0], owned[1], -1.0)
        spectra = [(spec_real, spec_imag)] + spectra
        weights = kernel[iteration + 1 :].astype(jnp.float32)
        stored = jnp.sum(weights[:, None] * history[: history.shape[0] - iteration], axis=0)
        sum_real = stored[0]
        sum_imag = stored[1]
        for offset, item in enumerate(spectra):
            weight = kernel[offset].astype(jnp.float32)
            sum_real = sum_real + weight * item[0]
            sum_imag = sum_imag + weight * item[1]
        back_real, back_imag = transform_last(sum_real, sum_imag, 1.0)
        leaving = jnp.stack([back_real, back_imag]).reshape(
            2, 1, 1, ky_local, strike_count, dip_count, line_rows
        )
        partway = lax.all_to_all(leaving, "strike", split_axis=4, concat_axis=1, tiled=True)
        returned = lax.all_to_all(partway, "dip", split_axis=5, concat_axis=2, tiled=True)
        returned = returned.reshape(2, total_y, line_rows).transpose(0, 2, 1)
        field_real, field_imag = transform_last(returned[0], returned[1], 1.0)
        functional = lax.all_to_all(field_real, "dip", split_axis=1, concat_axis=0, tiled=True)
    return (velocity, jnp.stack([stress_x, stress_y, stress_z]), slip, traction, functional)


LANES = 128
SUBLANES = 8
MESH = pl.DeviceIdType.MESH
INPUTS = 18
PASSED = (13, 14, 17)
KERNEL_VMEM = 67043328 - 1500000
HUGE = float(np.finfo(np.float32).max)


def split_bf16(value):
    high = value.astype(jnp.bfloat16)
    return high, (value - high.astype(jnp.float32)).astype(jnp.bfloat16)


def split_table(table):
    table = np.asarray(table, np.float32)
    high = table.astype(jnp.bfloat16)
    return high, (table - high.astype(np.float32)).astype(jnp.bfloat16)


def strike_table(total_x):
    index = np.arange(total_x)
    angle = 2.0 * np.pi / total_x * (index[:, None] * index[None, :] % total_x)
    return np.concatenate([np.cos(angle), np.sin(angle)], axis=1) / np.sqrt(total_x)


def dip_table(strike_count, dip_count, cols, total_y):
    half = SUBLANES // 2
    blocks = strike_count * dip_count
    block = np.arange(strike_count)[None, :] * dip_count + np.arange(dip_count)[:, None]
    mirrored = SUBLANES * (blocks - 1 - block) + half
    start = np.where(block < blocks // 2, SUBLANES * block, mirrored)
    modes = (start[..., None] + np.arange(half)).reshape(-1)
    modes = np.concatenate([modes, cols // 2 + np.arange(2 * SUBLANES)])
    angle = 2.0 * np.pi / cols * (modes[:, None] * np.arange(cols)[None, :] % cols)
    return np.concatenate([np.cos(angle), np.sin(angle)], axis=1) / np.sqrt(total_y)


def twiddle_table(dip_count, cols, total_y):
    place = np.arange(total_y).reshape(dip_count, 1, cols)
    freq = np.arange(dip_count)[None, :, None]
    angle = 2.0 * np.pi / total_y * (freq * place % total_y)
    return np.stack([np.cos(angle), -np.sin(angle)], axis=1).astype(np.float32)


def dot3(left, right_high, right_low):
    high, low = split_bf16(left)
    rows = left.shape[0]
    both = jnp.dot(
        jnp.concatenate([high, low], axis=0), right_high, preferred_element_type=jnp.float32
    )
    return both[:rows] + both[rows:] + jnp.dot(high, right_low, preferred_element_type=jnp.float32)


def dot3_nt(left_high, left_low, right):
    high, low = split_bf16(right)

    def product(a, b):
        return lax.dot_general(a, b, (((1,), (1,)), ((), ())), preferred_element_type=jnp.float32)

    return product(left_high, high) + product(left_high, low) + product(left_low, high)


def dot3_rows(left, right_high, right_low):
    high, low = split_bf16(left)
    rows = left.shape[0]

    def product(a, b):
        return lax.dot_general(a, b, (((1,), (1,)), ((), ())), preferred_element_type=jnp.float32)

    both = product(jnp.concatenate([high, low], axis=0), right_high)
    return both[:rows] + both[rows:] + product(high, right_low)


def total_of(terms):
    total = None
    for left, right in terms:
        total = left * right if total is None else total + left * right
    return total


def dip_inverse_lines(back, dip_hi, dip_lo, twiddle, places):
    dip_count, _, _, cols = twiddle.shape
    count = cols // 2
    wave = LANES // 2
    rows = wave // dip_count
    lines = back[...].reshape(count, LANES).T
    out = dot3(lines, dip_hi[:count], dip_lo[:count])
    real = out[:wave, :cols] - out[wave:, cols:]
    imag = out[:wave, cols:] + out[wave:, :cols]
    scale = 1.0 / math.sqrt(cols * dip_count)
    column = lax.broadcasted_iota(jnp.int32, (rows, cols), 1)
    last = lines[wave : wave + rows, 0:1] * jnp.where(column % 2 == 0, scale, -scale)
    result = []
    for i in places:
        terms = [(real[:rows] + last, twiddle[i, 0, 0:1, :])]
        for k0 in range(1, dip_count):
            at = slice(k0 * rows, (k0 + 1) * rows)
            terms.append((real[at], twiddle[i, 0, k0 : k0 + 1, :]))
            terms.append((imag[at], twiddle[i, 1, k0 : k0 + 1, :]))
        result.append(total_of(terms))
    return result


def rupture_kernel(strike_count, dip_count, *refs):
    sources, refs = refs[:INPUTS], refs[INPUTS:]
    results, refs = refs[:8], refs[8:]
    loaded, refs = list(refs[: INPUTS - 3]), refs[INPUTS - 3 :]
    for place, result in zip(PASSED, results[5:]):
        loaded.insert(place, result)
    (
        vel_in, stress_in, shear, buoy, prestress, normal_stress, crit_slip, slip_in, traction_in,
        functional_in, flags, hist, kern, dip_hi, dip_lo, strike_hi, strike_lo, twiddle,
    ) = loaded
    (
        padded, edge_x, edge_y, halo_x, halo_y, near_x, near_y,
        shared, gathered, send_f, recv_a, recv_b, lines_out,
        send_c, recv_c, modal, nought, nought_in, weight, source,
        load_sem, edge_sem, halo_sem, n_send, n_recv, g_send, g_recv,
        a_send, a_recv, b_send, b_recv, c_send, c_recv, x_send, x_recv, plane_sem,
    ) = refs
    vel, stress = results[:2]
    back = (recv_c, results[4])
    depth, rows, cols = vel_in.shape
    modes = hist.shape[2]
    total_x = hist.shape[3]
    stored_count = hist.shape[0]
    blocks = strike_count * dip_count
    half = modes // dip_count // 2
    wave = dip_count * rows
    front_modes = cols // 2
    my_s = lax.axis_index("strike")
    my_d = lax.axis_index("dip")
    my_block = my_s * dip_count + my_d
    upper = my_block // (blocks // 2)

    def ring(me, offset, count):
        return lax.rem(me + offset + count, count)

    def remote(src, dst, send_sem, recv_sem, target):
        return pltpu.make_async_remote_copy(
            src_ref=src,
            dst_ref=dst,
            send_sem=send_sem,
            recv_sem=recv_sem,
            device_id=target,
            device_id_type=MESH,
        )

    lane = lax.broadcasted_iota(jnp.int32, (rows, LANES), 1)
    column = lax.broadcasted_iota(jnp.int32, (rows, cols), 1)
    strip = lax.broadcasted_iota(jnp.int32, (SUBLANES, LANES), 1) // rows
    layer_row = lax.broadcasted_iota(jnp.int32, (SUBLANES, LANES), 0)
    real_half = layer_row < half
    sign = jnp.where(real_half, 1.0, -1.0)
    lone = jnp.logical_and(layer_row % half == 0, my_block == 0)
    swap = functools.partial(pltpu.roll, shift=half, axis=0)

    def slot(place_s, place_d):
        return place_d * strike_count + place_s

    def pack_x(turn, field):
        edge_x[turn, 0] = field[:, rows - 2 : rows, :]
        edge_x[turn, 1] = field[:, 0:2, :]

    def pack_y(turn, layer):
        low = jnp.zeros((rows, LANES), jnp.float32)
        high = jnp.zeros((rows, LANES), jnp.float32)
        for z in range(depth):
            here = lane // 2 == z
            last = layer(z)[:, cols - LANES :]
            first = layer(z)[:, :LANES]
            low = jnp.where(here, pltpu.roll(last, (2 * z + 2) % LANES, 1), low)
            high = jnp.where(here, pltpu.roll(first, 2 * z, 1) if z else first, high)
        edge_y[turn, 0] = low
        edge_y[turn, 1] = high

    def halo_copies(turn):
        copies = []
        for side, step in ((0, 1), (1, -1)):
            copies.append(
                remote(
                    edge_x.at[turn, side],
                    halo_x.at[turn, side],
                    edge_sem.at[turn, side],
                    halo_sem.at[turn, side],
                    {"strike": ring(my_s, step, strike_count)},
                )
            )
            copies.append(
                remote(
                    edge_y.at[turn, side],
                    halo_y.at[turn, side],
                    edge_sem.at[turn, side + 2],
                    halo_sem.at[turn, side + 2],
                    {"dip": ring(my_d, step, dip_count)},
                )
            )
        return copies

    def start_halos(turn):
        copies = halo_copies(turn)
        for copy in copies:
            copy.start()
        return copies

    def wait_halos(copies):
        for copy in copies:
            copy.wait_recv()

    def fill_padded(turn, field, first=0, last=depth):
        at = slice(first, last)
        padded[at, SUBLANES : SUBLANES + rows, :] = field[at]
        padded[at, SUBLANES - 2 : SUBLANES, :] = halo_x[turn, 0, at]
        padded[at, SUBLANES + rows : SUBLANES + rows + 2, :] = halo_x[turn, 1, at]

    def diff_x(z):
        def window(offset):
            return padded[z, SUBLANES + offset : SUBLANES + offset + rows, :]

        return coef_near * (window(1) - window(-1)) + coef_far * (window(2) - window(-2))

    def diff_y(turn, z, field):
        low = halo_y[turn, 0]
        high = halo_y[turn, 1]
        low_0, low_1 = low[:, 2 * z : 2 * z + 1], low[:, 2 * z + 1 : 2 * z + 2]
        high_0, high_1 = high[:, 2 * z : 2 * z + 1], high[:, 2 * z + 1 : 2 * z + 2]
        back_1 = jnp.where(column == 0, low_1, pltpu.roll(field, 1, 1))
        back_2 = jnp.where(
            column == 0, low_0, jnp.where(column == 1, low_1, pltpu.roll(field, 2, 1))
        )
        next_1 = jnp.where(column == cols - 1, high_0, pltpu.roll(field, cols - 1, 1))
        next_2 = jnp.where(
            column == cols - 2,
            high_0,
            jnp.where(column == cols - 1, high_1, pltpu.roll(field, cols - 2, 1)),
        )
        return coef_near * (next_1 - back_1) + coef_far * (next_2 - back_2)

    def diff_z(z, layer, ghost):
        def at(index):
            if index < 0:
                return ghost
            return layer(index) if index < depth else None

        total = None
        for offset, coef in ((1, coef_near), (-1, -coef_near), (2, coef_far), (-2, -coef_far)):
            value = at(z + offset)
            if value is not None:
                total = coef * value if total is None else total + coef * value
        return total

    def velocity_layer(turn, z, source, stress_ref, traction):
        divergence = (
            diff_x(z)
            + diff_y(turn, z, stress_ref[1, z])
            + diff_z(z, lambda i: stress_ref[2, i], traction)
        )
        vel[z] = source[z] + courant * buoy[z] * divergence

    def stress_z_layer(z, stress_ref):
        return stress_ref[2, z] + courant * shear[z] * diff_z(z, lambda i: vel[i], None)

    def stress_layers(turn, stress_ref):
        fill_padded(turn, vel)
        for z in range(depth):
            modulus = courant * shear[z]
            stress[0, z] = stress_ref[0, z] + modulus * diff_x(z)
            stress[1, z] = stress_ref[1, z] + modulus * diff_y(turn, z, vel[z])
            stress[2, z] = stress_z_layer(z, stress_ref)

    def start_near(kind, field):
        copies = []
        for side, step in ((0, 1), (1, -1)):
            row = 0 if side else rows - SUBLANES
            col = 0 if side else cols - LANES
            copies.append(
                remote(
                    field.at[pl.ds(1, 2), pl.ds(row, SUBLANES), :],
                    near_x.at[kind, side],
                    n_send.at[kind, side],
                    n_recv.at[kind, side],
                    {"strike": ring(my_s, step, strike_count)},
                )
            )
            copies.append(
                remote(
                    field.at[pl.ds(1, 2), :, pl.ds(col, LANES)],
                    near_y.at[kind, side],
                    n_send.at[kind, side + 2],
                    n_recv.at[kind, side + 2],
                    {"dip": ring(my_d, step, dip_count)},
                )
            )
        for copy in copies:
            copy.start()
        return copies

    def slope(field, axis):
        size = field.shape[axis]

        def at(offset):
            return pltpu.roll(field, -offset % size, axis)

        return coef_near * (at(1) - at(-1)) + coef_far * (at(2) - at(-2))

    def early_trial(traction):
        normal = [
            stress_in[2, z] + courant * shear[z] * diff_z(z, lambda i: vel[i], None)
            for z in range(min(5, depth))
        ]
        ahead = [None]
        zero = jnp.zeros((SUBLANES - 2, cols), jnp.float32)

        def widened(kind, field, z, axis):
            near = (near_x, near_y)[axis]
            return jnp.concatenate([near[kind, 0, z - 1], field[z], near[kind, 1, z - 1]], axis=axis)

        for z in (1, 2):
            face = jnp.concatenate(
                [zero, halo_x[0, 0, z], stress_in[0, z], halo_x[0, 1, z], zero], axis=0
            )
            face = face + courant * widened(0, shear, z, 0) * slope(widened(1, vel, z, 0), 0)
            total = slope(face, 0)[SUBLANES : SUBLANES + rows]
            face = jnp.concatenate(
                [
                    pltpu.roll(halo_y[0, 0], LANES - 2 - 2 * z, 1),
                    stress_in[1, z],
                    pltpu.roll(halo_y[0, 1], LANES - 2 * z, 1),
                ],
                axis=1,
            )
            face = face + courant * widened(0, shear, z, 1) * slope(widened(1, vel, z, 1), 1)
            total = total + slope(face, 1)[:, LANES : LANES + cols]
            total = total + diff_z(z, lambda i: normal[i], traction)
            ahead.append(vel[z] + courant * buoy[z] * total)
        return prestress[...] + (
            normal[0] + courant * shear[0] * diff_z(0, lambda i: ahead[i], None)
        )

    def start_gather(turn, value):
        shared[turn] = value
        gathered[turn, my_d] = value
        copies = []
        for k in range(1, dip_count):
            copy = remote(
                shared.at[turn],
                gathered.at[turn, my_d],
                g_send.at[turn, k],
                g_recv.at[turn, k],
                {"dip": ring(my_d, k, dip_count)},
            )
            copy.start()
            copies.append(copy)
        return copies

    def wait_gather(turn):
        for k in range(1, dip_count):
            source = ring(my_d, -k, dip_count)
            remote(
                shared.at[turn],
                gathered.at[turn, source],
                g_send.at[turn, k],
                g_recv.at[turn, k],
                {"dip": source},
            ).wait_recv()

    def start_b():
        recv_b[my_s] = send_f[1, slot(my_s, my_d)]
        copies = []
        for k in range(1, strike_count):
            target = ring(my_s, k, strike_count)
            copy = remote(
                send_f.at[1, slot(target, my_d)],
                recv_b.at[my_s],
                b_send.at[k],
                b_recv.at[0],
                {"strike": target},
            )
            copy.start()
            copies.append(copy)
        return copies

    offsets = [
        (i, k) for k in reversed(range(dip_count)) for i in reversed(range(strike_count)) if i or k
    ]

    def start_a():
        recv_a[slot(my_s, my_d)] = send_f[0, slot(my_s, my_d)]
        copies = []
        for i, k in offsets:
            target_s, target_d = ring(my_s, i, strike_count), ring(my_d, k, dip_count)
            copy = remote(
                send_f.at[0, slot(target_s, target_d)],
                recv_a.at[slot(my_s, my_d)],
                a_send.at[k, i],
                a_recv.at[0],
                {"strike": target_s, "dip": target_d},
            )
            copy.start()
            copies.append(copy)
        return copies

    def wait_all(landed, sem):
        others = landed.at[pl.ds(0, landed.shape[0] - 1)]
        pltpu.make_async_copy(others, others, sem).wait()

    def exchange_copies(turn):
        other = blocks - 1 - my_block
        single = 1 - jnp.minimum(lax.rem(my_block, blocks // 2), 1)
        mirror = lax.rem(blocks - my_block + single * (blocks // 2), blocks)
        upper_rows = pl.ds(modes // 2, modes // 2)
        return [
            remote(
                modal.at[turn, 0, :, upper_rows, :],
                modal.at[turn, 1, :, upper_rows, :],
                x_send.at[turn, 0],
                x_recv.at[turn, 0],
                {"strike": other // dip_count, "dip": lax.rem(other, dip_count)},
            ),
            remote(
                nought.at[turn],
                nought_in.at[turn],
                x_send.at[turn, 1],
                x_recv.at[turn, 1],
                {"strike": mirror // dip_count, "dip": lax.rem(mirror, dip_count)},
            ),
        ]

    def start_exchange(turn):
        copies = exchange_copies(turn)
        for copy in copies:
            copy.start()
        return copies

    def arrange(turn, copies):
        for copy in copies:
            copy.wait_recv()
        modal[turn, 1, :, modes : modes + 1, :] = nought_in[turn]
        for k0 in range(dip_count):
            for m in range(half):
                at = dip_count * m + k0
                plus = modal[turn, upper, :, pl.ds(modes // 2 * upper + at, 1), :]
                minus = modal[turn, 1 - upper, :, pl.ds(modes - modes // 2 * upper - at, 1), :]
                for side, value in enumerate((plus, minus)):
                    weight[turn, side, k0, m : m + 1, :] = value[0]
                    weight[turn, side, k0, half + m : half + m + 1, :] = value[0]
                    source[turn, side, k0, m : m + 1, :] = value[1]
                    source[turn, side, k0, half + m : half + m + 1, :] = value[2]

    def start_c(step):
        back[step][slot(my_s, my_d)] = send_c[step, my_s]
        copies = []
        for i, k in offsets:
            target_s, target_d = ring(my_s, i, strike_count), ring(my_d, k, dip_count)
            copy = remote(
                send_c.at[step, target_s],
                back[step].at[slot(my_s, my_d)],
                c_send.at[step, k, i],
                c_recv.at[step],
                {"strike": target_s, "dip": target_d},
            )
            copy.start()
            copies.append(copy)
        return copies

    def turned(i, part, k0):
        return twiddle[i, part, k0 : k0 + 1, :]

    def dip_forward(step, parts):
        real, imag = (
            jnp.concatenate(
                [
                    total_of([(part, turned(i, kind, k0)) for i, part in parts])
                    for k0 in range(dip_count)
                ],
                axis=0,
            )
            for kind in range(2)
        )
        both = jnp.concatenate(
            [
                jnp.concatenate([real, imag], axis=1),
                jnp.concatenate([imag, -real], axis=1),
            ],
            axis=0,
        )
        lone_row = jnp.logical_and(layer_row == 0, strip == dip_count)
        if step == 0:
            count, first = front_modes, 0
            tables = (dip_hi[...], dip_lo[...])
        else:
            count = strike_count * half
            first = my_d * strike_count
            at = pl.ds(pl.multiple_of(my_d * count, count), count)
            lone_row = jnp.logical_and(lone_row, my_d == 0)
            tables = [
                jnp.concatenate([table[at, :], table[front_modes:, :]], axis=0)
                for table in (dip_hi, dip_lo)
            ]
        out = dot3_nt(*tables, both)
        last = pltpu.roll(out[count : count + SUBLANES], wave, 1)
        head = jnp.where(lone_row, last, out[:SUBLANES])
        out = jnp.concatenate([head, out[SUBLANES:count]], axis=0)
        send_f[step, pl.ds(first, count // half)] = out.reshape(count // half, half, LANES)

    def strike_forward(pieces):
        stacks = [None] * dip_count
        for s, piece in enumerate(pieces):
            pair = jnp.concatenate([piece, pltpu.roll(piece, wave, 1)], axis=0)
            for k0 in range(dip_count):
                shift = rows * (s - k0) % LANES
                moved = pltpu.roll(pair, shift, 1) if shift else pair
                stacks[k0] = moved if s == 0 else jnp.where(strip == s, moved, stacks[k0])
        both = dot3(jnp.concatenate(stacks, axis=0), strike_hi[...], strike_lo[...])
        plus, minus = [], []
        for k0 in range(dip_count):
            tile = both[k0 * SUBLANES : (k0 + 1) * SUBLANES]
            cos, sin = tile[:, :total_x], tile[:, total_x:]
            crossed = swap(sin)
            ahead = cos + sign * crossed
            behind = sign * cos - crossed
            if k0 == 0:
                ahead = jnp.where(lone, jnp.where(real_half, cos, -crossed), ahead)
                behind = jnp.where(lone, jnp.where(real_half, swap(cos), -sin), behind)
            plus.append(ahead)
            minus.append(behind)
        return plus, minus

    def convolve(step, spectra):
        sums = []
        for side in range(2):
            tiles = []
            for k0 in range(dip_count):
                total = source[step, side, k0]
                for offset, item in enumerate(spectra):
                    total = total + weight[offset, side, k0] * item[side][k0]
                tiles.append(total)
            sums.append(tiles)
        return sums

    def strike_inverse(step, plus, minus):
        tiles = []
        for k0, (ahead, behind) in enumerate(zip(plus, minus)):
            direct = ahead + sign * behind
            crossed = -sign * swap(ahead - sign * behind)
            if k0 == 0:
                direct = jnp.where(lone, jnp.where(real_half, ahead, swap(behind)), direct)
                crossed = jnp.where(lone, -jnp.where(real_half, swap(ahead), behind), crossed)
            tiles.append(jnp.concatenate([direct, crossed], axis=1))
        out = dot3_rows(jnp.concatenate(tiles, axis=0), strike_hi[...], strike_lo[...])
        for s in range(strike_count):
            block = None
            for k0 in range(dip_count):
                shift = rows * (k0 - s) % LANES
                tile = out[k0 * SUBLANES : (k0 + 1) * SUBLANES]
                moved = pltpu.roll(tile, shift, 1) if shift else tile
                block = moved if k0 == 0 else jnp.where(strip == k0, moved, block)
            block = jnp.where(strip < dip_count, block, swap(pltpu.roll(block, wave, 1)))
            send_c[step, s] = block[:half]

    def dip_inverse(places):
        return dip_inverse_lines(back[0], dip_hi, dip_lo, twiddle, places)

    def store_history():
        zero = jnp.zeros((2, modes, total_x), jnp.float32)
        common = stored_count - STEPS + 1

        def term(t, j):
            return kern[j + t + 1].astype(jnp.float32)[None] * hist[j]

        def add(j, sums):
            return tuple(total + term(t, j) for t, total in enumerate(sums))

        sums = lax.fori_loop(0, common, add, (zero,) * STEPS)
        for t in range(STEPS):
            total = sums[t]
            for j in range(common, stored_count - t):
                total = total + term(t, j)
            values = (kern[t].astype(jnp.float32), total[0], total[1])
            for i, value in enumerate(values):
                modal[t, 0, i, 0:modes, :] = value
                nought[t, i] = value[0:1]

    def bound_of(slip):
        weaken = jnp.maximum(0.0, 1.0 - jnp.abs(slip) / crit_slip[...])
        strength = normal_stress[...] * (
            dynamic_friction + (static_friction - dynamic_friction) * weaken
        )
        return jnp.where(flags[...] == 1, strength, HUGE)

    def slide(trial, bound, slip):
        traction = jnp.clip(trial, -bound, bound)
        return traction, slip + time_step * ((trial - traction) / damping)

    barrier = pltpu.get_barrier_semaphore()
    for k in range(1, strike_count):
        pl.semaphore_signal(
            barrier, inc=1, device_id={"strike": ring(my_s, k, strike_count)}, device_id_type=MESH
        )
    for k in range(1, dip_count):
        pl.semaphore_signal(
            barrier, inc=1, device_id={"dip": ring(my_d, k, dip_count)}, device_id_type=MESH
        )
    loads = [
        pltpu.make_async_copy(sources[i], loaded[i], load_sem.at[i]) for i in range(INPUTS)
    ]
    loads[1].start()
    for i in range(INPUTS):
        if i != 1:
            loads[i].start()
    loads[1].wait()
    pack_x(0, stress_in.at[0])
    pack_y(0, lambda z: stress_in[1, z])
    pl.semaphore_wait(barrier, strike_count + dip_count - 2)

    started = []
    halos = start_halos(0)
    started += halos
    for k in range(1, dip_count):
        pl.semaphore_signal(
            plane_sem, inc=1, device_id={"dip": ring(my_d, k, dip_count)}, device_id_type=MESH
        )
    for i in range(INPUTS):
        if i != 1:
            loads[i].wait()
    near = start_near(0, shear)
    started += near
    store_history()
    pl.semaphore_wait(plane_sem, dip_count - 1)
    exchanged = start_exchange(0)
    started += exchanged

    ghost = traction_in[...]
    front = min(3, depth)
    base = prestress[...] + functional_in[...]
    bound = bound_of(slip_in[...])
    padded[1:front, SUBLANES : SUBLANES + rows, :] = stress_in[0, 1:front]
    pushed = [
        diff_z(z, lambda i: stress_in[2, i], ghost) for z in range(1, front)
    ]
    rigid = courant * shear[0]
    wait_halos(halos)
    for z in range(1, front):
        padded[z, SUBLANES - 2 : SUBLANES, :] = halo_x[0, 0, z]
        padded[z, SUBLANES + rows : SUBLANES + rows + 2, :] = halo_x[0, 1, z]
    for z in range(1, front):
        divergence = diff_x(z) + diff_y(0, z, stress_in[1, z]) + pushed[z - 1]
        vel[z] = vel_in[z] + courant * buoy[z] * divergence
    wide = start_near(1, vel)
    lifted = stress_in[2, 0] + rigid * diff_z(0, lambda i: vel[i], None)
    traction, slip = slide(base + lifted, bound, slip_in[...])
    dip_forward(0, [(my_d, slip)])
    started += start_a()
    started += start_gather(0, bound_of(slip))
    fill_padded(0, stress_in.at[0], 0, 1)
    fill_padded(0, stress_in.at[0], front, depth)
    for z in (0, *range(front, depth)):
        velocity_layer(0, z, vel_in, stress_in, ghost)
    pack_x(1, vel)
    pack_y(1, lambda z: vel[z])
    halos = start_halos(1)
    started += halos
    late = start_exchange(1)
    started += late
    wait_halos(near + wide)
    started += start_gather(1, early_trial(traction))
    arrange(0, exchanged)
    wait_all(recv_a, a_recv.at[0])
    pieces = []
    for s in range(strike_count):
        piece = recv_a[slot(s, 0)]
        for i in range(1, dip_count):
            piece = piece + recv_a[slot(s, i)]
        pieces.append(piece)
    spectra = [strike_forward(pieces)]
    strike_inverse(0, *convolve(0, spectra))
    started += start_c(0)

    wait_halos(halos)
    stress_layers(1, stress_in)
    pack_x(2, stress.at[0])
    pack_y(2, lambda z: stress[1, z])
    halos = start_halos(2)
    started += halos
    arrange(1, late)
    for turn in range(2):
        wait_gather(turn)
    wait_all(back[0], c_recv.at[0])
    changes = []
    for i, value in enumerate(dip_inverse(range(dip_count))):
        trial = gathered[1, i] + value
        bound = gathered[0, i]
        clipped = jnp.clip(trial, -bound, bound)
        change = time_step * ((trial - clipped) / damping)
        lines_out[0, i] = change
        lines_out[1, i] = clipped
        changes.append((i, change))
    dip_forward(1, changes)
    started += start_b()
    results[2][...] = slip + lines_out[0, my_d]
    results[3][...] = lines_out[1, my_d]
    wait_halos(halos)
    fill_padded(2, stress.at[0])
    for copy in wide:
        copy.wait_send()
    for z in range(depth):
        velocity_layer(2, z, vel, stress, traction)
    pack_x(3, vel)
    pack_y(3, lambda z: vel[z])
    halos = start_halos(3)
    started += halos
    wait_all(recv_b, b_recv.at[0])
    change = strike_forward([recv_b[s] for s in range(strike_count)])
    latest = [[old + new for old, new in zip(*pair)] for pair in zip(spectra[0], change)]
    spectra = [latest] + spectra
    strike_inverse(1, *convolve(1, spectra))
    started += start_c(1)
    wait_halos(halos)
    stress_layers(3, stress)
    for copy in started:
        copy.wait_send()
    wait_all(back[1], c_recv.at[1])


def last_kernel(*refs):
    sources, results, field, sems = refs[:8], refs[8:13], refs[13], refs[14]
    saves = [pltpu.make_async_copy(sources[i], results[i], sems.at[i]) for i in range(4)]
    for save in saves:
        save.start()
    field[...] = dip_inverse_lines(*sources[4:], [lax.axis_index("dip")])[0]
    saves.append(pltpu.make_async_copy(field, results[4], sems.at[4]))
    saves[4].start()
    for save in saves:
        save.wait()


def fits_kernel(strike_count, dip_count, depth, rows, cols, modes, total_x):
    return (
        STEPS == 2
        and depth > 2
        and strike_count > 1
        and dip_count > 1
        and modes == dip_count * SUBLANES
        and rows % SUBLANES == 0
        and cols == 2 * LANES
        and strike_count % 4 == 0
        and total_x == LANES
        and 2 * dip_count * rows == LANES
        and strike_count * dip_count * SUBLANES == cols
    )


def body(*args):
    velocity, history = args[0], args[11]
    strike_count = lax.axis_size("strike")
    dip_count = lax.axis_size("dip")
    depth, rows, cols = velocity.shape
    modes, total_x = history.shape[2:]
    if not fits_kernel(strike_count, dip_count, depth, rows, cols, modes, total_x):
        return general_body(*args)
    half = SUBLANES // 2
    blocks = strike_count * dip_count
    total_y = cols * dip_count
    tables = (
        *split_table(dip_table(strike_count, dip_count, cols, total_y)),
        *split_table(strike_table(total_x)),
        twiddle_table(dip_count, cols, total_y),
    )
    turns = 2 * STEPS
    f32 = jnp.float32
    dma = pltpu.SemaphoreType.DMA
    operands = (*args, *[jnp.asarray(table) for table in tables])
    shapes = (velocity.shape, args[1].shape) + ((rows, cols),) * 3
    outs = tuple(jax.ShapeDtypeStruct(shape, f32) for shape in shapes)
    held = tuple(pltpu.VMEM(shape, f32) for shape in shapes[:4])
    held += (pltpu.VMEM((blocks, half, LANES), f32),)
    held += tuple(pltpu.VMEM(operands[i].shape, operands[i].dtype) for i in PASSED)
    scratch = [
        pltpu.VMEM(operand.shape, operand.dtype)
        for i, operand in enumerate(operands)
        if i not in PASSED
    ] + [
        pltpu.VMEM((depth, rows + 2 * SUBLANES, cols), f32),
        pltpu.VMEM((turns, 2, depth, 2, cols), f32),
        pltpu.VMEM((turns, 2, rows, LANES), f32),
        pltpu.VMEM((turns, 2, depth, 2, cols), f32),
        pltpu.VMEM((turns, 2, rows, LANES), f32),
        pltpu.VMEM((2, 2, 2, SUBLANES, cols), f32),
        pltpu.VMEM((2, 2, 2, rows, LANES), f32),
        pltpu.VMEM((2, rows, cols), f32),
        pltpu.VMEM((2, dip_count, rows, cols), f32),
        pltpu.VMEM((STEPS, blocks, half, LANES), f32),
        pltpu.VMEM((blocks, half, LANES), f32),
        pltpu.VMEM((strike_count, half, LANES), f32),
        pltpu.VMEM((2, dip_count, rows, cols), f32),
        pltpu.VMEM((STEPS, strike_count, half, LANES), f32),
        pltpu.VMEM((blocks, half, LANES), f32),
        pltpu.VMEM((STEPS, 2, 3, modes + SUBLANES, total_x), f32),
        pltpu.VMEM((STEPS, 3, 1, total_x), f32),
        pltpu.VMEM((STEPS, 3, 1, total_x), f32),
        pltpu.VMEM((STEPS, 2, dip_count, SUBLANES, total_x), f32),
        pltpu.VMEM((STEPS, 2, dip_count, SUBLANES, total_x), f32),
        dma((len(operands),)),
        dma((turns, 4)),
        dma((turns, 4)),
        dma((2, 4)),
        dma((2, 4)),
        dma((2, dip_count)),
        dma((2, dip_count)),
        dma((dip_count, strike_count)),
        dma((1,)),
        dma((strike_count,)),
        dma((1,)),
        dma((STEPS, dip_count, strike_count)),
        dma((STEPS,)),
        dma((STEPS, 2)),
        dma((STEPS, 2)),
        pltpu.SemaphoreType.REGULAR,
    ]
    anywhere = pl.BlockSpec(memory_space=pl.ANY)
    results = pl.pallas_call(
        functools.partial(rupture_kernel, strike_count, dip_count),
        out_shape=held,
        in_specs=[pl.BlockSpec(memory_space=pltpu.HBM)] * len(operands),
        out_specs=(pl.BlockSpec(memory_space=pltpu.VMEM),) * len(held),
        scratch_shapes=scratch,
        compiler_params=pltpu.CompilerParams(
            collective_id=0, has_side_effects=True, vmem_limit_bytes=KERNEL_VMEM
        ),
    )(*operands)
    return pl.pallas_call(
        last_kernel,
        out_shape=outs,
        in_specs=[pl.BlockSpec(memory_space=pltpu.VMEM)] * len(held),
        out_specs=(anywhere,) * len(outs),
        scratch_shapes=[pltpu.VMEM((rows, cols), f32), dma((len(outs),))],
        compiler_params=pltpu.CompilerParams(vmem_limit_bytes=2**23),
    )(*results)


def solution(mesh):
    return jax.shard_map(
        body,
        mesh=mesh,
        in_specs=(
            P(None, "strike", "dip"),
            P(None, None, "strike", "dip"),
            P(None, "strike", "dip"),
            P(None, "strike", "dip"),
            P("strike", "dip"),
            P("strike", "dip"),
            P("strike", "dip"),
            P("strike", "dip"),
            P("strike", "dip"),
            P("strike", "dip"),
            P("strike", "dip"),
            P(None, None, ("strike", "dip"), None),
            P(None, ("strike", "dip"), None),
        ),
        out_specs=(
            P(None, "strike", "dip"),
            P(None, None, "strike", "dip"),
            P("strike", "dip"),
            P("strike", "dip"),
            P("strike", "dip"),
        ),
        check_vma=False,
    )
```

```python
import functools
import math

import jax
import jax.numpy as jnp
import numpy as np
from jax import lax
from jax.experimental import pallas as pl
from jax.experimental.pallas import tpu as pltpu
from jax.sharding import PartitionSpec as P

STEPS = 2


coef_near = 2.0 / 3.0
coef_far = -1.0 / 12.0
courant = 0.3
static_friction = 0.677
dynamic_friction = 0.525
damping = 0.5
time_step = 0.3


def padded_2(block, sides, width):
    for axis, dim in sides:
        count = lax.axis_size(axis)
        forward = [(i, i + 1) for i in range(count - 1)]
        forward.append((count - 1, 0))
        backward = [(target, source) for source, target in forward]
        low = lax.ppermute(
            lax.slice_in_dim(block, block.shape[dim] - width, None, axis=dim), axis, forward
        )
        high = lax.ppermute(lax.slice_in_dim(block, 0, width, axis=dim), axis, backward)
        block = jnp.concatenate([low, block, high], axis=dim)
    return block


def central(padded, axis, start, count):

    def window(offset):
        return lax.slice_in_dim(padded, start + offset, start + offset + count, axis=axis)

    return coef_near * (window(1) - window(-1)) + coef_far * (window(2) - window(-2))


def normal_diff(field, ghost):
    zeros = jnp.zeros_like(ghost)
    padded = jnp.concatenate([ghost, ghost, field, zeros, zeros], axis=0)
    return central(padded, 0, 2, field.shape[0])


def fault_update(prestress, normal_stress, crit_slip, flags, slip, stress_z, functional):
    trial = prestress + stress_z[0] + functional
    weaken = jnp.maximum(0.0, 1.0 - jnp.abs(slip) / crit_slip)
    strength = normal_stress * (dynamic_friction + (static_friction - dynamic_friction) * weaken)
    clipped = jnp.clip(trial, -strength, strength)
    traction = jnp.where(flags == 1, clipped, trial)
    rate = (trial - traction) / damping
    return (traction, slip + time_step * rate)


def factor_pair(length):
    first = 1
    candidate = 1
    while candidate * candidate <= length:
        if length % candidate == 0:
            first = candidate
        candidate += 1
    return (first, length // first)


def phase_table(count_a, count_b, length, sign):
    product = lax.iota(jnp.int32, count_a)[:, None] * lax.iota(jnp.int32, count_b)[None, :] % length
    angles = sign * 2.0 * math.pi / length * product.astype(jnp.float32)
    return (jnp.cos(angles), jnp.sin(angles))


def contract(form, left, right):
    return jnp.einsum(form, left, right, precision=lax.Precision.HIGHEST)


def transform_last(real_part, imag_part, sign):
    length = real_part.shape[-1]
    outer, inner = factor_pair(length)
    leading = real_part.shape[:-1]
    real_part = real_part.reshape(leading + (outer, inner))
    imag_part = imag_part.reshape(leading + (outer, inner))
    first_cos, first_sin = phase_table(outer, outer, outer, sign)
    middle_real = contract("kt,...tq->...kq", first_cos, real_part) - contract(
        "kt,...tq->...kq", first_sin, imag_part
    )
    middle_imag = contract("kt,...tq->...kq", first_cos, imag_part) + contract(
        "kt,...tq->...kq", first_sin, real_part
    )
    twist_cos, twist_sin = phase_table(outer, inner, length, sign)
    middle_real, middle_imag = (
        middle_real * twist_cos - middle_imag * twist_sin,
        middle_real * twist_sin + middle_imag * twist_cos,
    )
    second_cos, second_sin = phase_table(inner, inner, inner, sign)
    out_real = contract("...kt,tm->...km", middle_real, second_cos) - contract(
        "...kt,tm->...km", middle_imag, second_sin
    )
    out_imag = contract("...kt,tm->...km", middle_real, second_sin) + contract(
        "...kt,tm->...km", middle_imag, second_cos
    )
    scale = 1.0 / math.sqrt(length)
    out_real = jnp.swapaxes(out_real, -1, -2).reshape(leading + (length,)) * scale
    out_imag = jnp.swapaxes(out_imag, -1, -2).reshape(leading + (length,)) * scale
    return (out_real, out_imag)


def general_body(
    velocity,
    stress,
    shear_modulus,
    buoyancy,
    prestress,
    normal_stress,
    crit_slip,
    slip,
    traction,
    functional,
    flags,
    history,
    kernel,
):
    strike_count = lax.axis_size("strike")
    dip_count = lax.axis_size("dip")
    depth, rows_x, cols_y = velocity.shape
    ky_local = history.shape[2]
    total_x = history.shape[3]
    total_y = cols_y * dip_count
    line_rows = rows_x // dip_count
    stress_x, stress_y, stress_z = (stress[0], stress[1], stress[2])
    ghost_zero = jnp.zeros((1, rows_x, cols_y), jnp.float32)
    spectra = []
    for iteration in range(STEPS):
        padded_x = padded_2(stress_x, (("strike", 1),), 2)
        padded_y = padded_2(stress_y, (("dip", 2),), 2)
        divergence = (
            central(padded_x, 1, 2, rows_x)
            + central(padded_y, 2, 2, cols_y)
            + normal_diff(stress_z, traction[None])
        )
        velocity = velocity + courant * buoyancy * divergence
        padded_v = padded_2(velocity, (("strike", 1), ("dip", 2)), 2)
        grad_x = central(padded_v[:, :, 2 : cols_y + 2], 1, 2, rows_x)
        grad_y = central(padded_v[:, 2 : rows_x + 2, :], 2, 2, cols_y)
        stress_x = stress_x + courant * shear_modulus * grad_x
        stress_y = stress_y + courant * shear_modulus * grad_y
        stress_z = stress_z + courant * shear_modulus * normal_diff(velocity, ghost_zero)
        traction, slip = fault_update(
            prestress, normal_stress, crit_slip, flags, slip, stress_z, functional
        )
        lines = lax.all_to_all(slip, "dip", split_axis=0, concat_axis=1, tiled=True)
        part_real, part_imag = transform_last(lines, jnp.zeros_like(lines), -1.0)
        stacked = jnp.stack([part_real, part_imag]).reshape(
            2, line_rows, strike_count, dip_count, ky_local
        )
        stacked = stacked.transpose(0, 2, 3, 4, 1).reshape(
            2, strike_count, dip_count, ky_local, 1, 1, line_rows
        )
        halfway = lax.all_to_all(stacked, "strike", split_axis=1, concat_axis=4, tiled=True)
        owned = lax.all_to_all(halfway, "dip", split_axis=2, concat_axis=5, tiled=True)
        owned = owned.reshape(2, ky_local, total_x)
        spec_real, spec_imag = transform_last(owned[0], owned[1], -1.0)
        spectra = [(spec_real, spec_imag)] + spectra
        weights = kernel[iteration + 1 :].astype(jnp.float32)
        stored = jnp.sum(weights[:, None] * history[: history.shape[0] - iteration], axis=0)
        sum_real = stored[0]
        sum_imag = stored[1]
        for offset, item in enumerate(spectra):
            weight = kernel[offset].astype(jnp.float32)
            sum_real = sum_real + weight * item[0]
            sum_imag = sum_imag + weight * item[1]
        back_real, back_imag = transform_last(sum_real, sum_imag, 1.0)
        leaving = jnp.stack([back_real, back_imag]).reshape(
            2, 1, 1, ky_local, strike_count, dip_count, line_rows
        )
        partway = lax.all_to_all(leaving, "strike", split_axis=4, concat_axis=1, tiled=True)
        returned = lax.all_to_all(partway, "dip", split_axis=5, concat_axis=2, tiled=True)
        returned = returned.reshape(2, total_y, line_rows).transpose(0, 2, 1)
        field_real, field_imag = transform_last(returned[0], returned[1], 1.0)
        functional = lax.all_to_all(field_real, "dip", split_axis=1, concat_axis=0, tiled=True)
    return (velocity, jnp.stack([stress_x, stress_y, stress_z]), slip, traction, functional)


LANES = 128
SUBLANES = 8
MESH = pl.DeviceIdType.MESH
INPUTS = 18
PASSED = (13, 14, 17)
KERNEL_VMEM = 67043328 - 1500000
HUGE = float(np.finfo(np.float32).max)


def split_bf16(value):
    high = value.astype(jnp.bfloat16)
    return high, (value - high.astype(jnp.float32)).astype(jnp.bfloat16)


def split_table(table):
    table = np.asarray(table, np.float32)
    high = table.astype(jnp.bfloat16)
    return high, (table - high.astype(np.float32)).astype(jnp.bfloat16)


def strike_table(total_x):
    index = np.arange(total_x)
    angle = 2.0 * np.pi / total_x * (index[:, None] * index[None, :] % total_x)
    return np.concatenate([np.cos(angle), np.sin(angle)], axis=1) / np.sqrt(total_x)


def dip_table(strike_count, dip_count, cols, total_y):
    half = SUBLANES // 2
    blocks = strike_count * dip_count
    block = np.arange(strike_count)[None, :] * dip_count + np.arange(dip_count)[:, None]
    mirrored = SUBLANES * (blocks - 1 - block) + half
    start = np.where(block < blocks // 2, SUBLANES * block, mirrored)
    modes = (start[..., None] + np.arange(half)).reshape(-1)
    modes = np.concatenate([modes, cols // 2 + np.arange(2 * SUBLANES)])
    angle = 2.0 * np.pi / cols * (modes[:, None] * np.arange(cols)[None, :] % cols)
    return np.concatenate([np.cos(angle), np.sin(angle)], axis=1) / np.sqrt(total_y)


def twiddle_table(dip_count, cols, total_y):
    place = np.arange(total_y).reshape(dip_count, 1, cols)
    freq = np.arange(dip_count)[None, :, None]
    angle = 2.0 * np.pi / total_y * (freq * place % total_y)
    return np.stack([np.cos(angle), -np.sin(angle)], axis=1).astype(np.float32)


def dot3(left, right_high, right_low):
    high, low = split_bf16(left)
    rows = left.shape[0]
    both = jnp.dot(
        jnp.concatenate([high, low], axis=0), right_high, preferred_element_type=jnp.float32
    )
    return both[:rows] + both[rows:] + jnp.dot(high, right_low, preferred_element_type=jnp.float32)


def dot3_nt(left_high, left_low, right):
    high, low = split_bf16(right)

    def product(a, b):
        return lax.dot_general(a, b, (((1,), (1,)), ((), ())), preferred_element_type=jnp.float32)

    return product(left_high, high) + product(left_high, low) + product(left_low, high)


def dot3_rows(left, right_high, right_low):
    high, low = split_bf16(left)
    rows = left.shape[0]

    def product(a, b):
        return lax.dot_general(a, b, (((1,), (1,)), ((), ())), preferred_element_type=jnp.float32)

    both = product(jnp.concatenate([high, low], axis=0), right_high)
    return both[:rows] + both[rows:] + product(high, right_low)


def total_of(terms):
    total = None
    for left, right in terms:
        total = left * right if total is None else total + left * right
    return total


def dip_inverse_lines(back, dip_hi, dip_lo, twiddle, places):
    dip_count, _, _, cols = twiddle.shape
    count = cols // 2
    wave = LANES // 2
    rows = wave // dip_count
    lines = back[...].reshape(count, LANES).T
    out = dot3(lines, dip_hi[:count], dip_lo[:count])
    real = out[:wave, :cols] - out[wave:, cols:]
    imag = out[:wave, cols:] + out[wave:, :cols]
    scale = 1.0 / math.sqrt(cols * dip_count)
    column = lax.broadcasted_iota(jnp.int32, (rows, cols), 1)
    last = lines[wave : wave + rows, 0:1] * jnp.where(column % 2 == 0, scale, -scale)
    result = []
    for i in places:
        terms = [(real[:rows] + last, twiddle[i, 0, 0:1, :])]
        for k0 in range(1, dip_count):
            at = slice(k0 * rows, (k0 + 1) * rows)
            terms.append((real[at], twiddle[i, 0, k0 : k0 + 1, :]))
            terms.append((imag[at], twiddle[i, 1, k0 : k0 + 1, :]))
        result.append(total_of(terms))
    return result


def rupture_kernel(strike_count, dip_count, *refs):
    sources, refs = refs[:INPUTS], refs[INPUTS:]
    results, refs = refs[:8], refs[8:]
    loaded, refs = list(refs[: INPUTS - 3]), refs[INPUTS - 3 :]
    for place, result in zip(PASSED, results[5:]):
        loaded.insert(place, result)
    (
        vel_in, stress_in, shear, buoy, prestress, normal_stress, crit_slip, slip_in, traction_in,
        functional_in, flags, hist, kern, dip_hi, dip_lo, strike_hi, strike_lo, twiddle,
    ) = loaded
    (
        padded, edge_x, edge_y, halo_x, halo_y, near_x, near_y,
        shared, gathered, send_f, recv_a, recv_b, lines_out,
        send_c, recv_c, modal, nought, nought_in, weight, source,
        load_sem, edge_sem, halo_sem, n_send, n_recv, g_send, g_recv,
        a_send, a_recv, b_send, b_recv, c_send, c_recv, x_send, x_recv, plane_sem,
    ) = refs
    vel, stress = results[:2]
    back = (recv_c, results[4])
    depth, rows, cols = vel_in.shape
    modes = hist.shape[2]
    total_x = hist.shape[3]
    stored_count = hist.shape[0]
    blocks = strike_count * dip_count
    half = modes // dip_count // 2
    wave = dip_count * rows
    front_modes = cols // 2
    my_s = lax.axis_index("strike")
    my_d = lax.axis_index("dip")
    my_block = my_s * dip_count + my_d
    upper = my_block // (blocks // 2)

    strike_ring = [lax.rem(my_s + i, strike_count) for i in range(strike_count)]
    dip_ring = [lax.rem(my_d + i, dip_count) for i in range(dip_count)]

    def ring(me, offset, count):
        return (strike_ring if me is my_s else dip_ring)[offset % count]

    def remote(src, dst, send_sem, recv_sem, target):
        return pltpu.make_async_remote_copy(
            src_ref=src,
            dst_ref=dst,
            send_sem=send_sem,
            recv_sem=recv_sem,
            device_id=target,
            device_id_type=MESH,
        )

    lane = lax.broadcasted_iota(jnp.int32, (rows, LANES), 1)
    column = lax.broadcasted_iota(jnp.int32, (rows, cols), 1)
    strip = lax.broadcasted_iota(jnp.int32, (SUBLANES, LANES), 1) // rows
    layer_row = lax.broadcasted_iota(jnp.int32, (SUBLANES, LANES), 0)
    real_half = layer_row < half
    sign = jnp.where(real_half, 1.0, -1.0)
    lone = jnp.logical_and(layer_row % half == 0, my_block == 0)
    swap = functools.partial(pltpu.roll, shift=half, axis=0)

    def slot(place_s, place_d):
        return place_d * strike_count + place_s

    def pack_x(turn, field):
        edge_x[turn, 0] = field[:, rows - 2 : rows, :]
        edge_x[turn, 1] = field[:, 0:2, :]

    def pack_y(turn, layer):
        low = jnp.zeros((rows, LANES), jnp.float32)
        high = jnp.zeros((rows, LANES), jnp.float32)
        for z in range(depth):
            here = lane // 2 == z
            last = layer(z)[:, cols - LANES :]
            first = layer(z)[:, :LANES]
            low = jnp.where(here, pltpu.roll(last, (2 * z + 2) % LANES, 1), low)
            high = jnp.where(here, pltpu.roll(first, 2 * z, 1) if z else first, high)
        edge_y[turn, 0] = low
        edge_y[turn, 1] = high

    def halo_copies(turn):
        copies = []
        for side, step in ((0, 1), (1, -1)):
            copies.append(
                remote(
                    edge_x.at[turn, side],
                    halo_x.at[turn, side],
                    edge_sem.at[turn, side],
                    halo_sem.at[turn, side],
                    {"strike": ring(my_s, step, strike_count)},
                )
            )
            copies.append(
                remote(
                    edge_y.at[turn, side],
                    halo_y.at[turn, side],
                    edge_sem.at[turn, side + 2],
                    halo_sem.at[turn, side + 2],
                    {"dip": ring(my_d, step, dip_count)},
                )
            )
        return copies

    def start_halos(turn):
        copies = halo_copies(turn)
        for copy in copies:
            copy.start()
        return copies

    def wait_halos(copies):
        for copy in copies:
            copy.wait_recv()

    def fill_padded(turn, field, first=0, last=depth):
        at = slice(first, last)
        padded[at, SUBLANES : SUBLANES + rows, :] = field[at]
        padded[at, SUBLANES - 2 : SUBLANES, :] = halo_x[turn, 0, at]
        padded[at, SUBLANES + rows : SUBLANES + rows + 2, :] = halo_x[turn, 1, at]

    def diff_x(z):
        def window(offset):
            return padded[z, SUBLANES + offset : SUBLANES + offset + rows, :]

        return coef_near * (window(1) - window(-1)) + coef_far * (window(2) - window(-2))

    def diff_y(turn, z, field):
        low = halo_y[turn, 0]
        high = halo_y[turn, 1]
        low_0, low_1 = low[:, 2 * z : 2 * z + 1], low[:, 2 * z + 1 : 2 * z + 2]
        high_0, high_1 = high[:, 2 * z : 2 * z + 1], high[:, 2 * z + 1 : 2 * z + 2]
        back_1 = jnp.where(column == 0, low_1, pltpu.roll(field, 1, 1))
        back_2 = jnp.where(
            column == 0, low_0, jnp.where(column == 1, low_1, pltpu.roll(field, 2, 1))
        )
        next_1 = jnp.where(column == cols - 1, high_0, pltpu.roll(field, cols - 1, 1))
        next_2 = jnp.where(
            column == cols - 2,
            high_0,
            jnp.where(column == cols - 1, high_1, pltpu.roll(field, cols - 2, 1)),
        )
        return coef_near * (next_1 - back_1) + coef_far * (next_2 - back_2)

    def diff_z(z, layer, ghost):
        def at(index):
            if index < 0:
                return ghost
            return layer(index) if index < depth else None

        total = None
        for offset, coef in ((1, coef_near), (-1, -coef_near), (2, coef_far), (-2, -coef_far)):
            value = at(z + offset)
            if value is not None:
                total = coef * value if total is None else total + coef * value
        return total

    def velocity_layer(turn, z, source, stress_ref, traction):
        divergence = (
            diff_x(z)
            + diff_y(turn, z, stress_ref[1, z])
            + diff_z(z, lambda i: stress_ref[2, i], traction)
        )
        vel[z] = source[z] + courant * buoy[z] * divergence

    def stress_z_layer(z, stress_ref):
        return stress_ref[2, z] + courant * shear[z] * diff_z(z, lambda i: vel[i], None)

    def stress_layers(turn, stress_ref):
        fill_padded(turn, vel)
        for z in range(depth):
            modulus = courant * shear[z]
            stress[0, z] = stress_ref[0, z] + modulus * diff_x(z)
            stress[1, z] = stress_ref[1, z] + modulus * diff_y(turn, z, vel[z])
            stress[2, z] = stress_z_layer(z, stress_ref)

    def start_near(kind, field):
        copies = []
        for side, step in ((0, 1), (1, -1)):
            row = 0 if side else rows - SUBLANES
            col = 0 if side else cols - LANES
            copies.append(
                remote(
                    field.at[pl.ds(1, 2), pl.ds(row, SUBLANES), :],
                    near_x.at[kind, side],
                    n_send.at[kind, side],
                    n_recv.at[kind, side],
                    {"strike": ring(my_s, step, strike_count)},
                )
            )
            copies.append(
                remote(
                    field.at[pl.ds(1, 2), :, pl.ds(col, LANES)],
                    near_y.at[kind, side],
                    n_send.at[kind, side + 2],
                    n_recv.at[kind, side + 2],
                    {"dip": ring(my_d, step, dip_count)},
                )
            )
        for copy in copies:
            copy.start()
        return copies

    def slope(field, axis):
        size = field.shape[axis]

        def at(offset):
            return pltpu.roll(field, -offset % size, axis)

        return coef_near * (at(1) - at(-1)) + coef_far * (at(2) - at(-2))

    def early_trial(traction):
        normal = [
            stress_in[2, z] + courant * shear[z] * diff_z(z, lambda i: vel[i], None)
            for z in range(min(5, depth))
        ]
        ahead = [None]
        zero = jnp.zeros((SUBLANES - 2, cols), jnp.float32)

        def widened(kind, field, z, axis):
            near = (near_x, near_y)[axis]
            return jnp.concatenate([near[kind, 0, z - 1], field[z], near[kind, 1, z - 1]], axis=axis)

        for z in (1, 2):
            face = jnp.concatenate(
                [zero, halo_x[0, 0, z], stress_in[0, z], halo_x[0, 1, z], zero], axis=0
            )
            face = face + courant * widened(0, shear, z, 0) * slope(widened(1, vel, z, 0), 0)
            total = slope(face, 0)[SUBLANES : SUBLANES + rows]
            face = jnp.concatenate(
                [
                    pltpu.roll(halo_y[0, 0], LANES - 2 - 2 * z, 1),
                    stress_in[1, z],
                    pltpu.roll(halo_y[0, 1], LANES - 2 * z, 1),
                ],
                axis=1,
            )
            face = face + courant * widened(0, shear, z, 1) * slope(widened(1, vel, z, 1), 1)
            total = total + slope(face, 1)[:, LANES : LANES + cols]
            total = total + diff_z(z, lambda i: normal[i], traction)
            ahead.append(vel[z] + courant * buoy[z] * total)
        return prestress[...] + (
            normal[0] + courant * shear[0] * diff_z(0, lambda i: ahead[i], None)
        )

    def start_gather(turn, value):
        shared[turn] = value
        gathered[turn, my_d] = value
        copies = []
        for k in range(1, dip_count):
            copy = remote(
                shared.at[turn],
                gathered.at[turn, my_d],
                g_send.at[turn, k],
                g_recv.at[turn, k],
                {"dip": ring(my_d, k, dip_count)},
            )
            copy.start()
            copies.append(copy)
        return copies

    def wait_gather(turn):
        for k in range(1, dip_count):
            source = ring(my_d, -k, dip_count)
            remote(
                shared.at[turn],
                gathered.at[turn, source],
                g_send.at[turn, k],
                g_recv.at[turn, k],
                {"dip": source},
            ).wait_recv()

    def start_b():
        recv_b[my_s] = send_f[1, slot(my_s, my_d)]
        copies = []
        for k in range(1, strike_count):
            target = ring(my_s, k, strike_count)
            copy = remote(
                send_f.at[1, slot(target, my_d)],
                recv_b.at[my_s],
                b_send.at[0],
                b_recv.at[0],
                {"strike": target},
            )
            copy.start()
            copies.append(copy)
        return copies

    offsets = [
        (i, k) for k in reversed(range(dip_count)) for i in reversed(range(strike_count)) if i or k
    ]

    def start_a():
        recv_a[slot(my_s, my_d)] = send_f[0, slot(my_s, my_d)]
        copies = []
        for i, k in offsets:
            target_s, target_d = ring(my_s, i, strike_count), ring(my_d, k, dip_count)
            copy = remote(
                send_f.at[0, slot(target_s, target_d)],
                recv_a.at[slot(my_s, my_d)],
                a_send.at[0],
                a_recv.at[0],
                {"strike": target_s, "dip": target_d},
            )
            copy.start()
            copies.append(copy)
        return copies

    def wait_all(landed, sem):
        others = landed.at[pl.ds(0, landed.shape[0] - 1)]
        pltpu.make_async_copy(others, others, sem).wait()

    def exchange_copies(turn):
        other = blocks - 1 - my_block
        single = 1 - jnp.minimum(lax.rem(my_block, blocks // 2), 1)
        mirror = lax.rem(blocks - my_block + single * (blocks // 2), blocks)
        upper_rows = pl.ds(modes // 2, modes // 2)
        return [
            remote(
                modal.at[turn, 0, :, upper_rows, :],
                modal.at[turn, 1, :, upper_rows, :],
                x_send.at[turn, 0],
                x_recv.at[turn, 0],
                {"strike": other // dip_count, "dip": lax.rem(other, dip_count)},
            ),
            remote(
                nought.at[turn],
                nought_in.at[turn],
                x_send.at[turn, 1],
                x_recv.at[turn, 1],
                {"strike": mirror // dip_count, "dip": lax.rem(mirror, dip_count)},
            ),
        ]

    def start_exchange(turn):
        copies = exchange_copies(turn)
        for copy in copies:
            copy.start()
        return copies

    def arrange(turn, copies):
        for copy in copies:
            copy.wait_recv()
        modal[turn, 1, :, modes : modes + 1, :] = nought_in[turn]
        for k0 in range(dip_count):
            for m in range(half):
                at = dip_count * m + k0
                plus = modal[turn, upper, :, pl.ds(modes // 2 * upper + at, 1), :]
                minus = modal[turn, 1 - upper, :, pl.ds(modes - modes // 2 * upper - at, 1), :]
                for side, value in enumerate((plus, minus)):
                    weight[turn, side, k0, m : m + 1, :] = value[0]
                    weight[turn, side, k0, half + m : half + m + 1, :] = value[0]
                    source[turn, side, k0, m : m + 1, :] = value[1]
                    source[turn, side, k0, half + m : half + m + 1, :] = value[2]

    def start_c(step):
        back[step][slot(my_s, my_d)] = send_c[step, my_s]
        copies = []
        for i, k in offsets:
            target_s, target_d = ring(my_s, i, strike_count), ring(my_d, k, dip_count)
            copy = remote(
                send_c.at[step, target_s],
                back[step].at[slot(my_s, my_d)],
                c_send.at[step],
                c_recv.at[step],
                {"strike": target_s, "dip": target_d},
            )
            copy.start()
            copies.append(copy)
        return copies

    def turned(i, part, k0):
        return twiddle[i, part, k0 : k0 + 1, :]

    def dip_forward(step, parts):
        real, imag = (
            jnp.concatenate(
                [
                    total_of([(part, turned(i, kind, k0)) for i, part in parts])
                    for k0 in range(dip_count)
                ],
                axis=0,
            )
            for kind in range(2)
        )
        both = jnp.concatenate(
            [
                jnp.concatenate([real, imag], axis=1),
                jnp.concatenate([imag, -real], axis=1),
            ],
            axis=0,
        )
        lone_row = jnp.logical_and(layer_row == 0, strip == dip_count)
        if step == 0:
            count, first = front_modes, 0
            tables = (dip_hi[...], dip_lo[...])
        else:
            count = strike_count * half
            first = my_d * strike_count
            at = pl.ds(pl.multiple_of(my_d * count, count), count)
            lone_row = jnp.logical_and(lone_row, my_d == 0)
            tables = [
                jnp.concatenate([table[at, :], table[front_modes:, :]], axis=0)
                for table in (dip_hi, dip_lo)
            ]
        out = dot3_nt(*tables, both)
        last = pltpu.roll(out[count : count + SUBLANES], wave, 1)
        head = jnp.where(lone_row, last, out[:SUBLANES])
        out = jnp.concatenate([head, out[SUBLANES:count]], axis=0)
        send_f[step, pl.ds(first, count // half)] = out.reshape(count // half, half, LANES)

    def strike_forward(pieces):
        stacks = [None] * dip_count
        for s, piece in enumerate(pieces):
            pair = jnp.concatenate([piece, pltpu.roll(piece, wave, 1)], axis=0)
            for k0 in range(dip_count):
                shift = rows * (s - k0) % LANES
                moved = pltpu.roll(pair, shift, 1) if shift else pair
                stacks[k0] = moved if s == 0 else jnp.where(strip == s, moved, stacks[k0])
        both = dot3(jnp.concatenate(stacks, axis=0), strike_hi[...], strike_lo[...])
        plus, minus = [], []
        for k0 in range(dip_count):
            tile = both[k0 * SUBLANES : (k0 + 1) * SUBLANES]
            cos, sin = tile[:, :total_x], tile[:, total_x:]
            crossed = swap(sin)
            ahead = cos + sign * crossed
            behind = sign * cos - crossed
            if k0 == 0:
                ahead = jnp.where(lone, jnp.where(real_half, cos, -crossed), ahead)
                behind = jnp.where(lone, jnp.where(real_half, swap(cos), -sin), behind)
            plus.append(ahead)
            minus.append(behind)
        return plus, minus

    def convolve(step, spectra):
        sums = []
        for side in range(2):
            tiles = []
            for k0 in range(dip_count):
                total = source[step, side, k0]
                for offset, item in enumerate(spectra):
                    total = total + weight[offset, side, k0] * item[side][k0]
                tiles.append(total)
            sums.append(tiles)
        return sums

    def strike_inverse(step, plus, minus):
        tiles = []
        for k0, (ahead, behind) in enumerate(zip(plus, minus)):
            direct = ahead + sign * behind
            crossed = -sign * swap(ahead - sign * behind)
            if k0 == 0:
                direct = jnp.where(lone, jnp.where(real_half, ahead, swap(behind)), direct)
                crossed = jnp.where(lone, -jnp.where(real_half, swap(ahead), behind), crossed)
            tiles.append(jnp.concatenate([direct, crossed], axis=1))
        out = dot3_rows(jnp.concatenate(tiles, axis=0), strike_hi[...], strike_lo[...])
        for s in range(strike_count):
            block = None
            for k0 in range(dip_count):
                shift = rows * (k0 - s) % LANES
                tile = out[k0 * SUBLANES : (k0 + 1) * SUBLANES]
                moved = pltpu.roll(tile, shift, 1) if shift else tile
                block = moved if k0 == 0 else jnp.where(strip == k0, moved, block)
            block = jnp.where(strip < dip_count, block, swap(pltpu.roll(block, wave, 1)))
            send_c[step, s] = block[:half]

    def dip_inverse(places):
        return dip_inverse_lines(back[0], dip_hi, dip_lo, twiddle, places)

    def store_history():
        zero = jnp.zeros((2, modes, total_x), jnp.float32)
        common = stored_count - STEPS + 1

        def term(t, j):
            return kern[j + t + 1].astype(jnp.float32)[None] * hist[j]

        def add(j, sums):
            return tuple(total + term(t, j) for t, total in enumerate(sums))

        sums = lax.fori_loop(0, common, add, (zero,) * STEPS)
        for t in range(STEPS):
            total = sums[t]
            for j in range(common, stored_count - t):
                total = total + term(t, j)
            values = (kern[t].astype(jnp.float32), total[0], total[1])
            for i, value in enumerate(values):
                modal[t, 0, i, 0:modes, :] = value
                nought[t, i] = value[0:1]

    def bound_of(slip):
        weaken = jnp.maximum(0.0, 1.0 - jnp.abs(slip) / crit_slip[...])
        strength = normal_stress[...] * (
            dynamic_friction + (static_friction - dynamic_friction) * weaken
        )
        return jnp.where(flags[...] == 1, strength, HUGE)

    def slide(trial, bound, slip):
        traction = jnp.clip(trial, -bound, bound)
        return traction, slip + time_step * ((trial - traction) / damping)

    barrier = pltpu.get_barrier_semaphore()
    for k in range(1, strike_count):
        pl.semaphore_signal(
            barrier, inc=1, device_id={"strike": ring(my_s, k, strike_count)}, device_id_type=MESH
        )
    for k in range(1, dip_count):
        pl.semaphore_signal(
            barrier, inc=1, device_id={"dip": ring(my_d, k, dip_count)}, device_id_type=MESH
        )
    loads = [
        pltpu.make_async_copy(sources[i], loaded[i], load_sem.at[i]) for i in range(INPUTS)
    ]
    loads[1].start()
    for i in range(INPUTS):
        if i != 1:
            loads[i].start()
    loads[1].wait()
    pack_x(0, stress_in.at[0])
    pack_y(0, lambda z: stress_in[1, z])
    pl.semaphore_wait(barrier, strike_count + dip_count - 2)

    started = []
    halos = start_halos(0)
    started += halos
    for k in range(1, dip_count):
        pl.semaphore_signal(
            plane_sem, inc=1, device_id={"dip": ring(my_d, k, dip_count)}, device_id_type=MESH
        )
    for i in range(INPUTS):
        if i != 1:
            loads[i].wait()
    near = start_near(0, shear)
    started += near
    store_history()
    pl.semaphore_wait(plane_sem, dip_count - 1)
    exchanged = start_exchange(0)
    started += exchanged

    ghost = traction_in[...]
    front = min(3, depth)
    base = prestress[...] + functional_in[...]
    bound = bound_of(slip_in[...])
    padded[1:front, SUBLANES : SUBLANES + rows, :] = stress_in[0, 1:front]
    pushed = [
        diff_z(z, lambda i: stress_in[2, i], ghost) for z in range(1, front)
    ]
    rigid = courant * shear[0]
    wait_halos(halos)
    for z in range(1, front):
        padded[z, SUBLANES - 2 : SUBLANES, :] = halo_x[0, 0, z]
        padded[z, SUBLANES + rows : SUBLANES + rows + 2, :] = halo_x[0, 1, z]
    for z in range(1, front):
        divergence = diff_x(z) + diff_y(0, z, stress_in[1, z]) + pushed[z - 1]
        vel[z] = vel_in[z] + courant * buoy[z] * divergence
    wide = start_near(1, vel)
    lifted = stress_in[2, 0] + rigid * diff_z(0, lambda i: vel[i], None)
    traction, slip = slide(base + lifted, bound, slip_in[...])
    dip_forward(0, [(my_d, slip)])
    start_a()
    started += start_gather(0, bound_of(slip))
    fill_padded(0, stress_in.at[0], 0, 1)
    fill_padded(0, stress_in.at[0], front, depth)
    for z in (0, *range(front, depth)):
        velocity_layer(0, z, vel_in, stress_in, ghost)
    pack_x(1, vel)
    pack_y(1, lambda z: vel[z])
    halos = start_halos(1)
    started += halos
    late = start_exchange(1)
    started += late
    wait_halos(near + wide)
    started += start_gather(1, early_trial(traction))
    arrange(0, exchanged)
    wait_all(recv_a, a_recv.at[0])
    pieces = []
    for s in range(strike_count):
        piece = recv_a[slot(s, 0)]
        for i in range(1, dip_count):
            piece = piece + recv_a[slot(s, i)]
        pieces.append(piece)
    spectra = [strike_forward(pieces)]
    strike_inverse(0, *convolve(0, spectra))
    start_c(0)

    wait_halos(halos)
    stress_layers(1, stress_in)
    pack_x(2, stress.at[0])
    pack_y(2, lambda z: stress[1, z])
    halos = start_halos(2)
    started += halos
    arrange(1, late)
    for turn in range(2):
        wait_gather(turn)
    wait_all(back[0], c_recv.at[0])
    changes = []
    for i, value in enumerate(dip_inverse(range(dip_count))):
        trial = gathered[1, i] + value
        bound = gathered[0, i]
        clipped = jnp.clip(trial, -bound, bound)
        change = time_step * ((trial - clipped) / damping)
        lines_out[0, i] = change
        lines_out[1, i] = clipped
        changes.append((i, change))
    dip_forward(1, changes)
    start_b()
    results[2][...] = slip + lines_out[0, my_d]
    results[3][...] = lines_out[1, my_d]
    wait_halos(halos)
    fill_padded(2, stress.at[0])
    for copy in wide:
        copy.wait_send()
    for z in range(depth):
        velocity_layer(2, z, vel, stress, traction)
    pack_x(3, vel)
    pack_y(3, lambda z: vel[z])
    halos = start_halos(3)
    started += halos
    wait_all(recv_b, b_recv.at[0])
    change = strike_forward([recv_b[s] for s in range(strike_count)])
    latest = [[old + new for old, new in zip(*pair)] for pair in zip(spectra[0], change)]
    spectra = [latest] + spectra
    strike_inverse(1, *convolve(1, spectra))
    start_c(1)
    wait_halos(halos)
    stress_layers(3, stress)
    for copy in started:
        copy.wait_send()
    wait_all(recv_a, a_send.at[0])
    wait_all(recv_b, b_send.at[0])
    for step in range(STEPS):
        wait_all(back[step], c_send.at[step])
    wait_all(back[1], c_recv.at[1])


def last_kernel(*refs):
    sources, results, field, sems = refs[:8], refs[8:13], refs[13], refs[14]
    saves = [pltpu.make_async_copy(sources[i], results[i], sems.at[i]) for i in range(4)]
    for save in saves:
        save.start()
    field[...] = dip_inverse_lines(*sources[4:], [lax.axis_index("dip")])[0]
    saves.append(pltpu.make_async_copy(field, results[4], sems.at[4]))
    saves[4].start()
    for save in saves:
        save.wait()


def fits_kernel(strike_count, dip_count, depth, rows, cols, modes, total_x):
    return (
        STEPS == 2
        and depth > 2
        and strike_count > 1
        and dip_count > 1
        and modes == dip_count * SUBLANES
        and rows % SUBLANES == 0
        and cols == 2 * LANES
        and strike_count % 4 == 0
        and total_x == LANES
        and 2 * dip_count * rows == LANES
        and strike_count * dip_count * SUBLANES == cols
    )


def body(*args):
    velocity, history = args[0], args[11]
    strike_count = lax.axis_size("strike")
    dip_count = lax.axis_size("dip")
    depth, rows, cols = velocity.shape
    modes, total_x = history.shape[2:]
    if not fits_kernel(strike_count, dip_count, depth, rows, cols, modes, total_x):
        return general_body(*args)
    half = SUBLANES // 2
    blocks = strike_count * dip_count
    total_y = cols * dip_count
    tables = (
        *split_table(dip_table(strike_count, dip_count, cols, total_y)),
        *split_table(strike_table(total_x)),
        twiddle_table(dip_count, cols, total_y),
    )
    turns = 2 * STEPS
    f32 = jnp.float32
    dma = pltpu.SemaphoreType.DMA
    operands = (*args, *[jnp.asarray(table) for table in tables])
    shapes = (velocity.shape, args[1].shape) + ((rows, cols),) * 3
    outs = tuple(jax.ShapeDtypeStruct(shape, f32) for shape in shapes)
    held = tuple(pltpu.VMEM(shape, f32) for shape in shapes[:4])
    held += (pltpu.VMEM((blocks, half, LANES), f32),)
    held += tuple(pltpu.VMEM(operands[i].shape, operands[i].dtype) for i in PASSED)
    scratch = [
        pltpu.VMEM(operand.shape, operand.dtype)
        for i, operand in enumerate(operands)
        if i not in PASSED
    ] + [
        pltpu.VMEM((depth, rows + 2 * SUBLANES, cols), f32),
        pltpu.VMEM((turns, 2, depth, 2, cols), f32),
        pltpu.VMEM((turns, 2, rows, LANES), f32),
        pltpu.VMEM((turns, 2, depth, 2, cols), f32),
        pltpu.VMEM((turns, 2, rows, LANES), f32),
        pltpu.VMEM((2, 2, 2, SUBLANES, cols), f32),
        pltpu.VMEM((2, 2, 2, rows, LANES), f32),
        pltpu.VMEM((2, rows, cols), f32),
        pltpu.VMEM((2, dip_count, rows, cols), f32),
        pltpu.VMEM((STEPS, blocks, half, LANES), f32),
        pltpu.VMEM((blocks, half, LANES), f32),
        pltpu.VMEM((strike_count, half, LANES), f32),
        pltpu.VMEM((2, dip_count, rows, cols), f32),
        pltpu.VMEM((STEPS, strike_count, half, LANES), f32),
        pltpu.VMEM((blocks, half, LANES), f32),
        pltpu.VMEM((STEPS, 2, 3, modes + SUBLANES, total_x), f32),
        pltpu.VMEM((STEPS, 3, 1, total_x), f32),
        pltpu.VMEM((STEPS, 3, 1, total_x), f32),
        pltpu.VMEM((STEPS, 2, dip_count, SUBLANES, total_x), f32),
        pltpu.VMEM((STEPS, 2, dip_count, SUBLANES, total_x), f32),
        dma((len(operands),)),
        dma((turns, 4)),
        dma((turns, 4)),
        dma((2, 4)),
        dma((2, 4)),
        dma((2, dip_count)),
        dma((2, dip_count)),
        dma((1,)),
        dma((1,)),
        dma((1,)),
        dma((1,)),
        dma((STEPS,)),
        dma((STEPS,)),
        dma((STEPS, 2)),
        dma((STEPS, 2)),
        pltpu.SemaphoreType.REGULAR,
    ]
    anywhere = pl.BlockSpec(memory_space=pl.ANY)
    results = pl.pallas_call(
        functools.partial(rupture_kernel, strike_count, dip_count),
        out_shape=held,
        in_specs=[pl.BlockSpec(memory_space=pltpu.HBM)] * len(operands),
        out_specs=(pl.BlockSpec(memory_space=pltpu.VMEM),) * len(held),
        scratch_shapes=scratch,
        compiler_params=pltpu.CompilerParams(
            collective_id=0, has_side_effects=True, vmem_limit_bytes=KERNEL_VMEM
        ),
    )(*operands)
    return pl.pallas_call(
        last_kernel,
        out_shape=outs,
        in_specs=[pl.BlockSpec(memory_space=pltpu.VMEM)] * len(held),
        out_specs=(anywhere,) * len(outs),
        scratch_shapes=[pltpu.VMEM((rows, cols), f32), dma((len(outs),))],
        compiler_params=pltpu.CompilerParams(vmem_limit_bytes=2**23),
    )(*results)


def solution(mesh):
    return jax.shard_map(
        body,
        mesh=mesh,
        in_specs=(
            P(None, "strike", "dip"),
            P(None, None, "strike", "dip"),
            P(None, "strike", "dip"),
            P(None, "strike", "dip"),
            P("strike", "dip"),
            P("strike", "dip"),
            P("strike", "dip"),
            P("strike", "dip"),
            P("strike", "dip"),
            P("strike", "dip"),
            P("strike", "dip"),
            P(None, None, ("strike", "dip"), None),
            P(None, ("strike", "dip"), None),
        ),
        out_specs=(
            P(None, "strike", "dip"),
            P(None, None, "strike", "dip"),
            P("strike", "dip"),
            P("strike", "dip"),
            P("strike", "dip"),
        ),
        check_vma=False,
    )
```
